32 devices in a mesh: replica: 4 (over y, x), group: 8 (over z, core).
Axes of the slice: x: 2, y: 2, z: 4, core: 2. Of those that a mesh axis runs over, the one named last changes fastest.
Arguments:
- tokens: float32 [16384, 384], P(('replica', 'group')), may hold values from -6 to 6
- image_count: int32 [4], replicated, may hold values from 10 to 20, as said below
- w_qkv: float32 [384, 1152], P(None, 'group'), may hold values from -0.3125 to 0.3125
- w_out: float32 [384, 384], P(None, 'group'), may hold values from -1.75 to 1.75
- w_up: float32 [384, 1536], P(None, 'group'), may hold values from -0.3125 to 0.3125
- w_down: float32 [1536, 384], P('group'), may hold values from -0.15625 to 0.15625
- vectors: float32 [12, 384], P(None, 'group'), may hold values from -2 to 2
- cotangent: float32 [16384, 384], P(('replica', 'group')), may hold values from -6 to 6
- mom_qkv: float32 [384, 1152], P(None, 'group'), may hold values from -384 to 384
- mom_out: float32 [384, 384], P(None, 'group'), may hold values from -384 to 384
- mom_up: float32 [384, 1536], P(None, 'group'), may hold values from -384 to 384
- mom_down: float32 [1536, 384], P('group'), may hold values from -384 to 384
- mom_vectors: float32 [12, 384], P(None, 'group'), may hold values from -384 to 384
Outputs:
- block_out: float32 [16384, 384], P(('replica', 'group'))
- grad_tokens: float32 [16384, 384], P(('replica', 'group'))
- grad_qkv: float32 [384, 1152], P(None, 'group')
- grad_out: float32 [384, 384], P(None, 'group')
- grad_up: float32 [384, 1536], P(None, 'group')
- grad_down: float32 [1536, 384], P('group')
- grad_vectors: float32 [12, 384], P(None, 'group')
- new_mom_qkv: float32 [384, 1152], P(None, 'group')
- new_mom_out: float32 [384, 384], P(None, 'group')
- new_mom_up: float32 [384, 1536], P(None, 'group')
- new_mom_down: float32 [1536, 384], P('group')
- new_mom_vectors: float32 [12, 384], P(None, 'group')
- update_qkv: float32 [384, 1152], P(None, 'group')
- update_out: float32 [384, 384], P(None, 'group')
- update_up: float32 [384, 1536], P(None, 'group')
- update_down: float32 [1536, 384], P('group')
- update_vectors: float32 [12, 384], P(None, 'group')
The draws below stay inside these ranges and needn't reach their ends.
Inputs may be any that keep to these rules, and one draw needn't show every extreme that they name: Replica r holds images 0 to image_count[r] - 1 in its first 197 * image_count[r] slots; one replica holds 20 images and one holds 10.
All inputs are finite; a program needn't handle non-finite values.
Results may differ from the reference program's by a relative error of at most 0.0003.
Values sent between devices are 32-bit elements; how exact they have to be, the bound alone decides.
No kernel may reach another device: no remote copies, remote signals or barrier semaphores. Data moves between devices by JAX's collectives and lax.ppermute only.
A program may use at most 128 MiB of HBM per device.

```python
import jax
import jax.numpy as jnp
from jax import lax

D = 384
HEADS = 6
HEAD_DIM = 64
FF = 1536
L = 197
NS_STEPS = 5
SLAB = 4096
CAPACITY = 20
SEGS = 21
REPLICAS = 4
TOKENS = 16384


def draw_image_count(key, part):
    first_key, second_key = jax.random.split(jax.random.fold_in(key, 11))
    lowest = CAPACITY // 2
    counts = jax.random.randint(first_key, (REPLICAS,), lowest, CAPACITY + 1)
    shuffle = jax.random.permutation(second_key, REPLICAS)
    counts = counts.at[shuffle[0]].set(CAPACITY).at[shuffle[1]].set(lowest)
    return counts.astype(jnp.int32)


def block_levels(key, shape, shards, smallest, largest):
    loudness = 1.0
    for position, shards_of in shards:
        draws = jax.random.uniform(jax.random.fold_in(jax.random.fold_in(key, 6), position), (shards_of,), jnp.float32, smallest / len(shards), largest / len(shards))
        loudness = loudness * jnp.repeat(jnp.exp(draws), shape[position] // shards_of).reshape((-1,) + (1,) * (len(shape) - 1 - position))
    return loudness


def centred(key, dims, deviation, limit, pieces=(), held_as=jnp.bfloat16):
    entries = jax.random.normal(key, dims, jnp.float32) * deviation
    if len(pieces) > 0:
        entries = block_levels(key, dims, pieces, -0.22, 0.18) * entries
    return jnp.clip(entries, min=-limit, max=limit).astype(held_as)


def setup_inputs(seed: int = 0) -> dict:
    streams_of = jax.random.split(jax.random.key(seed), 14)
    return {
        "tokens": centred(streams_of[0], (TOKENS, D), 1.0, 6.0, ((0, 32),), jnp.float32),
        "image_count": draw_image_count(jax.random.fold_in(streams_of[13], 71), 0),
        "w_qkv": centred(streams_of[2], (D, 3 * D), D ** -0.5, 0.3125, ((1, 8),), jnp.float32),
        "w_out": centred(streams_of[3], (D, D), (D // 32) ** -0.5, 1.75, ((1, 8),), jnp.float32),
        "w_up": centred(streams_of[4], (D, FF), D ** -0.5, 0.3125, ((1, 8),), jnp.float32),
        "w_down": centred(streams_of[5], (FF, D), FF ** -0.5, 0.15625, ((0, 8),), jnp.float32),
        "vectors": centred(streams_of[6], (12, D), 0.3, 2.0, ((1, 8),), jnp.float32),
        "cotangent": centred(streams_of[7], (TOKENS, D), 1.0, 6.0, ((0, 32),), jnp.float32),
        "mom_qkv": centred(streams_of[8], (D, 3 * D), (0.5 * TOKENS ** 0.5), 384.0, ((1, 8),), jnp.float32),
        "mom_out": centred(streams_of[9], (D, D), (0.5 * TOKENS ** 0.5), 384.0, ((1, 8),), jnp.float32),
        "mom_up": centred(streams_of[10], (D, FF), (0.5 * TOKENS ** 0.5), 384.0, ((1, 8),), jnp.float32),
        "mom_down": centred(streams_of[11], (FF, D), (0.5 * TOKENS ** 0.5), 384.0, ((0, 8),), jnp.float32),
        "mom_vectors": centred(streams_of[12], (12, D), (0.5 * TOKENS ** 0.5), 384.0, ((1, 8),), jnp.float32),
    }


@jax.custom_vjp
def low(v):
    return lax.optimization_barrier(v.astype(jnp.bfloat16)).astype(jnp.float32)

@jax.custom_vjp
def low_back(v):
    return v

def low_keep(v):
    return (low(v), None)

def low_pass(kept, grad):
    return (grad,)

def back_keep(v):
    return (v, None)

def back_low(kept, grad):
    return (low(grad),)
low.defvjp(low_keep, low_pass)
low_back.defvjp(back_keep, back_low)
precise = lax.Precision.HIGHEST
ns_coeffs = (3.4445, -4.775, 2.0315)
norm_eps = 1e-06
ns_eps = 1e-07
muon_momentum = 0.95
vector_momentum = 0.9
muon_rate = 0.5
vector_rate = 0.001
mask_fill = -1e+30

def matmul(left_side, right_side):
    return jnp.dot(left_side, right_side, precision=precise, preferred_element_type=jnp.float32)

def layer_norm(values, scale_delta, offset):
    centered = values - lax.optimization_barrier(jnp.mean(values, axis=-1, keepdims=True))
    variance = lax.optimization_barrier(jnp.mean(centered * centered, axis=-1, keepdims=True))
    return centered * lax.rsqrt(variance + norm_eps) * (1.0 + scale_delta) + offset

def image_attention(queries, key_rows, values):
    slot_rows = queries.shape[0]
    padded = SEGS * L

    def shape_heads(block_rows):
        block_rows = jnp.pad(block_rows, ((0, padded - slot_rows), (0, 0)))
        return block_rows.reshape(SEGS, L, HEADS, HEAD_DIM)
    key_keep = (jnp.arange(padded) < slot_rows).reshape(SEGS, 1, 1, L)
    scores = jnp.einsum('sqhd,skhd->shqk', shape_heads(queries), shape_heads(key_rows), precision=precise) * HEAD_DIM ** (-0.5)
    scores = jnp.where(key_keep, scores, mask_fill)
    weights = jax.nn.softmax(scores, axis=-1)
    attended = jnp.einsum('shqk,skhd->sqhd', weights, shape_heads(values), precision=precise)
    return attended.reshape(padded, D)[:slot_rows]

def block_forward(params, slab_rows):
    w_qkv, w_out, w_up, w_down, vectors = params
    normed = layer_norm(slab_rows, vectors[0], vectors[1])
    projected = matmul(normed, w_qkv)
    queries = projected[:, :D] + vectors[2]
    key_rows = projected[:, D:2 * D]
    values = projected[:, 2 * D:] + vectors[3]
    attended = image_attention(queries, key_rows, values)
    middle = slab_rows + matmul(attended, w_out) + vectors[4]
    normed_two = layer_norm(middle, vectors[5], vectors[6])
    hidden = jax.nn.gelu(matmul(normed_two, w_up) + vectors[8:].reshape(FF), approximate=False)
    return middle + matmul(hidden, w_down) + vectors[7]

def forward_all(params, tokens):
    slabs = tokens.reshape(REPLICAS, SLAB, D)
    outputs = lax.map(jax.checkpoint(lambda slab_rows: block_forward(params, slab_rows)), slabs)
    return outputs.reshape(TOKENS, D)

def orthogonalize(matrix):
    current = matrix / (jnp.sqrt(jnp.sum(matrix * matrix)) + ns_eps)
    for step_index in range(NS_STEPS):
        gram_mat = matmul(current, current.T)
        polynomial = ns_coeffs[1] * gram_mat + ns_coeffs[2] * matmul(gram_mat, gram_mat)
        current = ns_coeffs[0] * current + matmul(polynomial, current)
    return current

def reference(tokens, image_count, w_qkv, w_out, w_up, w_down, vectors, cotangent, mom_qkv, mom_out, mom_up, mom_down, mom_vectors):
    live_rows = jnp.arange(SLAB, dtype=jnp.int32)[None, :] < (image_count * L)[:, None]
    masked = cotangent * live_rows.astype(jnp.float32).reshape(TOKENS, 1)
    params = (w_qkv, w_out, w_up, w_down, vectors)
    block_out, pullback = jax.vjp(forward_all, params, tokens)
    param_grads, grad_tokens = pullback(masked)
    grad_qkv, grad_out, grad_up, grad_down, grad_vectors = param_grads
    new_qkv = muon_momentum * mom_qkv + grad_qkv
    new_out = muon_momentum * mom_out + grad_out
    new_up = muon_momentum * mom_up + grad_up
    new_down = muon_momentum * mom_down + grad_down
    new_vectors = vector_momentum * mom_vectors + grad_vectors
    update_qkv = -muon_rate * max(1.0, w_qkv.shape[1] / w_qkv.shape[0]) ** 0.5 * orthogonalize(new_qkv)
    update_out = -muon_rate * max(1.0, w_out.shape[1] / w_out.shape[0]) ** 0.5 * orthogonalize(new_out)
    update_up = -muon_rate * max(1.0, w_up.shape[1] / w_up.shape[0]) ** 0.5 * orthogonalize(new_up)
    update_down = -muon_rate * max(1.0, w_down.shape[1] / w_down.shape[0]) ** 0.5 * orthogonalize(new_down.T).T
    update_vectors = -vector_rate * new_vectors
    return (block_out, grad_tokens, grad_qkv, grad_out, grad_up, grad_down, grad_vectors, new_qkv, new_out, new_up, new_down, new_vectors, update_qkv, update_out, update_up, update_down, update_vectors)
```

```python
import jax
import jax.numpy as jnp
from jax import lax
from jax.sharding import PartitionSpec as P

D = 384
HEADS = 6
HEAD_DIM = 64
FF = 1536
L = 197
NS_STEPS = 5


precise = lax.Precision.HIGHEST
ns_coeffs = (3.4445, -4.775, 2.0315)
norm_eps = 1e-06
ns_eps = 1e-07
muon_momentum = 0.95
vector_momentum = 0.9
muon_rate = 0.5
vector_rate = 0.001
mask_fill = -1e30


def with_halo(cells, sides, width):
    for axis, dim in sides:
        count = lax.axis_size(axis)
        ends = count - 1
        head = lax.slice_in_dim(cells, 0, width, axis=dim)
        tail = lax.slice_in_dim(cells, cells.shape[dim] - width, cells.shape[dim], axis=dim)
        cells = jnp.concatenate(
            [
                lax.ppermute(tail, axis, [(i, (i + 1) % count) for i in range(ends)]),
                cells,
                lax.ppermute(head, axis, [((i + 1) % count, i) for i in range(ends)]),
            ],
            axis=dim,
        )
    return cells


def from_behind(x, axis, by):
    peers = lax.axis_size(axis)
    pairs = [(i, i + by) for i in range(peers) if 0 <= i + by < peers]
    return lax.ppermute(x, axis, pairs)


def matmul(left_side, right_side):
    return jnp.dot(left_side, right_side, precision=precise, preferred_element_type=jnp.float32)


def layer_norm(values, scale_delta, offset):
    centered = values - jnp.mean(values, axis=-1, keepdims=True)
    variance = jnp.mean(centered * centered, axis=-1, keepdims=True)
    return centered * lax.rsqrt(variance + norm_eps) * (1.0 + scale_delta) + offset


def polar_factor(gram_mat, block):
    factor = None
    for step_index in range(NS_STEPS):
        square = matmul(gram_mat, gram_mat)
        poly = ns_coeffs[1] * gram_mat + ns_coeffs[2] * square + ns_coeffs[0] * jnp.eye(D, dtype=jnp.float32)
        factor = poly if factor is None else matmul(poly, factor)
        if step_index + 1 < NS_STEPS:
            gram_mat = matmul(poly, matmul(gram_mat, poly))
    return matmul(factor, block)


def local(
    tokens,
    image_count,
    w_qkv,
    w_out,
    w_up,
    w_down,
    vectors,
    cotangent,
    mom_qkv,
    mom_out,
    mom_up,
    mom_down,
    mom_vectors,
):
    group_size = lax.axis_size("group")
    group_index = lax.axis_index("group")
    replica_index = lax.axis_index("replica")
    tok_rows = tokens.shape[0]
    margin = L - 1
    slab_rows = group_size * tok_rows
    image_runs = tok_rows // L + 2
    span_rows = image_runs * L
    extent = tok_rows + 2 * margin + 2 * L
    image_total = lax.dynamic_index_in_dim(image_count, replica_index, 0, keepdims=False)
    first_slot = group_index * tok_rows
    first_image = first_slot // L
    offset = first_image * L - first_slot + margin
    key_pos = first_slot - margin + offset + jnp.arange(span_rows, dtype=jnp.int32)
    key_keep = ((key_pos >= 0) & (key_pos < slab_rows)).reshape(image_runs, 1, 1, L)
    query_pos = first_slot + jnp.arange(tok_rows, dtype=jnp.int32)
    live_rows = (query_pos < image_total * L).astype(jnp.float32)[:, None]

    def image_blocks(queries, widened):
        query_pad = jnp.pad(queries, ((margin, extent - margin - tok_rows), (0, 0)))
        pair_pad = jnp.pad(widened, ((0, 0), (0, extent - tok_rows - 2 * margin), (0, 0)))
        block_q = lax.dynamic_slice_in_dim(query_pad, offset, span_rows, 0).reshape(
            image_runs, L, HEADS, HEAD_DIM
        )
        block_k = lax.dynamic_slice_in_dim(pair_pad[0], offset, span_rows, 0).reshape(
            image_runs, L, HEADS, HEAD_DIM
        )
        block_v = lax.dynamic_slice_in_dim(pair_pad[1], offset, span_rows, 0).reshape(
            image_runs, L, HEADS, HEAD_DIM
        )
        scores = jnp.einsum("sqhd,skhd->shqk", block_q, block_k, precision=precise) * HEAD_DIM ** (
            -0.5
        )
        scores = jnp.where(key_keep, scores, mask_fill)
        weights = jax.nn.softmax(scores, axis=-1)
        attended = jnp.einsum("shqk,skhd->sqhd", weights, block_v, precision=precise).reshape(
            span_rows, D
        )
        placed = lax.dynamic_update_slice_in_dim(
            jnp.zeros((extent, D), jnp.float32), attended, offset, 0
        )
        return placed[margin : margin + tok_rows]

    def project_part(qkv_whole, vectors_whole, inputs):
        normed = layer_norm(inputs, vectors_whole[0], vectors_whole[1])
        projected = matmul(normed, qkv_whole)
        queries = projected[:, :D] + vectors_whole[2]
        key_value = jnp.stack([projected[:, D : 2 * D], projected[:, 2 * D :] + vectors_whole[3]])
        return (queries, key_value)

    def rest_part(out_whole, up_whole, down_whole, vectors_whole, inputs, queries, widened):
        attended = image_blocks(queries, widened)
        middle = inputs + matmul(attended, out_whole) + vectors_whole[4]
        normed_two = layer_norm(middle, vectors_whole[5], vectors_whole[6])
        hidden = jax.nn.gelu(
            matmul(normed_two, up_whole) + vectors_whole[8:].reshape(FF), approximate=False
        )
        return middle + matmul(hidden, down_whole) + vectors_whole[7]

    whole = (
        lax.all_gather(w_qkv, "group", axis=1, tiled=True),
        lax.all_gather(w_out, "group", axis=1, tiled=True),
        lax.all_gather(w_up, "group", axis=1, tiled=True),
        lax.all_gather(w_down, "group", axis=0, tiled=True),
        lax.all_gather(vectors, "group", axis=1, tiled=True),
    )
    queries, key_value = project_part(whole[0], whole[4], tokens)
    widened = with_halo(key_value, (("group", 1),), margin)
    block_out = rest_part(whole[1], whole[2], whole[3], whole[4], tokens, queries, widened)
    second = whole
    masked = cotangent * live_rows
    unused_out, rest_back = jax.vjp(
        rest_part, second[1], second[2], second[3], second[4], tokens, queries, widened
    )
    (
        grad_out_full,
        grad_up_full,
        grad_down_full,
        grad_vec_rest,
        grad_tok_rest,
        grad_queries,
        grad_widened,
    ) = rest_back(masked)
    lower_rim = grad_widened[:, :margin]
    upper_rim = grad_widened[:, margin + tok_rows :]
    from_above = from_behind(lower_rim, "group", -1)
    from_below = from_behind(upper_rim, "group", 1)
    grad_pair = grad_widened[:, margin : margin + tok_rows]
    grad_pair = grad_pair.at[:, :margin].add(from_below).at[:, tok_rows - margin :].add(from_above)
    unused_project, project_back = jax.vjp(project_part, second[0], second[4], tokens)
    grad_qkv_full, grad_vec_project, grad_tok_project = project_back((grad_queries, grad_pair))
    grad_tokens = grad_tok_project + grad_tok_rest
    shares = (
        lax.psum_scatter(grad_qkv_full, "group", scatter_dimension=1, tiled=True),
        lax.psum_scatter(grad_out_full, "group", scatter_dimension=1, tiled=True),
        lax.psum_scatter(grad_up_full, "group", scatter_dimension=1, tiled=True),
        lax.psum_scatter(grad_down_full, "group", scatter_dimension=0, tiled=True),
        lax.psum_scatter(
            grad_vec_project + grad_vec_rest, "group", scatter_dimension=1, tiled=True
        ),
    )
    gradients = lax.psum((shares[0], shares[1], shares[2], shares[3], shares[4]), "replica")
    new_qkv = muon_momentum * mom_qkv + gradients[0]
    new_out = muon_momentum * mom_out + gradients[1]
    new_up = muon_momentum * mom_up + gradients[2]
    new_down = muon_momentum * mom_down + gradients[3]
    new_vectors = vector_momentum * mom_vectors + gradients[4]
    oriented = (new_qkv, new_out, new_up, new_down.T)
    totals = lax.psum(
        (
            jnp.sum(oriented[0] * oriented[0]),
            jnp.sum(oriented[1] * oriented[1]),
            jnp.sum(oriented[2] * oriented[2]),
            jnp.sum(oriented[3] * oriented[3]),
        ),
        "group",
    )
    current = tuple((oriented[member] / (jnp.sqrt(totals[member]) + ns_eps) for member in range(4)))
    gram_sums = lax.psum(tuple(matmul(member, member.T) for member in current), "group")
    current = tuple(polar_factor(gram_sums[member], current[member]) for member in range(4))
    update_qkv = -muon_rate * 3.0**0.5 * current[0]
    update_out = -muon_rate * current[1]
    update_up = -muon_rate * (FF / D) ** 0.5 * current[2]
    update_down = (-muon_rate * current[3]).T
    update_vectors = -vector_rate * new_vectors
    return (
        block_out,
        grad_tokens,
        gradients[0],
        gradients[1],
        gradients[2],
        gradients[3],
        gradients[4],
        new_qkv,
        new_out,
        new_up,
        new_down,
        new_vectors,
        update_qkv,
        update_out,
        update_up,
        update_down,
        update_vectors,
    )


def solution(mesh):
    return jax.shard_map(
        local,
        mesh=mesh,
        in_specs=(
            P(("replica", "group"), None),
            P(),
            P(None, "group"),
            P(None, "group"),
            P(None, "group"),
            P("group", None),
            P(None, "group"),
            P(("replica", "group"), None),
            P(None, "group"),
            P(None, "group"),
            P(None, "group"),
            P("group", None),
            P(None, "group"),
        ),
        out_specs=(
            P(("replica", "group"), None),
            P(("replica", "group"), None),
            P(None, "group"),
            P(None, "group"),
            P(None, "group"),
            P("group", None),
            P(None, "group"),
            P(None, "group"),
            P(None, "group"),
            P(None, "group"),
            P("group", None),
            P(None, "group"),
            P(None, "group"),
            P(None, "group"),
            P(None, "group"),
            P("group", None),
            P(None, "group"),
        ),
        check_vma=False,
    )
```

```python
import functools

import jax
import jax.numpy as jnp
from jax import lax
from jax.experimental import pallas as pl
from jax.experimental.pallas import tpu as pltpu
from jax.sharding import PartitionSpec as P

D = 384
HEADS = 6
HEAD_DIM = 64
FF = 1536
L = 197
NS_STEPS = 5
SLOTS = 4
SLOT = 208
HALO = 200
TILE = 256

f32, bf16 = jnp.float32, jnp.bfloat16
high = lax.Precision.HIGH
precise = lax.Precision.HIGHEST
ns_coeffs = (3.4445, -4.775, 2.0315)
norm_eps = 1e-06
ns_eps = 1e-07
muon_momentum = 0.95
vector_momentum = 0.9
muon_rate = 0.5
vector_rate = 0.001
mask_fill = -1e30

NN = (((1,), (0,)), ((), ()))
NT = (((1,), (1,)), ((), ()))
TN = (((0,), (0,)), ((), ()))
VMEM = pl.BlockSpec(memory_space=pltpu.VMEM)
SMEM = pl.BlockSpec(memory_space=pltpu.SMEM)


def call(body, outs, scratch=(), flops=0, data=0):
    def run(scalars, *arrays):
        return pl.pallas_call(
            body,
            out_shape=[jax.ShapeDtypeStruct(s, t) for s, t in outs],
            in_specs=[SMEM] + [VMEM] * len(arrays),
            out_specs=[VMEM] * len(outs),
            scratch_shapes=[pltpu.VMEM(s, t) for s, t in scratch],
            compiler_params=pltpu.CompilerParams(vmem_limit_bytes=56 << 20),
            cost_estimate=pl.CostEstimate(flops=flops, bytes_accessed=data, transcendentals=0),
        )(scalars, *arrays)

    return run


def mm(a, b, dims):
    return lax.dot_general(a, b, dims, preferred_element_type=f32)


def fdot(a, b, dims, precision=high):
    return lax.dot_general(a, b, dims, precision=precision, preferred_element_type=f32)


def halves(x):
    hi = x.astype(bf16)
    return hi, (x - hi.astype(f32)).astype(bf16)


def triple(x):
    hi, lo = halves(x)
    return jnp.concatenate([hi, hi, lo], axis=1)


def by_rows(hi, lo, both):
    wide = mm(hi, both[:, : 2 * D], NN)
    return wide[:, :D] + wide[:, D:] + mm(lo, both[:, :D], NN)


def by_tokens(hi, lo, other):
    wide = mm(hi, other[:, D:], TN)
    return wide[:, :D] + wide[:, D:] + mm(lo, other[:, :D], TN)


def standardized(x):
    centered = x - jnp.mean(x, axis=-1, keepdims=True)
    rstd = lax.rsqrt(jnp.mean(centered * centered, axis=-1, keepdims=True) + norm_eps)
    return centered * rstd, rstd


def norm_back(d_norm, xhat, rstd, scale):
    g = d_norm * (1.0 + scale)
    return rstd * (
        g - jnp.mean(g, axis=-1, keepdims=True) - xhat * jnp.mean(g * xhat, axis=-1, keepdims=True)
    )


def row_sum(x):
    return jnp.sum(x, axis=0, keepdims=True)


def window_start(scalars, slot):
    start = HALO - scalars[0] + L * slot
    aligned = pl.multiple_of((start // 8) * 8, 8)
    return aligned, start - aligned


def fill_window(window, lower, own, upper):
    rows = own.shape[0]
    window[:HALO, :] = lower[...]
    window[HALO : HALO + rows, :] = own[...]
    window[HALO + rows : 2 * HALO + rows, :] = upper[...]
    window[2 * HALO + rows :, :] = jnp.zeros((window.shape[0] - 2 * HALO - rows, D), f32)


def load_slot(window, scalars, slot):
    aligned, shift = window_start(scalars, slot)
    block = window[pl.ds(aligned, SLOT + 8), :]
    return pltpu.roll(block, lax.rem(SLOT + 8 - shift, SLOT + 8), 0)[:SLOT]


def store_slot(window, scalars, slot, value):
    aligned, shift = window_start(scalars, slot)
    block = pltpu.roll(jnp.concatenate([value, jnp.zeros((8, D), f32)], axis=0), shift, 0)
    rows = lax.broadcasted_iota(jnp.int32, (SLOT + 8, 1), 0)
    window[pl.ds(aligned, SLOT + 8), :] = jnp.where(
        rows >= shift, block, window[pl.ds(aligned, SLOT + 8), :]
    )


def window_rows(rows):
    return 2 * HALO + rows + 96


def attend_kernel(
    scalars, lower, own, upper, w, vec, proj, xhats, rstds, n3, a3, probs, middle, window, mid_win
):
    fill_window(window, lower, own, upper)

    def slot_step(slot, carry):
        x = load_slot(window, scalars, slot)
        xhat, rstd = standardized(x)
        xhats[slot] = xhat
        rstds[slot] = jnp.broadcast_to(rstd, (SLOT, 128))
        left = triple(xhat * (1.0 + vec[0:1, :]) + vec[1:2, :])
        n3[slot] = left
        for part, bias in ((0, vec[2:3, :]), (1, None), (2, vec[3:4, :])):
            value = mm(left, w[part * D : (part + 1) * D, :], NT)
            proj[slot, :, part * D : (part + 1) * D] = value if bias is None else value + bias
        keys = jnp.minimum(L, scalars[1] - L * slot)
        keep = lax.broadcasted_iota(jnp.int32, (SLOT, SLOT), 1) < keys
        heads = []
        for h in range(HEADS):
            at = h * HEAD_DIM
            q = proj[slot, :, at : at + HEAD_DIM]
            k = proj[slot, :, D + at : D + at + HEAD_DIM]
            v = proj[slot, :, 2 * D + at : 2 * D + at + HEAD_DIM]
            scores = jnp.where(keep, fdot(q, k, NT) * HEAD_DIM**-0.5, mask_fill)
            weights = jnp.exp(scores - jnp.max(scores, axis=-1, keepdims=True))
            weights = weights / jnp.sum(weights, axis=-1, keepdims=True)
            probs[slot, h] = weights
            heads.append(fdot(weights, v, NN))
        att = triple(jnp.concatenate(heads, axis=1))
        a3[slot] = att
        store_slot(mid_win, scalars, slot, x + mm(att, w[3 * D :, :], NT) + vec[4:5, :])
        return carry

    lax.fori_loop(0, SLOTS, slot_step, 0)
    middle[...] = mid_win[HALO : HALO + own.shape[0], :]


def attend(scalars, lower, own, upper, w, vec):
    rows = own.shape[0]
    return call(
        attend_kernel,
        [
            ((SLOTS, SLOT, 3 * D), f32),
            ((SLOTS, SLOT, D), f32),
            ((SLOTS, SLOT, 128), f32),
            ((SLOTS, SLOT, 3 * D), bf16),
            ((SLOTS, SLOT, 3 * D), bf16),
            ((SLOTS, HEADS, SLOT, SLOT), f32),
            ((rows, D), f32),
        ],
        [((window_rows(rows), D), f32)] * 2,
        flops=3 * 10**10,
        data=20 << 20,
    )(scalars, lower, own, upper, w, vec)


def mlp_kernel(
    scalars, mid, cot, w, vec, bias, out, dmid, h_hi, h_lo, d_hi, d_lo, n3, m3, dvec, acc, acc_d, dbias
):
    rows = mid.shape[0]
    xhat, rstd = standardized(mid[...])
    n3[...] = triple(xhat * (1.0 + vec[5:6, :]) + vec[6:7, :])
    live = lax.broadcasted_iota(jnp.int32, (rows, 1), 0) < scalars[2]
    masked = jnp.where(live, cot[...], 0.0)
    m3[...] = triple(masked)
    acc[...] = jnp.zeros_like(acc)
    acc_d[...] = jnp.zeros_like(acc_d)

    def tile_step(t, carry):
        at = pl.multiple_of(t * TILE, TILE)
        up = w[pl.ds(at, TILE), :]
        down = w[pl.ds(FF + at, TILE), :]
        pre = mm(n3[...], up, NT) + bias[0:1, pl.ds(at, TILE)]
        d_hidden = mm(m3[...], down, NT)
        cdf = 0.5 + 0.5 * lax.erf(pre * (0.5**0.5))
        slope = cdf + pre * (jnp.exp(-0.5 * pre * pre) * 0.3989422804014327)
        hi, lo = halves(pre * cdf)
        h_hi[:, pl.ds(at, TILE)] = hi
        h_lo[:, pl.ds(at, TILE)] = lo
        acc[...] += by_rows(hi, lo, down)
        d_pre = d_hidden * slope
        dbias[0:1, pl.ds(at, TILE)] = row_sum(d_pre)
        hi, lo = halves(d_pre)
        d_hi[:, pl.ds(at, TILE)] = hi
        d_lo[:, pl.ds(at, TILE)] = lo
        acc_d[...] += by_rows(hi, lo, up)
        return carry

    lax.fori_loop(0, FF // TILE, tile_step, 0)
    out[...] = mid[...] + acc[...] + vec[7:8, :]
    d_norm = acc_d[...]
    xhat, rstd = standardized(mid[...])
    masked = jnp.where(live, cot[...], 0.0)
    d_middle = masked + norm_back(d_norm, xhat, rstd, vec[5:6, :])
    dmid[...] = d_middle
    zero = jnp.zeros((4, D), f32)
    dvec[...] = jnp.concatenate(
        [zero, row_sum(d_middle), row_sum(d_norm * xhat), row_sum(d_norm), row_sum(masked)]
        + [dbias[0:1, i * D : (i + 1) * D] for i in range(4)]
        + [zero],
        axis=0,
    )


def mlp(scalars, mid, cot, w, vec, bias):
    rows = mid.shape[0]
    return call(
        mlp_kernel,
        [((rows, D), f32)] * 2
        + [((rows, FF), bf16)] * 4
        + [((rows, 3 * D), bf16)] * 2
        + [((16, D), f32)],
        [((rows, D), f32)] * 2 + [((8, FF), f32)],
        flops=3 * 10**10,
        data=20 << 20,
    )(scalars, mid, cot, w, vec, bias)


def place(scalars, chips, i, j, k):
    owner = 2 * lax.rem(scalars[4] + k, chips) + lax.bitwise_xor(scalars[5], i)
    return owner, lax.bitwise_xor(scalars[3], j)


def first_rows(owner, quarter, piece):
    return pl.multiple_of(
        jnp.where(quarter < 3, owner * 3 * piece + quarter * piece, 3 * D + owner * piece), piece
    )


def second_rows(owner, quarter, piece):
    return pl.multiple_of(
        (quarter // 2) * FF + owner * 2 * piece + lax.rem(quarter, 2) * piece, piece
    )


def scatter_parts(scalars, total, outs, rows_of):
    for i, out in enumerate(outs):
        quarters, chips, piece, _ = out.shape
        for j in range(quarters):
            for k in range(chips):
                owner, quarter = place(scalars, chips, i, j, k)
                out[j, k] = total[pl.ds(rows_of(owner, quarter, piece), piece), :]


def mlp_grads_kernel(scalars, h_hi, h_lo, d_hi, d_lo, n3, m3, *rest):
    outs, total = rest[:-1], rest[-1]
    if len(outs) == 1:
        total = outs[0]

    def tile_step(t, carry):
        at = pl.multiple_of(t * TILE, TILE)
        total[pl.ds(at, TILE), :] = by_tokens(d_hi[:, pl.ds(at, TILE)], d_lo[:, pl.ds(at, TILE)], n3)
        total[pl.ds(FF + at, TILE), :] = by_tokens(
            h_hi[:, pl.ds(at, TILE)], h_lo[:, pl.ds(at, TILE)], m3
        )
        return carry

    lax.fori_loop(0, FF // TILE, tile_step, 0)
    if len(outs) == 2:
        scatter_parts(scalars, total, outs, second_rows)


def mlp_grads(scalars, parts, *arrays):
    outs = [(parts, f32)] * 2 if parts else [((2 * FF, D), f32)]
    return call(
        mlp_grads_kernel,
        outs,
        [((2 * FF if parts else 8, D), f32)],
        flops=2 * 10**10,
        data=20 << 20,
    )(scalars, *arrays)


def attend_back_kernel(
    scalars, lower, own, upper, w, vec, proj, xhats, rstds, n3, a3, probs, dvec_in, *rest
):
    outs, (dtok, dvec), (total, window, tok_win, dproj) = rest[:-6], rest[-6:-4], rest[-4:]
    if len(outs) == 1:
        total = outs[0]
    rows = own.shape[0]
    fill_window(window, lower, own, upper)
    total[...] = jnp.zeros_like(total)

    def slot_step(slot, sums):
        row = lax.broadcasted_iota(jnp.int32, (SLOT, 1), 0)
        at_own = row + L * slot - scalars[0]
        mine = (at_own >= 0) & (at_own < rows) & (row < L)
        d_mid = jnp.where(row < L, load_slot(window, scalars, slot), 0.0)
        d_att = by_rows(*halves(d_mid), w[3 * D :, :])
        total[3 * D :, :] += by_tokens(*halves(jnp.where(mine, d_mid, 0.0)), a3.at[slot])
        for h in range(HEADS):
            at = h * HEAD_DIM
            q = proj[slot, :, at : at + HEAD_DIM]
            k = proj[slot, :, D + at : D + at + HEAD_DIM]
            v = proj[slot, :, 2 * D + at : 2 * D + at + HEAD_DIM]
            d_out = d_att[:, at : at + HEAD_DIM]
            weights = probs[slot, h]
            d_weights = fdot(d_out, v, NT)
            mean = jnp.sum(weights * d_weights, axis=-1, keepdims=True)
            d_scores = weights * (d_weights - mean) * HEAD_DIM**-0.5
            dproj[:, at : at + HEAD_DIM] = fdot(d_scores, k, NN)
            dproj[:, D + at : D + at + HEAD_DIM] = fdot(d_scores, q, TN)
            dproj[:, 2 * D + at : 2 * D + at + HEAD_DIM] = fdot(weights, d_out, TN)
        d_proj = jnp.where(mine, dproj[...], 0.0)
        hi, lo = halves(d_proj)
        total[: 3 * D, :] += by_tokens(hi, lo, n3.at[slot])
        d_norm = by_rows(hi, lo, w[: 3 * D, :])
        xhat = xhats[slot]
        back = norm_back(d_norm, xhat, rstds[slot][:, 0:1], vec[0:1, :])
        store_slot(tok_win, scalars, slot, d_mid + back)
        new = jnp.concatenate(
            [row_sum(d_norm * xhat), row_sum(d_norm), row_sum(d_proj[:, :D]), row_sum(d_proj[:, 2 * D :])],
            axis=0,
        )
        return sums + new

    sums = lax.fori_loop(0, SLOTS, slot_step, jnp.zeros((4, D), f32))
    dtok[...] = tok_win[HALO : HALO + rows, :]
    dvec[...] = dvec_in[...] + jnp.concatenate([sums, jnp.zeros((12, D), f32)], axis=0)
    if len(outs) == 2:
        scatter_parts(scalars, total, outs, first_rows)


def attend_back(scalars, parts, own, *arrays):
    rows = own[1].shape[0]
    outs = [(parts, f32)] * 2 if parts else [((4 * D, D), f32)]
    return call(
        attend_back_kernel,
        outs + [((rows, D), f32), ((16, D), f32)],
        [((4 * D if parts else 8, D), f32)]
        + [((window_rows(rows), D), f32)] * 2
        + [((SLOT, 3 * D), f32)],
        flops=3 * 10**10,
        data=20 << 20,
    )(scalars, *own, *arrays)


def store_split(w, at, x):
    hi, lo = halves(x)
    w[pl.ds(at, x.shape[0]), :] = jnp.concatenate([hi, lo, hi], axis=1)


def unpack_kernel(rows_of, scalars, mine, other, *rest):
    vectors, (w, *small) = (rest[:2], rest[2:]) if len(rest) > 1 else ((), rest)
    quarters, chips, piece, _ = mine.shape
    for i, parts in enumerate((mine, other)):
        for j in range(quarters):
            for k in range(chips):
                owner, quarter = place(scalars, chips, i, j, chips - k)
                store_split(w, rows_of(owner, quarter, piece), parts[j, k])
    if small:
        vec, bias, flat = small
        for i, parts in enumerate(vectors):
            for k in range(chips):
                owner, _ = place(scalars, chips, i, 0, chips - k)
                step = parts.shape[1]
                for s in range(3):
                    flat[pl.ds(pl.multiple_of((owner * 3 + s) * step, step), step), :] = parts[
                        k, :, s * 128 : (s + 1) * 128
                    ]
        rows = jnp.transpose(flat[...])[:16, :]
        vec[...] = rows
        bias[...] = jnp.concatenate([rows[8 + s : 9 + s, :] for s in range(4)], axis=1)


def unpack(scalars, mine, other, rows_of, *vectors):
    total = 2 * mine.shape[0] * mine.shape[1] * mine.shape[2]
    outs = [((total, 3 * D), bf16)]
    if vectors:
        outs += [((16, D), f32), ((1, FF), f32)]
    return call(
        functools.partial(unpack_kernel, rows_of),
        outs,
        [((D, 128), f32)] if vectors else [],
        flops=10**8,
        data=total * D * 10,
    )(scalars, mine, other, *vectors)


def own_gradients_kernel(scalars, parts, mom, grads, new_mom, own, *gram):
    quarters, rows, _ = parts.shape
    piece = rows // 3
    for j in range(quarters):
        quarter = lax.bitwise_xor(scalars[3], j)
        grads[pl.ds(pl.multiple_of(quarter * piece, piece), piece), :] = parts[j, :piece]
        grads[
            pl.ds(pl.multiple_of((4 + 2 * quarter) * piece, 2 * piece), 2 * piece), :
        ] = parts[j, piece:]
    new_mom[...] = muon_momentum * mom[...] + grads[...]
    replica = scalars[3]
    start = jnp.where(replica == 0, 4, jnp.where(replica == 1, 0, jnp.where(replica == 2, 8, 3)))
    count = jnp.where(replica == 1, 3, jnp.where(replica == 3, 1, 4)) * piece
    row = lax.broadcasted_iota(jnp.int32, (4 * piece, 1), 0)
    block = jnp.where(
        row < count, new_mom[pl.ds(pl.multiple_of(start * piece, piece), 4 * piece), :], 0.0
    )
    own[...] = block
    keep, send, total = gram
    total[...] = fdot(block, block, TN, precise)
    chips, share, _ = keep.shape
    for i, out in enumerate((keep, send)):
        for k in range(chips):
            at = lax.bitwise_xor(scalars[5], i) * chips + lax.rem(scalars[4] + k, chips)
            out[k] = total[pl.ds(pl.multiple_of(at * share, share), share), :]


def own_gradients(scalars, parts, mom, chips):
    rows = mom.shape[0]
    share = D // (2 * chips)
    return call(
        own_gradients_kernel,
        [((rows, D), f32)] * 2 + [((rows // 3, D), f32)] + [((chips, share, D), f32)] * 2,
        [((D, D), f32)],
        flops=10**9,
        data=4 << 20,
    )(scalars, parts, mom)


def factor_of(gram):
    diagonal = lax.broadcasted_iota(jnp.int32, (D, D), 0) == lax.broadcasted_iota(jnp.int32, (D, D), 1)
    eye = jnp.where(diagonal, 1.0, 0.0)
    scale = 1.0 / (jnp.sqrt(jnp.sum(gram * eye)) + ns_eps)
    gram = gram * (scale * scale)
    factor = eye * scale
    for step_index in range(NS_STEPS):
        square = fdot(gram, gram, NN, precise)
        poly = ns_coeffs[1] * gram + ns_coeffs[2] * square + ns_coeffs[0] * eye
        factor = poly * scale if step_index == 0 else fdot(poly, factor, NN, precise)
        if step_index + 1 < NS_STEPS:
            gram = fdot(poly, fdot(gram, poly, NN, precise), NN, precise)
    return factor


def update_kernel(scalars, mine, other, own, out, total):
    chips, share, _ = mine.shape
    for i, parts in enumerate((mine, other)):
        for k in range(chips):
            at = lax.bitwise_xor(scalars[5], i) * chips + lax.rem(scalars[4] + chips - k, chips)
            total[pl.ds(pl.multiple_of(at * share, share), share), :] = parts[k]
    replica = scalars[3]
    rate = jnp.where(replica == 1, 3.0**0.5, jnp.where(replica == 0, (FF / D) ** 0.5, 1.0))
    out[...] = fdot(own[...], factor_of(total[...]), NN, precise) * (-muon_rate * rate)


def update(scalars, mine, other, own):
    return call(
        update_kernel, [(own.shape, f32)], [((D, D), f32)], flops=3 * 10**10, data=4 << 20
    )(scalars, mine, other, own)[0]


def local(
    tokens,
    image_count,
    w_qkv,
    w_out,
    w_up,
    w_down,
    vectors,
    cotangent,
    mom_qkv,
    mom_out,
    mom_up,
    mom_down,
    mom_vectors,
):
    group_size = lax.axis_size("group")
    replicas = lax.axis_size("replica")
    group_index = lax.axis_index("group")
    replica_index = lax.axis_index("replica")
    chips = group_size // 2
    tok_rows = tokens.shape[0]
    slab_rows = group_size * tok_rows
    image_total = lax.dynamic_index_in_dim(image_count, replica_index, 0, keepdims=False)
    first_slot = group_index * tok_rows
    first_image = first_slot // L
    scalars = jnp.stack(
        [
            first_slot - first_image * L,
            slab_rows - first_image * L,
            image_total * L - first_slot,
            replica_index,
            group_index // 2,
            group_index % 2,
        ]
    ).astype(jnp.int32)

    def swap(x):
        return lax.ppermute(x, "group", [(i, i ^ 1) for i in range(group_size)])

    def rotate(x, by):
        return lax.ppermute(
            x, "group", [(i, (i + 2 * by) % group_size) for i in range(group_size)]
        )

    def cross(x, by):
        return lax.ppermute(x, "replica", [(i, i ^ by) for i in range(replicas)])

    def halo(x):
        ends = group_size - 1
        lower = lax.ppermute(x[tok_rows - HALO :], "group", [(i, i + 1) for i in range(ends)])
        upper = lax.ppermute(x[:HALO], "group", [(i + 1, i) for i in range(ends)])
        return lower, x, upper

    def along_chips(x):
        return jnp.stack([x] + [rotate(x, k) for k in range(1, chips)])

    def along_replicas(x):
        return jnp.stack([x] + [cross(x, j) for j in range(1, replicas)])

    width = D // group_size
    piece = 4 * width // replicas
    cuts = (3 * width, width, 4 * width, 4 * width)
    first_stack = jnp.concatenate([w_qkv.T, w_out.T], axis=0)
    second_stack = jnp.concatenate([w_up.T, w_down], axis=0)
    mom_stack = jnp.concatenate([mom_qkv.T, mom_out.T, mom_up.T, mom_down], axis=0)
    around = halo(tokens)

    def split(stack):
        one, two, three, four = (stack[sum(cuts[:i]) : sum(cuts[: i + 1])] for i in range(4))
        return one.T, two.T, three.T, four

    def finish(block_out, grad_tokens, grads, new_mom, dvec, updates):
        grad_vectors = lax.dynamic_slice_in_dim(dvec[:12], group_index * width, width, 1)
        new_vectors = vector_momentum * mom_vectors + grad_vectors
        return (
            block_out,
            grad_tokens,
            *split(grads),
            grad_vectors,
            *split(new_mom),
            new_vectors,
            *updates,
            -vector_rate * new_vectors,
        )

    if replicas != 4 or piece % 16:
        def rows_of(stack, inner):
            parts = lax.all_gather(stack, "group")
            rows = jnp.concatenate(
                [parts[:, :inner].reshape(-1, D), parts[:, inner:].reshape(-1, D)], axis=0
            )
            hi, lo = halves(rows)
            return jnp.concatenate([hi, lo, hi], axis=1)

        def shares_of(total, cut, inner):
            one, two = total[:cut], total[cut:]
            parts = jnp.concatenate(
                [one.reshape(group_size, inner, D), two.reshape(group_size, -1, D)], axis=1
            )
            return lax.psum_scatter(parts, "group", scatter_dimension=0)

        w_one, w_two = rows_of(first_stack, 3 * width), rows_of(second_stack, 4 * width)
        vec = jnp.pad(lax.all_gather(vectors, "group", axis=1, tiled=True), ((0, 4), (0, 0)))
        *saved, middle = attend(scalars, *around, w_one, vec)
        block_out, d_middle, *kept, dvec = mlp(
            scalars, middle, cotangent, w_two, vec, vec[8:12].reshape(1, FF)
        )
        second = mlp_grads(scalars, None, *kept)[0]
        first, grad_tokens, dvec = attend_back(
            scalars, None, halo(d_middle), w_one, vec, *saved, dvec
        )
        grads, dvec = lax.psum(
            (
                jnp.concatenate(
                    [shares_of(first, 3 * D, 3 * width), shares_of(second, FF, 4 * width)], axis=0
                ),
                lax.psum(dvec, "group"),
            ),
            "replica",
        )
        new_mom = muon_momentum * mom_stack + grads
        blocks = [new_mom[sum(cuts[:i]) : sum(cuts[: i + 1])] for i in range(4)]
        grams = lax.psum(jnp.stack([fdot(x, x, TN, precise) for x in blocks]), "group")
        updates = [
            fdot(x, factor_of(grams[i]), NN, precise) * (-muon_rate * rate)
            for i, (x, rate) in enumerate(zip(blocks, (3.0**0.5, 1.0, (FF / D) ** 0.5, 1.0)))
        ]
        updates = [x if i == 3 else x.T for i, x in enumerate(updates)]
        return finish(block_out, grad_tokens, grads, new_mom, dvec, updates)

    vec_block = jnp.pad(vectors.T, ((0, 0), (0, 116)))
    third = width // 3
    vec_block = jnp.concatenate([vec_block[s * third : (s + 1) * third] for s in range(3)], axis=1)
    my_first = lax.dynamic_slice_in_dim(first_stack, replica_index * piece, piece, 0)
    my_second = lax.dynamic_slice_in_dim(second_stack, replica_index * 2 * piece, 2 * piece, 0)

    def sum_parts(parts):
        t = parts[0] + sum(cross(parts[j], j) for j in range(1, replicas))
        return t[0] + sum(rotate(t[k], k) for k in range(1, chips))

    spread = along_chips(jnp.concatenate([my_first, vec_block], axis=0))
    vec_parts, first = spread[:, piece:], spread[:, :piece]
    first = [first] + [cross(first, j) for j in range(1, replicas)]
    second = [my_second] + [rotate(my_second, k) for k in range(1, chips)]
    *both, vec_parts = lax.optimization_barrier((*first, *second, vec_parts))
    first, second = jnp.stack(both[:replicas]), jnp.stack(both[replicas:])
    first_other, vec_other = swap(first), swap(vec_parts)
    second, first_other = lax.optimization_barrier((second, first_other))
    second = [second] + [cross(second, j) for j in range(1, replicas)]
    w_one, vec, bias = unpack(scalars, first, first_other, first_rows, vec_parts, vec_other)
    *saved, middle = attend(scalars, *around, w_one, vec)
    *second, middle = lax.optimization_barrier((*second, middle))
    second = jnp.stack(second)
    w_two = unpack(scalars, second, swap(second), second_rows)[0]
    block_out, d_middle, *kept, dvec = mlp(scalars, middle, cotangent, w_two, vec, bias)
    d_around = halo(d_middle)
    keep, send = mlp_grads(scalars, (replicas, chips, 2 * piece, D), *kept)
    second_sum = sum_parts(keep + swap(send))
    keep, send, grad_tokens, dvec = attend_back(
        scalars, (replicas, chips, piece, D), d_around, w_one, vec, *saved, dvec
    )
    first_sum = sum_parts(keep + swap(send))
    parts = along_replicas(jnp.concatenate([first_sum, second_sum], axis=0))
    grads, new_mom, own, keep, send = own_gradients(scalars, parts, mom_stack, chips)
    t = keep + swap(send)
    t = t[0] + sum(rotate(t[k], k) for k in range(1, chips))
    gram = along_chips(t)
    gram_other = swap(gram)
    gram, dvec = lax.optimization_barrier((gram, dvec))
    for axis, by in (("group", 1), ("replica", 1), ("replica", 2), ("group", 2), ("group", 4)):
        size = lax.axis_size(axis)
        dvec = dvec + lax.ppermute(dvec, axis, [(i, i ^ by) for i in range(size)])
    updates = along_replicas(update(scalars, gram, gram_other, own))

    def from_replica(owner, rows):
        at = lax.bitwise_xor(replica_index, owner)
        return lax.dynamic_index_in_dim(updates, at, 0, keepdims=False)[:rows]

    return finish(
        block_out,
        grad_tokens,
        grads,
        new_mom,
        dvec,
        (
            from_replica(1, 3 * width).T,
            from_replica(3, width).T,
            from_replica(0, 4 * width).T,
            from_replica(2, 4 * width),
        ),
    )


def solution(mesh):
    tokens, whole, columns, rows = P(("replica", "group"), None), P(), P(None, "group"), P("group", None)
    params = (columns, columns, columns, rows, columns)
    return jax.shard_map(
        local,
        mesh=mesh,
        in_specs=(tokens, whole, *params, tokens, *params),
        out_specs=(tokens, tokens, *params, *params, *params),
        check_vma=False,
    )
```

```python
import functools

import jax
import jax.numpy as jnp
from jax import lax
from jax.experimental import pallas as pl
from jax.experimental.pallas import tpu as pltpu
from jax.sharding import PartitionSpec as P

D = 384
HEADS = 6
HEAD_DIM = 64
FF = 1536
L = 197
NS_STEPS = 5
SLOTS = 4
SLOT = 208
HALO = 200
TILE = 256

f32, bf16 = jnp.float32, jnp.bfloat16
high = lax.Precision.HIGH
precise = lax.Precision.HIGHEST
ns_coeffs = (3.4445, -4.775, 2.0315)
norm_eps = 1e-06
ns_eps = 1e-07
muon_momentum = 0.95
vector_momentum = 0.9
muon_rate = 0.5
vector_rate = 0.001
mask_fill = -1e30

UPPER = ((0, 0), (0, 1), (0, 2), (1, 1), (1, 2), (2, 2))
NN = (((1,), (0,)), ((), ()))
NT = (((1,), (1,)), ((), ()))
TN = (((0,), (0,)), ((), ()))
VMEM = pl.BlockSpec(memory_space=pltpu.VMEM)
SMEM = pl.BlockSpec(memory_space=pltpu.SMEM)


def call(body, outs, scratch=(), flops=0, data=0):
    def run(scalars, *arrays):
        return pl.pallas_call(
            body,
            out_shape=[jax.ShapeDtypeStruct(s, t) for s, t in outs],
            in_specs=[SMEM] + [VMEM] * len(arrays),
            out_specs=[VMEM] * len(outs),
            scratch_shapes=[pltpu.VMEM(s, t) for s, t in scratch],
            compiler_params=pltpu.CompilerParams(vmem_limit_bytes=28 << 20),
            cost_estimate=pl.CostEstimate(flops=flops, bytes_accessed=data, transcendentals=0),
        )(scalars, *arrays)

    return run


def mm(a, b, dims):
    return lax.dot_general(a, b, dims, preferred_element_type=f32)


def fdot(a, b, dims, precision=high):
    return lax.dot_general(a, b, dims, precision=precision, preferred_element_type=f32)


def halves(x):
    hi = x.astype(bf16)
    return hi, (x - hi.astype(f32)).astype(bf16)


def triple(x):
    hi, lo = halves(x)
    return jnp.concatenate([hi, hi, lo], axis=1)


def by_rows(hi, lo, both):
    wide = mm(hi, both[:, : 2 * D], NN)
    return wide[:, :D] + wide[:, D:] + mm(lo, both[:, :D], NN)


def by_tokens(hi, lo, other):
    wide = mm(hi, other[:, D:], TN)
    return wide[:, :D] + wide[:, D:] + mm(lo, other[:, :D], TN)


def standardized(x):
    centered = x - jnp.mean(x, axis=-1, keepdims=True)
    rstd = lax.rsqrt(jnp.mean(centered * centered, axis=-1, keepdims=True) + norm_eps)
    return centered * rstd, rstd


def norm_back(d_norm, xhat, rstd, scale):
    g = d_norm * (1.0 + scale)
    return rstd * (
        g - jnp.mean(g, axis=-1, keepdims=True) - xhat * jnp.mean(g * xhat, axis=-1, keepdims=True)
    )


def row_sum(x):
    return jnp.sum(x, axis=0, keepdims=True)


def window_start(scalars, slot):
    start = HALO - scalars[0] + L * slot
    aligned = pl.multiple_of((start // 8) * 8, 8)
    return aligned, start - aligned


def fill_window(window, lower, own, upper):
    rows = own.shape[0]
    window[:HALO, :] = lower[...]
    window[HALO : HALO + rows, :] = own[...]
    window[HALO + rows : 2 * HALO + rows, :] = upper[...]
    window[2 * HALO + rows :, :] = jnp.zeros((window.shape[0] - 2 * HALO - rows, D), f32)


def load_slot(window, scalars, slot):
    aligned, shift = window_start(scalars, slot)
    block = window[pl.ds(aligned, SLOT + 8), :]
    return pltpu.roll(block, lax.rem(SLOT + 8 - shift, SLOT + 8), 0)[:SLOT]


def store_slot(window, scalars, slot, value):
    aligned, shift = window_start(scalars, slot)
    block = jnp.concatenate([value, jnp.zeros((8, value.shape[1]), f32)], axis=0)
    block = pltpu.roll(block, shift, 0)
    rows = lax.broadcasted_iota(jnp.int32, (SLOT + 8, 1), 0)
    window[pl.ds(aligned, SLOT + 8), :] = jnp.where(
        rows >= shift, block, window[pl.ds(aligned, SLOT + 8), :]
    )


def window_rows(rows):
    return 2 * HALO + rows + 96


def pairs(x):
    hi, lo = halves(x)
    return [
        jnp.concatenate([hi[:, at : at + HEAD_DIM], lo[:, at : at + HEAD_DIM]], axis=1)
        for at in range(0, D, HEAD_DIM)
    ]


def twice(x):
    return jnp.concatenate([x, x], axis=1)


def spread(x):
    hi, lo = x[:, :HEAD_DIM], x[:, HEAD_DIM:]
    return jnp.concatenate([hi, hi, lo, lo], axis=1)


def times(hi, lo, other):
    wide = mm(hi, other, NN)
    return wide[:, :HEAD_DIM] + wide[:, HEAD_DIM:] + mm(lo, other[:, :HEAD_DIM], NN)


def times_down(other, hi, lo):
    tall = mm(other, hi, NN)
    return tall[:HEAD_DIM] + tall[HEAD_DIM:] + mm(other[:HEAD_DIM], lo, NN)


def attend_kernel(
    scalars, lower, own, upper, w, vec, q2, kt2, v2, probs_hi, probs_lo, a3, middle, window, proj, att_win
):
    rows = own.shape[0]
    fill_window(window, lower, own, upper)
    step = (2 * HALO + rows) // 3

    def project_step(t, carry):
        at = pl.multiple_of(t * step, 16)
        xhat, _ = standardized(window[pl.ds(at, step), :])
        left = triple(xhat * (1.0 + vec[0:1, :]) + vec[1:2, :])
        for part, bias in ((0, vec[2:3, :]), (1, None), (2, vec[3:4, :])):
            value = mm(left, w[part * D : (part + 1) * D, :], NT)
            proj[pl.ds(at, step), part * D : (part + 1) * D] = value if bias is None else value + bias
        return carry

    lax.fori_loop(0, 3, project_step, 0)
    proj[2 * HALO + rows :, :] = jnp.zeros((96, 3 * D), f32)

    def slot_step(slot, carry):
        qkv = load_slot(proj, scalars, slot)
        keys = jnp.minimum(L, scalars[1] - L * slot)
        keep = lax.broadcasted_iota(jnp.int32, (SLOT, SLOT), 0) < keys
        q, k, v = (pairs(qkv[:, part * D : (part + 1) * D]) for part in range(3))
        heads = []
        for h in range(HEADS):
            q2[slot, h] = q[h]
            v2[slot, h] = v[h]
            kt2[slot, h] = jnp.transpose(k[h])
            scores = mm(twice(k[h]), spread(q[h]), NT) * HEAD_DIM**-0.5
            scores = jnp.where(keep, scores, mask_fill)
            weights = jnp.exp(scores - jnp.max(scores, axis=0, keepdims=True))
            weights = weights * (1.0 / jnp.sum(weights, axis=0, keepdims=True))
            hi, lo = halves(weights)
            probs_hi[slot, h] = hi
            probs_lo[slot, h] = lo
            heads.append(times_down(jnp.transpose(v[h]), hi, lo))
        store_slot(att_win, scalars, slot, jnp.transpose(jnp.concatenate(heads, axis=0)))
        return carry

    lax.fori_loop(0, SLOTS, slot_step, 0)
    att = triple(att_win[HALO : HALO + rows, :])
    a3[...] = att
    middle[...] = own[...] + mm(att, w[3 * D :, :], NT) + vec[4:5, :]


def attend(scalars, lower, own, upper, w, vec):
    rows = own.shape[0]
    return call(
        attend_kernel,
        [
            ((SLOTS, HEADS, SLOT, 128), bf16),
            ((SLOTS, HEADS, 128, SLOT), bf16),
            ((SLOTS, HEADS, SLOT, 128), bf16),
            ((SLOTS, HEADS, SLOT, SLOT), bf16),
            ((SLOTS, HEADS, SLOT, SLOT), bf16),
            ((rows, 3 * D), bf16),
            ((rows, D), f32),
        ],
        [
            ((window_rows(rows), D), f32),
            ((window_rows(rows), 3 * D), f32),
            ((window_rows(rows), D), f32),
        ],
        flops=10**8,
        data=1 << 18,
    )(scalars, lower, own, upper, w, vec)


def mlp_kernel(scalars, mid, cot, w, vec, bias, out, slope, n3, m3, *rest):
    parts, (total, acc) = rest[:-2], rest[-2:]
    if len(parts) == 1:
        total = parts[0]
    rows = mid.shape[0]
    xhat, _ = standardized(mid[...])
    n3[...] = triple(xhat * (1.0 + vec[5:6, :]) + vec[6:7, :])
    live = lax.broadcasted_iota(jnp.int32, (rows, 1), 0) < scalars[2]
    m3[...] = triple(jnp.where(live, cot[...], 0.0))
    acc[...] = jnp.zeros_like(acc)

    def tile_step(t, carry):
        at = pl.multiple_of(t * TILE, TILE)
        pre = mm(n3[...], w[pl.ds(at, TILE), :], NT) + bias[0:1, pl.ds(at, TILE)]
        cdf = 0.5 + 0.5 * lax.erf(pre * (0.5**0.5))
        slope[:, pl.ds(at, TILE)] = cdf + pre * (jnp.exp(-0.5 * pre * pre) * 0.3989422804014327)
        hi, lo = halves(pre * cdf)
        acc[...] += by_rows(hi, lo, w[pl.ds(FF + at, TILE), :])
        total[pl.ds(at, TILE), :] = by_tokens(hi, lo, m3)
        return carry

    lax.fori_loop(0, FF // TILE, tile_step, 0)
    out[...] = mid[...] + acc[...] + vec[7:8, :]
    scatter_parts(scalars, total, parts, quarter_rows)


def mlp(scalars, parts, mid, cot, w, vec, bias):
    rows = mid.shape[0]
    outs, scratch = part_outs(parts, FF)
    return call(
        mlp_kernel,
        [((rows, D), f32), ((rows, FF), f32)] + [((rows, 3 * D), bf16)] * 2 + outs,
        [scratch, ((rows, D), f32)],
        flops=10**8,
        data=1 << 18,
    )(scalars, mid, cot, w, vec, bias)


def mlp_back_kernel(scalars, mid, cot, w, vec, slope, m3, dmid, d_hi, d_lo, dvec, acc, dbias):
    rows = mid.shape[0]
    acc[...] = jnp.zeros_like(acc)

    def tile_step(t, carry):
        at = pl.multiple_of(t * TILE, TILE)
        d_pre = mm(m3[...], w[pl.ds(FF + at, TILE), :], NT) * slope[:, pl.ds(at, TILE)]
        dbias[0:1, pl.ds(at, TILE)] = row_sum(d_pre)
        hi, lo = halves(d_pre)
        d_hi[:, pl.ds(at, TILE)] = hi
        d_lo[:, pl.ds(at, TILE)] = lo
        acc[...] += by_rows(hi, lo, w[pl.ds(at, TILE), :])
        return carry

    lax.fori_loop(0, FF // TILE, tile_step, 0)
    d_norm = acc[...]
    xhat, rstd = standardized(mid[...])
    live = lax.broadcasted_iota(jnp.int32, (rows, 1), 0) < scalars[2]
    masked = jnp.where(live, cot[...], 0.0)
    d_middle = masked + norm_back(d_norm, xhat, rstd, vec[5:6, :])
    dmid[...] = d_middle
    zero = jnp.zeros((4, D), f32)
    dvec[...] = jnp.concatenate(
        [zero, row_sum(d_middle), row_sum(d_norm * xhat), row_sum(d_norm), row_sum(masked)]
        + [dbias[0:1, i * D : (i + 1) * D] for i in range(4)]
        + [zero],
        axis=0,
    )


def mlp_back(scalars, mid, cot, w, vec, slope, m3):
    rows = mid.shape[0]
    return call(
        mlp_back_kernel,
        [((rows, D), f32)] + [((rows, FF), bf16)] * 2 + [((16, D), f32)],
        [((rows, D), f32), ((8, FF), f32)],
        flops=10**8,
        data=1 << 18,
    )(scalars, mid, cot, w, vec, slope, m3)


def place(scalars, chips, i, j, k):
    owner = 2 * lax.rem(scalars[4] + k, chips) + lax.bitwise_xor(scalars[5], i)
    return owner, lax.bitwise_xor(scalars[3], j)


def first_rows(owner, quarter, piece):
    return pl.multiple_of(
        jnp.where(quarter < 3, owner * 3 * piece + quarter * piece, 3 * D + owner * piece), piece
    )


def second_rows(owner, quarter, piece):
    half = piece // 2
    at = owner * 4 * half + quarter * half
    return pl.multiple_of(at, half), pl.multiple_of(FF + at, half)


def quarter_rows(owner, quarter, piece):
    return pl.multiple_of(owner * 4 * piece + quarter * piece, piece)


def part_outs(parts, rows):
    if parts is None:
        return [((rows, D), f32)], ((8, D), f32)
    return [(parts, f32)] * 4 + [((4, *parts), f32)], ((rows, D), f32)


def scatter_parts(scalars, total, outs, rows_of):
    if len(outs) == 1:
        return
    chips, piece, _ = outs[0].shape
    for n in range(8):
        for k in range(chips):
            owner, quarter = place(scalars, chips, n // 4, n % 4, k)
            rows = total[pl.ds(rows_of(owner, quarter, piece), piece), :]
            if n < 4:
                outs[n][k] = rows
            else:
                outs[4][n - 4, k] = rows


def up_grads_kernel(scalars, d_hi, d_lo, n3, *rest):
    outs, total = rest[:-1], rest[-1]
    if len(outs) == 1:
        total = outs[0]

    def tile_step(t, carry):
        at = pl.multiple_of(t * TILE, TILE)
        total[pl.ds(at, TILE), :] = by_tokens(d_hi[:, pl.ds(at, TILE)], d_lo[:, pl.ds(at, TILE)], n3)
        return carry

    lax.fori_loop(0, FF // TILE, tile_step, 0)
    scatter_parts(scalars, total, outs, quarter_rows)


def up_grads(scalars, parts, *arrays):
    outs, scratch = part_outs(parts, FF)
    return call(up_grads_kernel, outs, [scratch], flops=10**8, data=1 << 18)(scalars, *arrays)


def attend_back_kernel(first_slot, scalars, lower, own, upper, w, q2, kt2, v2, probs_hi, probs_lo, out, window):
    rows = own.shape[0]
    fill_window(window, lower, own, upper)

    def slot_step(step, carry):
        slot = first_slot + step
        row = lax.broadcasted_iota(jnp.int32, (SLOT, 1), 0)
        at_own = row + L * slot - scalars[0]
        mine = (at_own >= 0) & (at_own < rows) & (row < L)
        d_mid = jnp.where(row < L, load_slot(window, scalars, slot), 0.0)
        d_out = pairs(by_rows(*halves(d_mid), w[3 * D :, :]))
        d_q, d_k, d_v = [], [], []
        for h in range(HEADS):
            hi, lo = probs_hi[slot, h], probs_lo[slot, h]
            weights = hi.astype(f32) + lo.astype(f32)
            d_weights = mm(twice(v2[slot, h]), spread(d_out[h]), NT)
            mean = jnp.sum(weights * d_weights, axis=0, keepdims=True)
            s_hi, s_lo = halves(weights * (d_weights - mean) * HEAD_DIM**-0.5)
            d_v.append(times(hi, lo, d_out[h]))
            d_k.append(times(s_hi, s_lo, q2[slot, h]))
            d_q.append(times_down(kt2[slot, h], s_hi, s_lo))
        d_q = jnp.transpose(jnp.concatenate(d_q, axis=0))
        d_proj = jnp.concatenate([d_q] + d_k + d_v, axis=1)
        out[step] = jnp.where(mine, d_proj, 0.0)
        return carry

    lax.fori_loop(0, out.shape[0], slot_step, 0)


def attend_back(scalars, first_slot, slots, around, w, *saved):
    rows = around[1].shape[0]
    return call(
        functools.partial(attend_back_kernel, first_slot),
        [((slots, SLOT, 3 * D), f32)],
        [((window_rows(rows), D), f32)],
        flops=10**8,
        data=1 << 18,
    )(scalars, *around, w, *saved)[0]


def attend_grads_kernel(scalars, some, more, tokens, d_mid, vec, a3, *rest):
    outs, (d_hi, d_lo, sums), (total, window) = rest[:-5], rest[-5:-2], rest[-2:]
    if len(outs) == 1:
        total = outs[0]
    rows = tokens.shape[0]
    for i, part in enumerate((some, more)):
        for step in range(part.shape[0]):
            store_slot(window, scalars, i * some.shape[0] + step, part[step])
    xhat, _ = standardized(tokens[...])
    n3 = triple(xhat * (1.0 + vec[0:1, :]) + vec[1:2, :])
    for part in range(3):
        d_proj = window[HALO : HALO + rows, part * D : (part + 1) * D]
        hi, lo = halves(d_proj)
        d_hi[:, part * D : (part + 1) * D] = hi
        d_lo[:, part * D : (part + 1) * D] = lo
        total[part * D : (part + 1) * D, :] = by_tokens(hi, lo, n3)
        if part != 1:
            sums[part // 2 : part // 2 + 1, :] = row_sum(d_proj)
    total[3 * D :, :] = by_tokens(*halves(d_mid[...]), a3)
    scatter_parts(scalars, total, outs, first_rows)


def attend_grads(scalars, parts, some, more, tokens, d_mid, vec, a3):
    rows = tokens.shape[0]
    outs, scratch = part_outs(parts, 4 * D)
    return call(
        attend_grads_kernel,
        outs + [((rows, 3 * D), bf16)] * 2 + [((8, D), f32)],
        [scratch, ((window_rows(rows), 3 * D), f32)],
        flops=10**8,
        data=1 << 18,
    )(scalars, some, more, tokens, d_mid, vec, a3)


def token_grads_kernel(scalars, d_hi, d_lo, w, tokens, d_mid, vec, sums, dvec_in, dtok, dvec):
    xhat, rstd = standardized(tokens[...])
    d_norm = by_rows(d_hi[...], d_lo[...], w[: 3 * D, :])
    dtok[...] = d_mid[...] + norm_back(d_norm, xhat, rstd, vec[0:1, :])
    new = [row_sum(d_norm * xhat), row_sum(d_norm), sums[0:2, :], jnp.zeros((12, D), f32)]
    dvec[...] = dvec_in[...] + jnp.concatenate(new, axis=0)


def token_grads(scalars, *arrays):
    rows = arrays[0].shape[0]
    return call(
        token_grads_kernel, [((rows, D), f32), ((16, D), f32)], flops=10**8, data=1 << 18
    )(scalars, *arrays)


def store_split(w, at, x):
    hi, lo = halves(x)
    w[pl.ds(at, x.shape[0]), :] = jnp.concatenate([hi, lo, hi], axis=1)


def unpack_kernel(rows_of, chips, piece, step, scalars, *refs):
    mine, other, rest = refs[:4], refs[4:8], refs[8:]
    if step:
        vectors, (w, vec, bias, flat) = rest[:2], rest[2:]
    else:
        (w,) = rest
    for i, parts in enumerate((mine, other)):
        for j in range(4):
            for k in range(chips):
                owner, quarter = place(scalars, chips, i, j, chips - k)
                at = rows_of(owner, quarter, piece)
                at = at if isinstance(at, tuple) else (at,)
                share = piece // len(at)
                for n, to in enumerate(at):
                    base = k * piece + n * share
                    store_split(w, to, parts[j][base : base + share, :])
    if step:
        for i, parts in enumerate(vectors):
            for k in range(chips):
                owner, _ = place(scalars, chips, i, 0, chips - k)
                for s in range(3):
                    flat[pl.ds(pl.multiple_of((owner * 3 + s) * step, step), step), :] = parts[
                        k * step : (k + 1) * step, s * 128 : (s + 1) * 128
                    ]
        rows = jnp.transpose(flat[...])[:16, :]
        vec[...] = rows
        bias[...] = jnp.concatenate([rows[8 + s : 9 + s, :] for s in range(4)], axis=1)


def unpack(scalars, chips, mine, other, rows_of, *vectors):
    total = 8 * mine[0].shape[0]
    outs = [((total, 3 * D), bf16)]
    if vectors:
        outs += [((16, D), f32), ((1, FF), f32)]
    return call(
        functools.partial(
            unpack_kernel,
            rows_of,
            chips,
            mine[0].shape[0] // chips,
            vectors[0].shape[0] // chips if vectors else 0,
        ),
        outs,
        [((D, 128), f32)] if vectors else [],
        flops=10**8,
        data=1 << 18,
    )(scalars, *mine, *other, *vectors)


def own_gradients_kernel(scalars, *refs):
    parts, (mom, grads, new_mom, own, *gram) = refs[:4], refs[4:]
    piece = own.shape[0] // 4
    for j in range(4):
        quarter = lax.bitwise_xor(scalars[3], j)
        grads[pl.ds(pl.multiple_of(quarter * piece, piece), piece), :] = parts[j][:piece, :]
        for n in (1, 2):
            grads[pl.ds(pl.multiple_of((4 * n + quarter) * piece, piece), piece), :] = parts[j][
                n * piece : (n + 1) * piece, :
            ]
    new_mom[...] = muon_momentum * mom[...] + grads[...]
    replica = scalars[3]
    start = jnp.where(replica == 0, 4, jnp.where(replica == 1, 0, jnp.where(replica == 2, 8, 3)))
    count = jnp.where(replica == 1, 3, jnp.where(replica == 3, 1, 4)) * piece
    row = lax.broadcasted_iota(jnp.int32, (4 * piece, 1), 0)
    block = jnp.where(
        row < count, new_mom[pl.ds(pl.multiple_of(start * piece, piece), 4 * piece), :], 0.0
    )
    own[...] = block
    keep, send, total = gram
    gram = fdot(block, block, TN, precise)
    for n, (row, column) in enumerate(UPPER):
        total[n * 128 : (n + 1) * 128, :] = gram[
            row * 128 : (row + 1) * 128, column * 128 : (column + 1) * 128
        ]
    chips, share, _ = keep.shape
    for i, out in enumerate((keep, send)):
        for k in range(chips):
            at = lax.bitwise_xor(scalars[5], i) * chips + lax.rem(scalars[4] + k, chips)
            out[k] = total[pl.ds(pl.multiple_of(at * share, share), share), :]


def own_gradients(scalars, parts, mom, chips):
    rows = mom.shape[0]
    share = 128 * len(UPPER) // (2 * chips)
    return call(
        own_gradients_kernel,
        [((rows, D), f32)] * 2 + [((rows // 3, D), f32)] + [((chips, share, 128), f32)] * 2,
        [((128 * len(UPPER), 128), f32)],
        flops=10**8,
        data=1 << 18,
    )(scalars, *parts, mom)


def pieces(x):
    hi, mid = halves(x)
    return hi, mid, (x - hi.astype(f32) - mid.astype(f32)).astype(bf16)


def full_product(a, b):
    (ah, am, al), (bh, bm, bl) = a, b
    return mm(
        jnp.concatenate([ah, ah, am, ah, al, am], axis=1),
        jnp.concatenate([bh, bm, bh, bl, bh, bm], axis=0),
        NN,
    )


def three_product(a, b):
    (ah, am, _), (bh, bm, _) = a, b
    return mm(
        jnp.concatenate([ah, am, ah], axis=1), jnp.concatenate([bh, bh, bm], axis=0), NN
    )


def polar(gram, block):
    diagonal = lax.broadcasted_iota(jnp.int32, (D, D), 0) == lax.broadcasted_iota(jnp.int32, (D, D), 1)
    eye = jnp.where(diagonal, 1.0, 0.0)
    scale = 1.0 / (jnp.sqrt(jnp.sum(gram * eye)) + ns_eps)
    gram = gram * (scale * scale)
    block = block * scale
    for step_index in range(NS_STEPS):
        more = step_index + 1 < NS_STEPS
        g = pieces(gram)
        square = (full_product if more else three_product)(g, g)
        poly = ns_coeffs[1] * gram + ns_coeffs[2] * square + ns_coeffs[0] * eye
        p = pieces(poly)
        if more:
            gram = full_product(p, pieces(full_product(p, g)))
        block = three_product(pieces(block), p)
    return block


def update_kernel(scalars, mine, other, own, out, total):
    chips, share, _ = mine.shape
    for i, parts in enumerate((mine, other)):
        for k in range(chips):
            at = lax.bitwise_xor(scalars[5], i) * chips + lax.rem(scalars[4] + chips - k, chips)
            total[pl.ds(pl.multiple_of(at * share, share), share), :] = parts[k]
    blocks = {}
    for n, (row, column) in enumerate(UPPER):
        blocks[row, column] = total[n * 128 : (n + 1) * 128, :]
        if row != column:
            blocks[column, row] = jnp.transpose(blocks[row, column])
    gram = jnp.concatenate(
        [jnp.concatenate([blocks[row, column] for column in range(3)], axis=1) for row in range(3)],
        axis=0,
    )
    replica = scalars[3]
    rate = jnp.where(replica == 1, 3.0**0.5, jnp.where(replica == 0, (FF / D) ** 0.5, 1.0))
    out[...] = polar(gram, own[...]) * (-muon_rate * rate)


def update(scalars, mine, other, own):
    return call(
        update_kernel, [(own.shape, f32)], [((128 * len(UPPER), 128), f32)], flops=10**8, data=1 << 18
    )(scalars, mine, other, own)[0]


def local(
    tokens,
    image_count,
    w_qkv,
    w_out,
    w_up,
    w_down,
    vectors,
    cotangent,
    mom_qkv,
    mom_out,
    mom_up,
    mom_down,
    mom_vectors,
):
    group_size = lax.axis_size("group")
    replicas = lax.axis_size("replica")
    group_index = lax.axis_index("group")
    replica_index = lax.axis_index("replica")
    chips = group_size // 2
    tok_rows = tokens.shape[0]
    slab_rows = group_size * tok_rows
    image_total = lax.dynamic_index_in_dim(image_count, replica_index, 0, keepdims=False)
    first_slot = group_index * tok_rows
    first_image = first_slot // L
    scalars = jnp.stack(
        [
            first_slot - first_image * L,
            slab_rows - first_image * L,
            image_total * L - first_slot,
            replica_index,
            group_index // 2,
            group_index % 2,
        ]
    ).astype(jnp.int32)

    def swap(x):
        return lax.ppermute(x, "group", [(i, i ^ 1) for i in range(group_size)])

    def rotate(x, by):
        return lax.ppermute(
            x, "group", [(i, (i + 2 * by) % group_size) for i in range(group_size)]
        )

    def cross(x, by):
        return lax.ppermute(x, "replica", [(i, i ^ by) for i in range(replicas)])

    def halo(x):
        ends = group_size - 1
        lower = lax.ppermute(x[tok_rows - HALO :], "group", [(i, i + 1) for i in range(ends)])
        upper = lax.ppermute(x[:HALO], "group", [(i + 1, i) for i in range(ends)])
        return lower, x, upper

    def along_chips(x):
        return jnp.stack([x] + [rotate(x, k) for k in range(1, chips)])

    width = D // group_size
    piece = 4 * width // replicas
    cuts = (3 * width, width, 4 * width, 4 * width)
    first_stack = jnp.concatenate([w_qkv.T, w_out.T], axis=0)
    second_stack = jnp.concatenate([w_up.T, w_down], axis=0)
    mom_stack = jnp.concatenate([mom_qkv.T, mom_out.T, mom_up.T, mom_down], axis=0)
    around = halo(tokens)

    def split(stack):
        one, two, three, four = (stack[sum(cuts[:i]) : sum(cuts[: i + 1])] for i in range(4))
        return one.T, two.T, three.T, four

    def finish(block_out, grad_tokens, grads, new_mom, dvec, updates):
        grad_vectors = lax.dynamic_slice_in_dim(dvec[:12], group_index * width, width, 1)
        new_vectors = vector_momentum * mom_vectors + grad_vectors
        return (
            block_out,
            grad_tokens,
            *split(grads),
            grad_vectors,
            *split(new_mom),
            new_vectors,
            *updates,
            -vector_rate * new_vectors,
        )

    if replicas != 4 or piece % 16:
        def rows_of(stack, inner):
            parts = lax.all_gather(stack, "group")
            rows = jnp.concatenate(
                [parts[:, :inner].reshape(-1, D), parts[:, inner:].reshape(-1, D)], axis=0
            )
            hi, lo = halves(rows)
            return jnp.concatenate([hi, lo, hi], axis=1)

        def shares_of(total, cut, inner):
            one, two = total[:cut], total[cut:]
            parts = jnp.concatenate(
                [one.reshape(group_size, inner, D), two.reshape(group_size, -1, D)], axis=1
            )
            return lax.psum_scatter(parts, "group", scatter_dimension=0)

        w_one, w_two = rows_of(first_stack, 3 * width), rows_of(second_stack, 4 * width)
        vec = jnp.pad(lax.all_gather(vectors, "group", axis=1, tiled=True), ((0, 4), (0, 0)))
        *saved, a3, middle = attend(scalars, *around, w_one, vec)
        block_out, slope, n3, m3, down = mlp(
            scalars, None, middle, cotangent, w_two, vec, vec[8:12].reshape(1, FF)
        )
        d_middle, d_hi, d_lo, dvec = mlp_back(scalars, middle, cotangent, w_two, vec, slope, m3)
        second = jnp.concatenate([up_grads(scalars, None, d_hi, d_lo, n3)[0], down], axis=0)
        d_around = halo(d_middle)
        some, more = (attend_back(scalars, i, 2, d_around, w_one, *saved) for i in (0, 2))
        first, d_hi, d_lo, sums = attend_grads(
            scalars, None, some, more, tokens, d_middle, vec, a3
        )
        grad_tokens, dvec = token_grads(
            scalars, d_hi, d_lo, w_one, tokens, d_middle, vec, sums, dvec
        )
        grads, dvec = lax.psum(
            (
                jnp.concatenate(
                    [shares_of(first, 3 * D, 3 * width), shares_of(second, FF, 4 * width)], axis=0
                ),
                lax.psum(dvec, "group"),
            ),
            "replica",
        )
        new_mom = muon_momentum * mom_stack + grads
        blocks = [new_mom[sum(cuts[:i]) : sum(cuts[: i + 1])] for i in range(4)]
        grams = lax.psum(jnp.stack([fdot(x, x, TN, precise) for x in blocks]), "group")
        updates = [
            polar(grams[i], x) * (-muon_rate * rate)
            for i, (x, rate) in enumerate(zip(blocks, (3.0**0.5, 1.0, (FF / D) ** 0.5, 1.0)))
        ]
        updates = [x if i == 3 else x.T for i, x in enumerate(updates)]
        return finish(block_out, grad_tokens, grads, new_mom, dvec, updates)

    vec_block = jnp.pad(vectors.T, ((0, 0), (0, 116)))
    third = width // 3
    vec_block = jnp.concatenate([vec_block[s * third : (s + 1) * third] for s in range(3)], axis=1)
    my_first = lax.dynamic_slice_in_dim(first_stack, replica_index * piece, piece, 0)
    my_second = jnp.concatenate(
        [
            lax.dynamic_slice_in_dim(second_stack, (4 * n + replica_index) * piece, piece, 0)
            for n in range(2)
        ],
        axis=0,
    )

    others = range(1, replicas)
    start = jnp.concatenate([my_first, vec_block], axis=0)
    start = [start] + [rotate(start, k) for k in range(1, chips)]
    first = jnp.concatenate([x[:piece] for x in start], axis=0)
    vec_parts = jnp.concatenate([x[piece:] for x in start], axis=0)
    first, vec_parts, my_second, lower, upper, scalars = lax.optimization_barrier(
        (first, vec_parts, my_second, around[0], around[2], scalars)
    )
    around = lower, tokens, upper
    first_other, vec_other = [swap(first)], swap(vec_parts)
    first = [first] + [cross(first, j) for j in others]
    second = [my_second] + [rotate(my_second, k) for k in range(1, chips)]
    first[1:], second = lax.optimization_barrier((first[1:], second))
    second = jnp.concatenate(second, axis=0)
    second = [second] + [cross(second, j) for j in others]
    second_other = [swap(second[0])]
    first_other += [swap(first[j]) for j in others]
    w_one, vec, bias = unpack(
        scalars, chips, first, first_other, first_rows, vec_parts, vec_other
    )
    *saved, a3, middle = attend(scalars, *around, w_one, vec)
    for j in others:
        second[j], middle = lax.optimization_barrier((second[j], middle))
        second_other.append(swap(second[j]))
    w_two = unpack(scalars, chips, second, second_other, second_rows)[0]
    shape = (chips, piece, D)

    def join(keep, other):
        return [x + other[j] for j, x in enumerate(keep)]

    def exchange(parts):
        return [parts[0]] + [cross(parts[j], j) for j in others]

    block_out, slope, n3, m3, *keep, send = mlp(
        scalars, shape, middle, cotangent, w_two, vec, bias
    )
    other = swap(send)
    d_middle, d_hi, d_lo, dvec = mlp_back(scalars, middle, cotangent, w_two, vec, slope, m3)
    down, d_middle, d_hi = lax.optimization_barrier((join(keep, other), d_middle, d_hi))
    down = exchange(down)
    d_around = halo(d_middle)
    *keep, send = up_grads(scalars, shape, d_hi, d_lo, n3)
    keep, send, d_around = lax.optimization_barrier((keep, send, d_around))
    other = swap(send)
    some = attend_back(scalars, 0, 2, d_around, w_one, *saved)
    up, some, d_around = lax.optimization_barrier((join(keep, other), some, d_around))
    up = exchange(up)
    more = attend_back(scalars, 2, 2, d_around, w_one, *saved)
    *keep, send, d_hi, d_lo, sums = attend_grads(
        scalars, shape, some, more, tokens, d_middle, vec, a3
    )
    grad_tokens, dvec = token_grads(scalars, d_hi, d_lo, w_one, tokens, d_middle, vec, sums, dvec)
    keep, send, dvec, up, down = lax.optimization_barrier((keep, send, dvec, up, down))
    first = exchange(join(keep, swap(send)))
    dvec = dvec + swap(dvec)

    def over_chips(parts, *extra):
        parts = [
            jnp.concatenate([sum((x[k] for x in parts[1:]), parts[0][k]), *extra], axis=0)
            for k in range(chips)
        ]
        return sum((rotate(parts[k], k) for k in range(1, chips)), parts[0])

    down_sum, up_sum = over_chips(down), over_chips(up)
    first_sum = over_chips(first, dvec)
    sums = jnp.concatenate([first_sum[:piece], up_sum, down_sum, first_sum[piece:]], axis=0)
    parts = [sums] + [cross(sums, j) for j in others]
    dvec = sum((x[3 * piece :] for x in parts[1:]), parts[0][3 * piece :])
    grads, new_mom, own, keep, send = own_gradients(scalars, parts, mom_stack, chips)
    t = keep + swap(send)
    t = t[0] + sum(rotate(t[k], k) for k in range(1, chips))
    gram = along_chips(t)
    update_own = update(scalars, gram, swap(gram), own)
    updates = [update_own] + [cross(update_own, j) for j in others]

    def from_replica(owner, rows):
        at = lax.bitwise_xor(replica_index, owner)
        return lax.select_n(at, *(x[:rows] for x in updates))

    return finish(
        block_out,
        grad_tokens,
        grads,
        new_mom,
        dvec,
        (
            from_replica(1, 3 * width).T,
            from_replica(3, width).T,
            from_replica(0, 4 * width).T,
            from_replica(2, 4 * width),
        ),
    )


def solution(mesh):
    tokens, whole, columns, rows = P(("replica", "group"), None), P(), P(None, "group"), P("group", None)
    params = (columns, columns, columns, rows, columns)
    return jax.shard_map(
        local,
        mesh=mesh,
        in_specs=(tokens, whole, *params, tokens, *params),
        out_specs=(tokens, tokens, *params, *params, *params),
        check_vma=False,
    )
```

```python
import functools

import jax
import jax.numpy as jnp
from jax import lax
from jax.experimental import pallas as pl
from jax.experimental.pallas import tpu as pltpu
from jax.sharding import PartitionSpec as P

D = 384
HEADS = 6
HEAD_DIM = 64
FF = 1536
L = 197
NS_STEPS = 5
SLOTS = 4
SLOT = 208
HALO = 200
TILE = 512

f32, bf16 = jnp.float32, jnp.bfloat16
high = lax.Precision.HIGH
precise = lax.Precision.HIGHEST
ns_coeffs = (3.4445, -4.775, 2.0315)
norm_eps = 1e-06
ns_eps = 1e-07
muon_momentum = 0.95
vector_momentum = 0.9
muon_rate = 0.5
vector_rate = 0.001
mask_fill = -1e30

UPPER = ((0, 0), (0, 1), (0, 2), (1, 1), (1, 2), (2, 2))
NN = (((1,), (0,)), ((), ()))
NT = (((1,), (1,)), ((), ()))
TN = (((0,), (0,)), ((), ()))
VMEM = pl.BlockSpec(memory_space=pltpu.VMEM)
SMEM = pl.BlockSpec(memory_space=pltpu.SMEM)


def call(body, outs, scratch=(), flops=0, data=0):
    def run(scalars, *arrays):
        return pl.pallas_call(
            body,
            out_shape=[jax.ShapeDtypeStruct(s, t) for s, t in outs],
            in_specs=[SMEM] + [VMEM] * len(arrays),
            out_specs=[VMEM] * len(outs),
            scratch_shapes=[pltpu.VMEM(s, t) for s, t in scratch],
            compiler_params=pltpu.CompilerParams(vmem_limit_bytes=28 << 20),
            cost_estimate=pl.CostEstimate(flops=flops, bytes_accessed=data, transcendentals=0),
        )(scalars, *arrays)

    return run


def mm(a, b, dims):
    return lax.dot_general(a, b, dims, preferred_element_type=f32)


def fdot(a, b, dims, precision=high):
    return lax.dot_general(a, b, dims, precision=precision, preferred_element_type=f32)


def halves(x):
    hi = x.astype(bf16)
    return hi, (x - hi.astype(f32)).astype(bf16)


def triple(x):
    hi, lo = halves(x)
    return jnp.concatenate([hi, hi, lo], axis=1)


def by_rows(hi, lo, both):
    wide = mm(hi, both[:, : 2 * D], NN)
    return wide[:, :D] + wide[:, D:] + mm(lo, both[:, :D], NN)


def by_tokens(hi, lo, other):
    wide = mm(hi, other[:, D:], TN)
    return wide[:, :D] + wide[:, D:] + mm(lo, other[:, :D], TN)


def standardized(x):
    centered = x - jnp.mean(x, axis=-1, keepdims=True)
    rstd = lax.rsqrt(jnp.mean(centered * centered, axis=-1, keepdims=True) + norm_eps)
    return centered * rstd, rstd


def norm_back(d_norm, xhat, rstd, scale):
    g = d_norm * (1.0 + scale)
    return rstd * (
        g - jnp.mean(g, axis=-1, keepdims=True) - xhat * jnp.mean(g * xhat, axis=-1, keepdims=True)
    )


def row_sum(x):
    return jnp.sum(x, axis=0, keepdims=True)


def window_start(scalars, slot):
    start = HALO - scalars[0] + L * slot
    aligned = pl.multiple_of((start // 8) * 8, 8)
    return aligned, start - aligned


def fill_window(window, lower, own, upper):
    rows = own.shape[0]
    window[:HALO, :] = lower[...]
    window[HALO : HALO + rows, :] = own[...]
    window[HALO + rows : 2 * HALO + rows, :] = upper[...]
    window[2 * HALO + rows :, :] = jnp.zeros((window.shape[0] - 2 * HALO - rows, D), f32)


def load_slot(window, scalars, slot):
    aligned, shift = window_start(scalars, slot)
    block = window[pl.ds(aligned, SLOT + 8), :]
    return pltpu.roll(block, lax.rem(SLOT + 8 - shift, SLOT + 8), 0)[:SLOT]


def store_slot(window, scalars, slot, value):
    aligned, shift = window_start(scalars, slot)
    block = jnp.concatenate([value, jnp.zeros((8, value.shape[1]), f32)], axis=0)
    block = pltpu.roll(block, shift, 0)
    rows = lax.broadcasted_iota(jnp.int32, (SLOT + 8, 1), 0)
    window[pl.ds(aligned, SLOT + 8), :] = jnp.where(
        rows >= shift, block, window[pl.ds(aligned, SLOT + 8), :]
    )


def window_rows(rows):
    return 2 * HALO + rows + 96


def pairs(x):
    hi, lo = halves(x)
    return [
        jnp.concatenate([hi[:, at : at + HEAD_DIM], lo[:, at : at + HEAD_DIM]], axis=1)
        for at in range(0, D, HEAD_DIM)
    ]


def twice(x):
    return jnp.concatenate([x, x], axis=1)


def spread(x):
    hi, lo = x[:, :HEAD_DIM], x[:, HEAD_DIM:]
    return jnp.concatenate([hi, hi, lo, lo], axis=1)


def times(hi, lo, other):
    wide = mm(hi, other, NN)
    return wide[:, :HEAD_DIM] + wide[:, HEAD_DIM:] + mm(lo, other[:, :HEAD_DIM], NN)


def times_down(other, hi, lo):
    tall = mm(other, hi, NN)
    return tall[:HEAD_DIM] + tall[HEAD_DIM:] + mm(other[:HEAD_DIM], lo, NN)


def attend_kernel(
    scalars, lower, own, upper, w, vec, q2, kt2, v2, probs_hi, probs_lo, a3, middle, window, proj, att_win
):
    rows = own.shape[0]
    fill_window(window, lower, own, upper)
    step = (2 * HALO + rows) // 3

    def project_step(t, carry):
        at = pl.multiple_of(t * step, 16)
        xhat, _ = standardized(window[pl.ds(at, step), :])
        left = triple(xhat * (1.0 + vec[0:1, :]) + vec[1:2, :])
        for part, bias in ((0, vec[2:3, :]), (1, None), (2, vec[3:4, :])):
            value = mm(left, w[part * D : (part + 1) * D, :], NT)
            proj[pl.ds(at, step), part * D : (part + 1) * D] = value if bias is None else value + bias
        return carry

    lax.fori_loop(0, 3, project_step, 0)
    proj[2 * HALO + rows :, :] = jnp.zeros((96, 3 * D), f32)

    def slot_step(slot, carry):
        qkv = load_slot(proj, scalars, slot)
        keys = jnp.minimum(L, scalars[1] - L * slot)
        keep = lax.broadcasted_iota(jnp.int32, (SLOT, SLOT), 0) < keys
        q, k, v = (pairs(qkv[:, part * D : (part + 1) * D]) for part in range(3))
        heads = []
        for h in range(HEADS):
            q2[slot, h] = q[h]
            v2[slot, h] = v[h]
            kt2[slot, h] = jnp.transpose(k[h])
            scores = mm(twice(k[h]), spread(q[h]), NT) * HEAD_DIM**-0.5
            scores = jnp.where(keep, scores, mask_fill)
            weights = jnp.exp(scores - jnp.max(scores, axis=0, keepdims=True))
            weights = weights * (1.0 / jnp.sum(weights, axis=0, keepdims=True))
            hi, lo = halves(weights)
            probs_hi[slot, h] = hi
            probs_lo[slot, h] = lo
            heads.append(times_down(jnp.transpose(v[h]), hi, lo))
        store_slot(att_win, scalars, slot, jnp.transpose(jnp.concatenate(heads, axis=0)))
        return carry

    lax.fori_loop(0, SLOTS, slot_step, 0)
    att = triple(att_win[HALO : HALO + rows, :])
    a3[...] = att
    middle[...] = own[...] + mm(att, w[3 * D :, :], NT) + vec[4:5, :]


def attend(scalars, lower, own, upper, w, vec):
    rows = own.shape[0]
    return call(
        attend_kernel,
        [
            ((SLOTS, HEADS, SLOT, 128), bf16),
            ((SLOTS, HEADS, 128, SLOT), bf16),
            ((SLOTS, HEADS, SLOT, 128), bf16),
            ((SLOTS, HEADS, SLOT, SLOT), bf16),
            ((SLOTS, HEADS, SLOT, SLOT), bf16),
            ((rows, 3 * D), bf16),
            ((rows, D), f32),
        ],
        [
            ((window_rows(rows), D), f32),
            ((window_rows(rows), 3 * D), f32),
            ((window_rows(rows), D), f32),
        ],
        flops=10**8,
        data=1 << 18,
    )(scalars, lower, own, upper, w, vec)


def mlp_kernel(scalars, mid, cot, w, vec, bias, out, slope, n3, m3, *rest):
    parts, (total, h_hi, h_lo) = rest[:-3], rest[-3:]
    if len(parts) == 1:
        total = parts[0]
    rows = mid.shape[0]
    xhat, _ = standardized(mid[...])
    n3[...] = triple(xhat * (1.0 + vec[5:6, :]) + vec[6:7, :])
    live = lax.broadcasted_iota(jnp.int32, (rows, 1), 0) < scalars[2]
    m3[...] = triple(jnp.where(live, cot[...], 0.0))

    def tile_step(t, carry):
        at = pl.multiple_of(t * TILE, TILE)
        pre = mm(n3[...], w[pl.ds(at, TILE), :], NT) + bias[0:1, pl.ds(at, TILE)]
        cdf = 0.5 + 0.5 * lax.erf(pre * (0.5**0.5))
        slope[:, pl.ds(at, TILE)] = cdf + pre * (jnp.exp(-0.5 * pre * pre) * 0.3989422804014327)
        hi, lo = halves(pre * cdf)
        h_hi[:, pl.ds(at, TILE)] = hi
        h_lo[:, pl.ds(at, TILE)] = lo
        total[pl.ds(at, TILE), :] = by_tokens(hi, lo, m3)
        return carry

    lax.fori_loop(0, FF // TILE, tile_step, 0)
    out[...] = mid[...] + by_rows(h_hi[...], h_lo[...], w[FF:, :]) + vec[7:8, :]
    scatter_parts(scalars, total, parts, quarter_rows)


def mlp(scalars, parts, mid, cot, w, vec, bias):
    rows = mid.shape[0]
    outs, scratch = part_outs(parts, FF)
    return call(
        mlp_kernel,
        [((rows, D), f32), ((rows, FF), f32)] + [((rows, 3 * D), bf16)] * 2 + outs,
        [scratch] + [((rows, FF), bf16)] * 2,
        flops=10**8,
        data=1 << 18,
    )(scalars, mid, cot, w, vec, bias)


def mlp_back_kernel(scalars, mid, cot, w, vec, slope, m3, dmid, d_hi, d_lo, dvec, dbias):
    rows = mid.shape[0]

    def tile_step(t, carry):
        at = pl.multiple_of(t * TILE, TILE)
        d_pre = mm(m3[...], w[pl.ds(FF + at, TILE), :], NT) * slope[:, pl.ds(at, TILE)]
        dbias[0:1, pl.ds(at, TILE)] = row_sum(d_pre)
        hi, lo = halves(d_pre)
        d_hi[:, pl.ds(at, TILE)] = hi
        d_lo[:, pl.ds(at, TILE)] = lo
        return carry

    lax.fori_loop(0, FF // TILE, tile_step, 0)
    d_norm = by_rows(d_hi[...], d_lo[...], w[:FF, :])
    xhat, rstd = standardized(mid[...])
    live = lax.broadcasted_iota(jnp.int32, (rows, 1), 0) < scalars[2]
    masked = jnp.where(live, cot[...], 0.0)
    d_middle = masked + norm_back(d_norm, xhat, rstd, vec[5:6, :])
    dmid[...] = d_middle
    zero = jnp.zeros((4, D), f32)
    dvec[...] = jnp.concatenate(
        [zero, row_sum(d_middle), row_sum(d_norm * xhat), row_sum(d_norm), row_sum(masked)]
        + [dbias[0:1, i * D : (i + 1) * D] for i in range(4)]
        + [zero],
        axis=0,
    )


def mlp_back(scalars, mid, cot, w, vec, slope, m3):
    rows = mid.shape[0]
    return call(
        mlp_back_kernel,
        [((rows, D), f32)] + [((rows, FF), bf16)] * 2 + [((16, D), f32)],
        [((8, FF), f32)],
        flops=10**8,
        data=1 << 18,
    )(scalars, mid, cot, w, vec, slope, m3)


def place(scalars, chips, i, j, k):
    owner = 2 * lax.rem(scalars[4] + k, chips) + lax.bitwise_xor(scalars[5], i)
    return owner, lax.bitwise_xor(scalars[3], j)


def first_rows(owner, quarter, piece):
    return pl.multiple_of(
        jnp.where(quarter < 3, owner * 3 * piece + quarter * piece, 3 * D + owner * piece), piece
    )


def second_rows(owner, quarter, piece):
    half = piece // 2
    at = owner * 4 * half + quarter * half
    return pl.multiple_of(at, half), pl.multiple_of(FF + at, half)


def quarter_rows(owner, quarter, piece):
    return pl.multiple_of(owner * 4 * piece + quarter * piece, piece)


def part_outs(parts, rows):
    if parts is None:
        return [((rows, D), f32)], ((8, D), f32)
    return [(parts, f32)] * 4 + [((4, *parts), f32)], ((rows, D), f32)


def scatter_parts(scalars, total, outs, rows_of):
    if len(outs) == 1:
        return
    chips, piece, _ = outs[0].shape
    for n in range(8):
        for k in range(chips):
            owner, quarter = place(scalars, chips, n // 4, n % 4, k)
            rows = total[pl.ds(rows_of(owner, quarter, piece), piece), :]
            if n < 4:
                outs[n][k] = rows
            else:
                outs[4][n - 4, k] = rows


def up_grads_kernel(scalars, d_hi, d_lo, n3, *rest):
    outs, total = rest[:-1], rest[-1]
    if len(outs) == 1:
        total = outs[0]

    def tile_step(t, carry):
        at = pl.multiple_of(t * TILE, TILE)
        total[pl.ds(at, TILE), :] = by_tokens(d_hi[:, pl.ds(at, TILE)], d_lo[:, pl.ds(at, TILE)], n3)
        return carry

    lax.fori_loop(0, FF // TILE, tile_step, 0)
    scatter_parts(scalars, total, outs, quarter_rows)


def up_grads(scalars, parts, *arrays):
    outs, scratch = part_outs(parts, FF)
    return call(up_grads_kernel, outs, [scratch], flops=10**8, data=1 << 18)(scalars, *arrays)


def attend_back_kernel(first_slot, scalars, lower, own, upper, w, q2, kt2, v2, probs_hi, probs_lo, out, window):
    rows = own.shape[0]
    fill_window(window, lower, own, upper)

    def slot_step(step, carry):
        slot = first_slot + step
        row = lax.broadcasted_iota(jnp.int32, (SLOT, 1), 0)
        at_own = row + L * slot - scalars[0]
        mine = (at_own >= 0) & (at_own < rows) & (row < L)
        d_mid = jnp.where(row < L, load_slot(window, scalars, slot), 0.0)
        d_out = pairs(by_rows(*halves(d_mid), w[3 * D :, :]))
        d_q, d_k, d_v = [], [], []
        for h in range(HEADS):
            hi, lo = probs_hi[slot, h], probs_lo[slot, h]
            weights = hi.astype(f32) + lo.astype(f32)
            d_weights = mm(twice(v2[slot, h]), spread(d_out[h]), NT)
            mean = jnp.sum(weights * d_weights, axis=0, keepdims=True)
            s_hi, s_lo = halves(weights * (d_weights - mean) * HEAD_DIM**-0.5)
            d_v.append(times(hi, lo, d_out[h]))
            d_k.append(times(s_hi, s_lo, q2[slot, h]))
            d_q.append(times_down(kt2[slot, h], s_hi, s_lo))
        d_q = jnp.transpose(jnp.concatenate(d_q, axis=0))
        d_proj = jnp.concatenate([d_q] + d_k + d_v, axis=1)
        out[step] = jnp.where(mine, d_proj, 0.0)
        return carry

    lax.fori_loop(0, out.shape[0], slot_step, 0)


def attend_back(scalars, first_slot, slots, around, w, *saved):
    rows = around[1].shape[0]
    return call(
        functools.partial(attend_back_kernel, first_slot),
        [((slots, SLOT, 3 * D), f32)],
        [((window_rows(rows), D), f32)],
        flops=10**8,
        data=1 << 18,
    )(scalars, *around, w, *saved)[0]


def attend_grads_kernel(scalars, some, more, tokens, d_mid, vec, a3, *rest):
    outs, (d_hi, d_lo, sums), (total, window) = rest[:-5], rest[-5:-2], rest[-2:]
    if len(outs) == 1:
        total = outs[0]
    rows = tokens.shape[0]
    for i, part in enumerate((some, more)):

        def slot_step(step, carry, i=i, part=part):
            store_slot(window, scalars, i * part.shape[0] + step, part[step])
            return carry

        lax.fori_loop(0, part.shape[0], slot_step, 0)
    xhat, _ = standardized(tokens[...])
    n3 = triple(xhat * (1.0 + vec[0:1, :]) + vec[1:2, :])

    def part_step(part, carry):
        at = pl.ds(pl.multiple_of(part * D, D), D)
        d_proj = window[HALO : HALO + rows, at]
        hi, lo = halves(d_proj)
        d_hi[:, at] = hi
        d_lo[:, at] = lo
        total[at, :] = by_tokens(hi, lo, n3)
        sums[part] = jnp.broadcast_to(row_sum(d_proj), (8, D))
        return carry

    lax.fori_loop(0, 3, part_step, 0)
    total[3 * D :, :] = by_tokens(*halves(d_mid[...]), a3)
    scatter_parts(scalars, total, outs, first_rows)


def attend_grads(scalars, parts, some, more, tokens, d_mid, vec, a3):
    rows = tokens.shape[0]
    outs, scratch = part_outs(parts, 4 * D)
    return call(
        attend_grads_kernel,
        outs + [((rows, 3 * D), bf16)] * 2 + [((3, 8, D), f32)],
        [scratch, ((window_rows(rows), 3 * D), f32)],
        flops=10**8,
        data=1 << 18,
    )(scalars, some, more, tokens, d_mid, vec, a3)


def token_grads_kernel(scalars, d_hi, d_lo, w, tokens, d_mid, vec, sums, dvec_in, dtok, dvec):
    xhat, rstd = standardized(tokens[...])
    d_norm = by_rows(d_hi[...], d_lo[...], w[: 3 * D, :])
    dtok[...] = d_mid[...] + norm_back(d_norm, xhat, rstd, vec[0:1, :])
    new = [row_sum(d_norm * xhat), row_sum(d_norm), sums[0, 0:1], sums[2, 0:1], jnp.zeros((12, D), f32)]
    dvec[...] = dvec_in[...] + jnp.concatenate(new, axis=0)


def token_grads(scalars, *arrays):
    rows = arrays[0].shape[0]
    return call(
        token_grads_kernel, [((rows, D), f32), ((16, D), f32)], flops=10**8, data=1 << 18
    )(scalars, *arrays)


def store_split(w, at, x):
    hi, lo = halves(x)
    w[pl.ds(at, x.shape[0]), :] = jnp.concatenate([hi, lo, hi], axis=1)


def unpack_kernel(rows_of, chips, piece, step, scalars, *refs):
    mine, other, rest = refs[:4], refs[4:8], refs[8:]
    if step:
        vectors, (w, vec, bias, flat) = rest[:2], rest[2:]
    else:
        (w,) = rest
    for i, parts in enumerate((mine, other)):
        for j in range(4):
            for k in range(chips):
                owner, quarter = place(scalars, chips, i, j, chips - k)
                at = rows_of(owner, quarter, piece)
                at = at if isinstance(at, tuple) else (at,)
                share = piece // len(at)
                for n, to in enumerate(at):
                    base = k * piece + n * share
                    store_split(w, to, parts[j][base : base + share, :])
    if step:
        for i, parts in enumerate(vectors):
            for k in range(chips):
                owner, _ = place(scalars, chips, i, 0, chips - k)
                for s in range(3):
                    flat[pl.ds(pl.multiple_of((owner * 3 + s) * step, step), step), :] = parts[
                        k * step : (k + 1) * step, s * 128 : (s + 1) * 128
                    ]
        rows = jnp.transpose(flat[...])[:16, :]
        vec[...] = rows
        bias[...] = jnp.concatenate([rows[8 + s : 9 + s, :] for s in range(4)], axis=1)


def unpack(scalars, chips, mine, other, rows_of, *vectors):
    total = 8 * mine[0].shape[0]
    outs = [((total, 3 * D), bf16)]
    if vectors:
        outs += [((16, D), f32), ((1, FF), f32)]
    return call(
        functools.partial(
            unpack_kernel,
            rows_of,
            chips,
            mine[0].shape[0] // chips,
            vectors[0].shape[0] // chips if vectors else 0,
        ),
        outs,
        [((D, 128), f32)] if vectors else [],
        flops=10**8,
        data=1 << 18,
    )(scalars, *mine, *other, *vectors)


def own_gradients_kernel(scalars, *refs):
    parts, (mom, grads, new_mom, own, *gram) = refs[:4], refs[4:]
    piece = own.shape[0] // 4
    for j in range(4):
        quarter = lax.bitwise_xor(scalars[3], j)
        grads[pl.ds(pl.multiple_of(quarter * piece, piece), piece), :] = parts[j][:piece, :]
        for n in (1, 2):
            grads[pl.ds(pl.multiple_of((4 * n + quarter) * piece, piece), piece), :] = parts[j][
                n * piece : (n + 1) * piece, :
            ]
    new_mom[...] = muon_momentum * mom[...] + grads[...]
    replica = scalars[3]
    start = jnp.where(replica == 0, 4, jnp.where(replica == 1, 0, jnp.where(replica == 2, 8, 3)))
    count = jnp.where(replica == 1, 3, jnp.where(replica == 3, 1, 4)) * piece
    row = lax.broadcasted_iota(jnp.int32, (4 * piece, 1), 0)
    block = jnp.where(
        row < count, new_mom[pl.ds(pl.multiple_of(start * piece, piece), 4 * piece), :], 0.0
    )
    own[...] = block
    keep, send, total = gram
    gram = fdot(block, block, TN, precise)
    for n, (row, column) in enumerate(UPPER):
        total[n * 128 : (n + 1) * 128, :] = gram[
            row * 128 : (row + 1) * 128, column * 128 : (column + 1) * 128
        ]
    chips, share, _ = keep.shape
    for i, out in enumerate((keep, send)):
        for k in range(chips):
            at = lax.bitwise_xor(scalars[5], i) * chips + lax.rem(scalars[4] + k, chips)
            out[k] = total[pl.ds(pl.multiple_of(at * share, share), share), :]


def own_gradients(scalars, parts, mom, chips):
    rows = mom.shape[0]
    share = 128 * len(UPPER) // (2 * chips)
    return call(
        own_gradients_kernel,
        [((rows, D), f32)] * 2 + [((rows // 3, D), f32)] + [((chips, share, 128), f32)] * 2,
        [((128 * len(UPPER), 128), f32)],
        flops=10**8,
        data=1 << 18,
    )(scalars, *parts, mom)


def pieces(x):
    hi, mid = halves(x)
    return hi, mid, (x - hi.astype(f32) - mid.astype(f32)).astype(bf16)


def full_product(a, b):
    (ah, am, al), (bh, bm, bl) = a, b
    return mm(
        jnp.concatenate([ah, ah, am, ah, al, am], axis=1),
        jnp.concatenate([bh, bm, bh, bl, bh, bm], axis=0),
        NN,
    )


def three_product(a, b):
    (ah, am, _), (bh, bm, _) = a, b
    return mm(
        jnp.concatenate([ah, am, ah], axis=1), jnp.concatenate([bh, bh, bm], axis=0), NN
    )


def identity():
    row = lax.broadcasted_iota(jnp.int32, (D, D), 0)
    return jnp.where(row == lax.broadcasted_iota(jnp.int32, (D, D), 1), 1.0, 0.0)


def polynomial(gram, product):
    g = pieces(gram)
    return g, ns_coeffs[1] * gram + ns_coeffs[2] * product(g, g) + ns_coeffs[0] * identity()


def polar_step(gram, block):
    g, poly = polynomial(gram, full_product)
    p = pieces(poly)
    return full_product(p, pieces(full_product(p, g))), three_product(pieces(block), p)


def polar_end(gram, block):
    return three_product(pieces(block), pieces(polynomial(gram, three_product)[1]))


def polar_start(gram, block):
    scale = 1.0 / (jnp.sqrt(jnp.sum(gram * identity())) + ns_eps)
    return gram * (scale * scale), block * scale


def polar(gram, block):
    state = polar_start(gram, block)
    for _ in range(NS_STEPS - 1):
        state = polar_step(*state)
    return polar_end(*state)


def update_kernel(scalars, mine, other, own, out, total, gram, block):
    chips, share, _ = mine.shape
    for i, parts in enumerate((mine, other)):
        for k in range(chips):
            at = lax.bitwise_xor(scalars[5], i) * chips + lax.rem(scalars[4] + chips - k, chips)
            total[pl.ds(pl.multiple_of(at * share, share), share), :] = parts[k]
    blocks = {}
    for n, (row, column) in enumerate(UPPER):
        blocks[row, column] = total[n * 128 : (n + 1) * 128, :]
        if row != column:
            blocks[column, row] = jnp.transpose(blocks[row, column])
    gram[...], block[...] = polar_start(
        jnp.concatenate(
            [jnp.concatenate([blocks[row, column] for column in range(3)], axis=1) for row in range(3)],
            axis=0,
        ),
        own[...],
    )

    def step(_, carry):
        gram[...], block[...] = polar_step(gram[...], block[...])
        return carry

    lax.fori_loop(0, NS_STEPS - 1, step, 0)
    replica = scalars[3]
    rate = jnp.where(replica == 1, 3.0**0.5, jnp.where(replica == 0, (FF / D) ** 0.5, 1.0))
    out[...] = polar_end(gram[...], block[...]) * (-muon_rate * rate)


def update(scalars, mine, other, own):
    return call(
        update_kernel,
        [(own.shape, f32)],
        [((128 * len(UPPER), 128), f32), ((D, D), f32), (own.shape, f32)],
        flops=10**8, data=1 << 18
    )(scalars, mine, other, own)[0]


def local(
    tokens,
    image_count,
    w_qkv,
    w_out,
    w_up,
    w_down,
    vectors,
    cotangent,
    mom_qkv,
    mom_out,
    mom_up,
    mom_down,
    mom_vectors,
):
    group_size = lax.axis_size("group")
    replicas = lax.axis_size("replica")
    group_index = lax.axis_index("group")
    replica_index = lax.axis_index("replica")
    chips = group_size // 2
    tok_rows = tokens.shape[0]
    slab_rows = group_size * tok_rows
    image_total = lax.dynamic_index_in_dim(image_count, replica_index, 0, keepdims=False)
    first_slot = group_index * tok_rows
    first_image = first_slot // L
    scalars = jnp.stack(
        [
            first_slot - first_image * L,
            slab_rows - first_image * L,
            image_total * L - first_slot,
            replica_index,
            group_index // 2,
            group_index % 2,
        ]
    ).astype(jnp.int32)

    def swap(x):
        return lax.ppermute(x, "group", [(i, i ^ 1) for i in range(group_size)])

    def rotate(x, by):
        return lax.ppermute(
            x, "group", [(i, (i + 2 * by) % group_size) for i in range(group_size)]
        )

    def cross(x, by):
        return lax.ppermute(x, "replica", [(i, i ^ by) for i in range(replicas)])

    def halo(x):
        ends = group_size - 1
        lower = lax.ppermute(x[tok_rows - HALO :], "group", [(i, i + 1) for i in range(ends)])
        upper = lax.ppermute(x[:HALO], "group", [(i + 1, i) for i in range(ends)])
        return lower, x, upper

    def along_chips(x):
        return jnp.stack([x] + [rotate(x, k) for k in range(1, chips)])

    width = D // group_size
    piece = 4 * width // replicas
    cuts = (3 * width, width, 4 * width, 4 * width)
    first_stack = jnp.concatenate([w_qkv.T, w_out.T], axis=0)
    second_stack = jnp.concatenate([w_up.T, w_down], axis=0)
    mom_stack = jnp.concatenate([mom_qkv.T, mom_out.T, mom_up.T, mom_down], axis=0)
    around = halo(tokens)

    def split(stack):
        one, two, three, four = (stack[sum(cuts[:i]) : sum(cuts[: i + 1])] for i in range(4))
        return one.T, two.T, three.T, four

    def finish(block_out, grad_tokens, grads, new_mom, dvec, updates):
        grad_vectors = lax.dynamic_slice_in_dim(dvec[:12], group_index * width, width, 1)
        new_vectors = vector_momentum * mom_vectors + grad_vectors
        return (
            block_out,
            grad_tokens,
            *split(grads),
            grad_vectors,
            *split(new_mom),
            new_vectors,
            *updates,
            -vector_rate * new_vectors,
        )

    if replicas != 4 or piece % 16:
        def rows_of(stack, inner):
            parts = lax.all_gather(stack, "group")
            rows = jnp.concatenate(
                [parts[:, :inner].reshape(-1, D), parts[:, inner:].reshape(-1, D)], axis=0
            )
            hi, lo = halves(rows)
            return jnp.concatenate([hi, lo, hi], axis=1)

        def shares_of(total, cut, inner):
            one, two = total[:cut], total[cut:]
            parts = jnp.concatenate(
                [one.reshape(group_size, inner, D), two.reshape(group_size, -1, D)], axis=1
            )
            return lax.psum_scatter(parts, "group", scatter_dimension=0)

        w_one, w_two = rows_of(first_stack, 3 * width), rows_of(second_stack, 4 * width)
        vec = jnp.pad(lax.all_gather(vectors, "group", axis=1, tiled=True), ((0, 4), (0, 0)))
        *saved, a3, middle = attend(scalars, *around, w_one, vec)
        block_out, slope, n3, m3, down = mlp(
            scalars, None, middle, cotangent, w_two, vec, vec[8:12].reshape(1, FF)
        )
        d_middle, d_hi, d_lo, dvec = mlp_back(scalars, middle, cotangent, w_two, vec, slope, m3)
        second = jnp.concatenate([up_grads(scalars, None, d_hi, d_lo, n3)[0], down], axis=0)
        d_around = halo(d_middle)
        some, more = (attend_back(scalars, i, 2, d_around, w_one, *saved) for i in (0, 2))
        first, d_hi, d_lo, sums = attend_grads(
            scalars, None, some, more, tokens, d_middle, vec, a3
        )
        grad_tokens, dvec = token_grads(
            scalars, d_hi, d_lo, w_one, tokens, d_middle, vec, sums, dvec
        )
        grads, dvec = lax.psum(
            (
                jnp.concatenate(
                    [shares_of(first, 3 * D, 3 * width), shares_of(second, FF, 4 * width)], axis=0
                ),
                lax.psum(dvec, "group"),
            ),
            "replica",
        )
        new_mom = muon_momentum * mom_stack + grads
        blocks = [new_mom[sum(cuts[:i]) : sum(cuts[: i + 1])] for i in range(4)]
        grams = lax.psum(jnp.stack([fdot(x, x, TN, precise) for x in blocks]), "group")
        updates = [
            polar(grams[i], x) * (-muon_rate * rate)
            for i, (x, rate) in enumerate(zip(blocks, (3.0**0.5, 1.0, (FF / D) ** 0.5, 1.0)))
        ]
        updates = [x if i == 3 else x.T for i, x in enumerate(updates)]
        return finish(block_out, grad_tokens, grads, new_mom, dvec, updates)

    vec_block = jnp.pad(vectors.T, ((0, 0), (0, 116)))
    third = width // 3
    vec_block = jnp.concatenate([vec_block[s * third : (s + 1) * third] for s in range(3)], axis=1)
    my_first = lax.dynamic_slice_in_dim(first_stack, replica_index * piece, piece, 0)
    my_second = jnp.concatenate(
        [
            lax.dynamic_slice_in_dim(second_stack, (4 * n + replica_index) * piece, piece, 0)
            for n in range(2)
        ],
        axis=0,
    )

    others = range(1, replicas)
    start = jnp.concatenate([my_first, vec_block], axis=0)
    start = [start] + [rotate(start, k) for k in range(1, chips)]
    first = jnp.concatenate([x[:piece] for x in start], axis=0)
    vec_parts = jnp.concatenate([x[piece:] for x in start], axis=0)
    first, vec_parts, my_second, lower, upper, scalars = lax.optimization_barrier(
        (first, vec_parts, my_second, around[0], around[2], scalars)
    )
    around = lower, tokens, upper
    first_other, vec_other = [swap(first)], swap(vec_parts)
    first = [first] + [cross(first, j) for j in others]
    second = [my_second] + [rotate(my_second, k) for k in range(1, chips)]
    first[1:], second = lax.optimization_barrier((first[1:], second))
    second = jnp.concatenate(second, axis=0)
    second = [second] + [cross(second, j) for j in others]
    second_other = [swap(second[0])]
    first_other += [swap(first[j]) for j in others]
    w_one, vec, bias = unpack(
        scalars, chips, first, first_other, first_rows, vec_parts, vec_other
    )
    *saved, a3, middle = attend(scalars, *around, w_one, vec)
    for j in others:
        second[j], middle = lax.optimization_barrier((second[j], middle))
        second_other.append(swap(second[j]))
    w_two = unpack(scalars, chips, second, second_other, second_rows)[0]
    shape = (chips, piece, D)

    def join(keep, other):
        return [x + other[j] for j, x in enumerate(keep)]

    def exchange(parts):
        return [parts[0]] + [cross(parts[j], j) for j in others]

    block_out, slope, n3, m3, *keep, send = mlp(
        scalars, shape, middle, cotangent, w_two, vec, bias
    )
    other = swap(send)
    d_middle, d_hi, d_lo, dvec = mlp_back(scalars, middle, cotangent, w_two, vec, slope, m3)
    down, d_middle, d_hi = lax.optimization_barrier((join(keep, other), d_middle, d_hi))
    down = exchange(down)
    d_around = halo(d_middle)
    *keep, send = up_grads(scalars, shape, d_hi, d_lo, n3)
    keep, send, d_around = lax.optimization_barrier((keep, send, d_around))
    other = swap(send)
    some = attend_back(scalars, 0, 2, d_around, w_one, *saved)
    up, some, d_around = lax.optimization_barrier((join(keep, other), some, d_around))
    up = exchange(up)
    more = attend_back(scalars, 2, 2, d_around, w_one, *saved)
    *keep, send, d_hi, d_lo, sums = attend_grads(
        scalars, shape, some, more, tokens, d_middle, vec, a3
    )
    grad_tokens, dvec = token_grads(scalars, d_hi, d_lo, w_one, tokens, d_middle, vec, sums, dvec)
    keep, send, dvec, up, down = lax.optimization_barrier((keep, send, dvec, up, down))
    first = exchange(join(keep, swap(send)))
    dvec = dvec + swap(dvec)

    def over_chips(parts, *extra):
        parts = [
            jnp.concatenate([sum((x[k] for x in parts[1:]), parts[0][k]), *extra], axis=0)
            for k in range(chips)
        ]
        return sum((rotate(parts[k], k) for k in range(1, chips)), parts[0])

    down_sum, up_sum = over_chips(down), over_chips(up)
    first_sum = over_chips(first, dvec)
    sums = jnp.concatenate([first_sum[:piece], up_sum, down_sum, first_sum[piece:]], axis=0)
    parts = [sums] + [cross(sums, j) for j in others]
    dvec = sum((x[3 * piece :] for x in parts[1:]), parts[0][3 * piece :])
    grads, new_mom, own, keep, send = own_gradients(scalars, parts, mom_stack, chips)
    t = keep + swap(send)
    t = t[0] + sum(rotate(t[k], k) for k in range(1, chips))
    gram = along_chips(t)
    update_own = update(scalars, gram, swap(gram), own)
    updates = [update_own] + [cross(update_own, j) for j in others]

    def from_replica(owner, rows):
        at = lax.bitwise_xor(replica_index, owner)
        return lax.select_n(at, *(x[:rows] for x in updates))

    return finish(
        block_out,
        grad_tokens,
        grads,
        new_mom,
        dvec,
        (
            from_replica(1, 3 * width).T,
            from_replica(3, width).T,
            from_replica(0, 4 * width).T,
            from_replica(2, 4 * width),
        ),
    )


def solution(mesh):
    tokens, whole, columns, rows = P(("replica", "group"), None), P(), P(None, "group"), P("group", None)
    params = (columns, columns, columns, rows, columns)
    return jax.shard_map(
        local,
        mesh=mesh,
        in_specs=(tokens, whole, *params, tokens, *params),
        out_specs=(tokens, tokens, *params, *params, *params),
        check_vma=False,
    )
```

```python
import functools

import jax
import jax.numpy as jnp
from jax import lax
from jax.experimental import pallas as pl
from jax.experimental.pallas import tpu as pltpu
from jax.sharding import PartitionSpec as P

D = 384
HEADS = 6
HEAD_DIM = 64
FF = 1536
L = 197
NS_STEPS = 5
SLOTS = 4
SLOT = 208
HALO = 200
TILE = 512

f32, bf16 = jnp.float32, jnp.bfloat16
high = lax.Precision.HIGH
precise = lax.Precision.HIGHEST
ns_coeffs = (3.4445, -4.775, 2.0315)
norm_eps = 1e-06
ns_eps = 1e-07
muon_momentum = 0.95
vector_momentum = 0.9
muon_rate = 0.5
vector_rate = 0.001
mask_fill = -1e30

UPPER = ((0, 0), (0, 1), (0, 2), (1, 1), (1, 2), (2, 2))
NN = (((1,), (0,)), ((), ()))
NT = (((1,), (1,)), ((), ()))
TN = (((0,), (0,)), ((), ()))
VMEM = pl.BlockSpec(memory_space=pltpu.VMEM)
SMEM = pl.BlockSpec(memory_space=pltpu.SMEM)


def call(body, outs, scratch=(), flops=0, data=0):
    def run(scalars, *arrays):
        return pl.pallas_call(
            body,
            out_shape=[jax.ShapeDtypeStruct(s, t) for s, t in outs],
            in_specs=[SMEM] + [VMEM] * len(arrays),
            out_specs=[VMEM] * len(outs),
            scratch_shapes=[pltpu.VMEM(s, t) for s, t in scratch],
            compiler_params=pltpu.CompilerParams(vmem_limit_bytes=28 << 20),
            cost_estimate=pl.CostEstimate(flops=flops, bytes_accessed=data, transcendentals=0),
        )(scalars, *arrays)

    return run


def mm(a, b, dims):
    return lax.dot_general(a, b, dims, preferred_element_type=f32)


def fdot(a, b, dims, precision=high):
    return lax.dot_general(a, b, dims, precision=precision, preferred_element_type=f32)


def halves(x):
    hi = x.astype(bf16)
    return hi, (x - hi.astype(f32)).astype(bf16)


def triple(x):
    hi, lo = halves(x)
    return jnp.concatenate([hi, hi, lo], axis=1)


def by_rows(hi, lo, both):
    wide = mm(hi, both[:, : 2 * D], NN)
    return wide[:, :D] + wide[:, D:] + mm(lo, both[:, :D], NN)


def by_tokens(hi, lo, other):
    wide = mm(hi, other[:, D:], TN)
    return wide[:, :D] + wide[:, D:] + mm(lo, other[:, :D], TN)


def standardized(x):
    centered = x - jnp.mean(x, axis=-1, keepdims=True)
    rstd = lax.rsqrt(jnp.mean(centered * centered, axis=-1, keepdims=True) + norm_eps)
    return centered * rstd, rstd


def norm_back(d_norm, xhat, rstd, scale):
    g = d_norm * (1.0 + scale)
    return rstd * (
        g - jnp.mean(g, axis=-1, keepdims=True) - xhat * jnp.mean(g * xhat, axis=-1, keepdims=True)
    )


def row_sum(x):
    return jnp.sum(x, axis=0, keepdims=True)


def window_start(scalars, slot):
    start = HALO - scalars[0] + L * slot
    aligned = pl.multiple_of((start // 8) * 8, 8)
    return aligned, start - aligned


def fill_window(window, lower, own, upper):
    rows = own.shape[0]
    window[:HALO, :] = lower[...]
    window[HALO : HALO + rows, :] = own[...]
    window[HALO + rows : 2 * HALO + rows, :] = upper[...]
    window[2 * HALO + rows :, :] = jnp.zeros((window.shape[0] - 2 * HALO - rows, D), f32)


def load_slot(window, scalars, slot):
    aligned, shift = window_start(scalars, slot)
    block = window[pl.ds(aligned, SLOT + 8), :]
    return pltpu.roll(block, lax.rem(SLOT + 8 - shift, SLOT + 8), 0)[:SLOT]


def store_slot(window, scalars, slot, value):
    aligned, shift = window_start(scalars, slot)
    block = jnp.concatenate([value, jnp.zeros((8, value.shape[1]), f32)], axis=0)
    block = pltpu.roll(block, shift, 0)
    rows = lax.broadcasted_iota(jnp.int32, (SLOT + 8, 1), 0)
    window[pl.ds(aligned, SLOT + 8), :] = jnp.where(
        rows >= shift, block, window[pl.ds(aligned, SLOT + 8), :]
    )


def window_rows(rows):
    return 2 * HALO + rows + 96


def pairs(x):
    hi, lo = halves(x)
    return [
        jnp.concatenate([hi[:, at : at + HEAD_DIM], lo[:, at : at + HEAD_DIM]], axis=1)
        for at in range(0, D, HEAD_DIM)
    ]


def twice(x):
    return jnp.concatenate([x, x], axis=1)


def spread(x):
    hi, lo = x[:, :HEAD_DIM], x[:, HEAD_DIM:]
    return jnp.concatenate([hi, hi, lo, lo], axis=1)


def times(hi, lo, other):
    wide = mm(hi, other, NN)
    return wide[:, :HEAD_DIM] + wide[:, HEAD_DIM:] + mm(lo, other[:, :HEAD_DIM], NN)


def times_down(other, hi, lo):
    tall = mm(other, hi, NN)
    return tall[:HEAD_DIM] + tall[HEAD_DIM:] + mm(other[:HEAD_DIM], lo, NN)


def attend_kernel(
    scalars, lower, own, upper, w, vec, q2, kt2, v2, probs_hi, probs_lo, a3, middle, window, proj, att_win
):
    rows = own.shape[0]
    fill_window(window, lower, own, upper)
    step = (2 * HALO + rows) // 3

    def project_step(t, carry):
        at = pl.multiple_of(t * step, 16)
        xhat, _ = standardized(window[pl.ds(at, step), :])
        left = triple(xhat * (1.0 + vec[0:1, :]) + vec[1:2, :])
        for part, bias in ((0, vec[2:3, :]), (1, None), (2, vec[3:4, :])):
            value = mm(left, w[part * D : (part + 1) * D, :], NT)
            proj[pl.ds(at, step), part * D : (part + 1) * D] = value if bias is None else value + bias
        return carry

    lax.fori_loop(0, 3, project_step, 0)
    proj[2 * HALO + rows :, :] = jnp.zeros((96, 3 * D), f32)

    def slot_step(slot, carry):
        qkv = load_slot(proj, scalars, slot)
        keys = jnp.minimum(L, scalars[1] - L * slot)
        keep = lax.broadcasted_iota(jnp.int32, (SLOT, SLOT), 0) < keys
        q, k, v = (pairs(qkv[:, part * D : (part + 1) * D]) for part in range(3))
        heads = []
        for h in range(HEADS):
            q2[slot, h] = q[h]
            v2[slot, h] = v[h]
            kt2[slot, h] = jnp.transpose(k[h])
            scores = mm(twice(k[h]), spread(q[h]), NT) * HEAD_DIM**-0.5
            scores = jnp.where(keep, scores, mask_fill)
            weights = jnp.exp(scores - jnp.max(scores, axis=0, keepdims=True))
            weights = weights * (1.0 / jnp.sum(weights, axis=0, keepdims=True))
            hi, lo = halves(weights)
            probs_hi[slot, h] = hi
            probs_lo[slot, h] = lo
            heads.append(times_down(jnp.transpose(v[h]), hi, lo))
        store_slot(att_win, scalars, slot, jnp.transpose(jnp.concatenate(heads, axis=0)))
        return carry

    lax.fori_loop(0, SLOTS, slot_step, 0)
    att = triple(att_win[HALO : HALO + rows, :])
    a3[...] = att
    middle[...] = own[...] + mm(att, w[3 * D :, :], NT) + vec[4:5, :]


def attend(scalars, lower, own, upper, w, vec):
    rows = own.shape[0]
    return call(
        attend_kernel,
        [
            ((SLOTS, HEADS, SLOT, 128), bf16),
            ((SLOTS, HEADS, 128, SLOT), bf16),
            ((SLOTS, HEADS, SLOT, 128), bf16),
            ((SLOTS, HEADS, SLOT, SLOT), bf16),
            ((SLOTS, HEADS, SLOT, SLOT), bf16),
            ((rows, 3 * D), bf16),
            ((rows, D), f32),
        ],
        [
            ((window_rows(rows), D), f32),
            ((window_rows(rows), 3 * D), f32),
            ((window_rows(rows), D), f32),
        ],
        flops=10**8,
        data=1 << 18,
    )(scalars, lower, own, upper, w, vec)


def mlp_kernel(scalars, mid, cot, w, vec, bias, out, slope, n3, m3, *rest):
    parts, (total, h_hi, h_lo) = rest[:-3], rest[-3:]
    if len(parts) == 1:
        total = parts[0]
    rows = mid.shape[0]
    xhat, _ = standardized(mid[...])
    n3[...] = triple(xhat * (1.0 + vec[5:6, :]) + vec[6:7, :])
    live = lax.broadcasted_iota(jnp.int32, (rows, 1), 0) < scalars[2]
    m3[...] = triple(jnp.where(live, cot[...], 0.0))

    def tile_step(t, carry):
        at = pl.multiple_of(t * TILE, TILE)
        pre = mm(n3[...], w[pl.ds(at, TILE), :], NT) + bias[0:1, pl.ds(at, TILE)]
        cdf = 0.5 + 0.5 * lax.erf(pre * (0.5**0.5))
        slope[:, pl.ds(at, TILE)] = cdf + pre * (jnp.exp(-0.5 * pre * pre) * 0.3989422804014327)
        hi, lo = halves(pre * cdf)
        h_hi[:, pl.ds(at, TILE)] = hi
        h_lo[:, pl.ds(at, TILE)] = lo
        total[pl.ds(at, TILE), :] = by_tokens(hi, lo, m3)
        return carry

    lax.fori_loop(0, FF // TILE, tile_step, 0)
    out[...] = mid[...] + by_rows(h_hi[...], h_lo[...], w[FF:, :]) + vec[7:8, :]
    scatter_parts(scalars, total, parts, quarter_rows)


def mlp(scalars, parts, mid, cot, w, vec, bias):
    rows = mid.shape[0]
    outs, scratch = part_outs(parts, FF)
    return call(
        mlp_kernel,
        [((rows, D), f32), ((rows, FF), f32)] + [((rows, 3 * D), bf16)] * 2 + outs,
        [scratch] + [((rows, FF), bf16)] * 2,
        flops=10**8,
        data=1 << 18,
    )(scalars, mid, cot, w, vec, bias)


def mlp_back_kernel(scalars, mid, cot, w, vec, slope, n3, m3, dmid, dvec, *rest):
    parts, (total, d_hi, d_lo, dbias) = rest[:-4], rest[-4:]
    if len(parts) == 1:
        total = parts[0]
    rows = mid.shape[0]

    def tile_step(t, carry):
        at = pl.multiple_of(t * TILE, TILE)
        d_pre = mm(m3[...], w[pl.ds(FF + at, TILE), :], NT) * slope[:, pl.ds(at, TILE)]
        dbias[0:1, pl.ds(at, TILE)] = row_sum(d_pre)
        hi, lo = halves(d_pre)
        d_hi[:, pl.ds(at, TILE)] = hi
        d_lo[:, pl.ds(at, TILE)] = lo
        total[pl.ds(at, TILE), :] = by_tokens(hi, lo, n3)
        return carry

    lax.fori_loop(0, FF // TILE, tile_step, 0)
    scatter_parts(scalars, total, parts, quarter_rows)
    d_norm = by_rows(d_hi[...], d_lo[...], w[:FF, :])
    xhat, rstd = standardized(mid[...])
    live = lax.broadcasted_iota(jnp.int32, (rows, 1), 0) < scalars[2]
    masked = jnp.where(live, cot[...], 0.0)
    d_middle = masked + norm_back(d_norm, xhat, rstd, vec[5:6, :])
    dmid[...] = d_middle
    zero = jnp.zeros((4, D), f32)
    dvec[...] = jnp.concatenate(
        [zero, row_sum(d_middle), row_sum(d_norm * xhat), row_sum(d_norm), row_sum(masked)]
        + [dbias[0:1, i * D : (i + 1) * D] for i in range(4)]
        + [zero],
        axis=0,
    )


def mlp_back(scalars, parts, mid, cot, w, vec, slope, n3, m3):
    rows = mid.shape[0]
    outs, scratch = part_outs(parts, FF)
    return call(
        mlp_back_kernel,
        [((rows, D), f32), ((16, D), f32)] + outs,
        [scratch] + [((rows, FF), bf16)] * 2 + [((8, FF), f32)],
        flops=10**8,
        data=1 << 18,
    )(scalars, mid, cot, w, vec, slope, n3, m3)


def place(scalars, i, j, k):
    owner = 2 * lax.bitwise_xor(scalars[4], k) + lax.bitwise_xor(scalars[5], i)
    return owner, lax.bitwise_xor(scalars[3], j)


def first_rows(owner, quarter, piece):
    return pl.multiple_of(
        jnp.where(quarter < 3, owner * 3 * piece + quarter * piece, 3 * D + owner * piece), piece
    )


def second_rows(owner, quarter, piece):
    half = piece // 2
    at = owner * 4 * half + quarter * half
    return pl.multiple_of(at, half), pl.multiple_of(FF + at, half)


def quarter_rows(owner, quarter, piece):
    return pl.multiple_of(owner * 4 * piece + quarter * piece, piece)


def part_outs(parts, rows):
    if parts is None:
        return [((rows, D), f32)], ((8, D), f32)
    return [(parts, f32)] * 4 + [((4, *parts), f32)], ((rows, D), f32)


def scatter_parts(scalars, total, outs, rows_of):
    if len(outs) == 1:
        return
    chips, piece, _ = outs[0].shape
    for n in range(8):
        for k in range(chips):
            owner, quarter = place(scalars, n // 4, n % 4, k)
            rows = total[pl.ds(rows_of(owner, quarter, piece), piece), :]
            if n < 4:
                outs[n][k] = rows
            else:
                outs[4][n - 4, k] = rows


def attend_back_kernel(first_slot, scalars, lower, own, upper, w, q2, kt2, v2, probs_hi, probs_lo, out, window):
    rows = own.shape[0]
    fill_window(window, lower, own, upper)

    def slot_step(step, carry):
        slot = first_slot + step
        row = lax.broadcasted_iota(jnp.int32, (SLOT, 1), 0)
        at_own = row + L * slot - scalars[0]
        mine = (at_own >= 0) & (at_own < rows) & (row < L)
        d_mid = jnp.where(row < L, load_slot(window, scalars, slot), 0.0)
        d_out = pairs(by_rows(*halves(d_mid), w[3 * D :, :]))
        d_q, d_k, d_v = [], [], []
        for h in range(HEADS):
            hi, lo = probs_hi[slot, h], probs_lo[slot, h]
            weights = hi.astype(f32) + lo.astype(f32)
            d_weights = mm(twice(v2[slot, h]), spread(d_out[h]), NT)
            mean = jnp.sum(weights * d_weights, axis=0, keepdims=True)
            s_hi, s_lo = halves(weights * (d_weights - mean) * HEAD_DIM**-0.5)
            d_v.append(times(hi, lo, d_out[h]))
            d_k.append(times(s_hi, s_lo, q2[slot, h]))
            d_q.append(times_down(kt2[slot, h], s_hi, s_lo))
        d_q = jnp.transpose(jnp.concatenate(d_q, axis=0))
        d_proj = jnp.concatenate([d_q] + d_k + d_v, axis=1)
        out[step] = jnp.where(mine, d_proj, 0.0)
        return carry

    lax.fori_loop(0, out.shape[0], slot_step, 0)


def attend_back(scalars, first_slot, slots, around, w, *saved):
    rows = around[1].shape[0]
    return call(
        functools.partial(attend_back_kernel, first_slot),
        [((slots, SLOT, 3 * D), f32)],
        [((window_rows(rows), D), f32)],
        flops=10**8,
        data=1 << 18,
    )(scalars, *around, w, *saved)[0]


def attend_grads_kernel(scalars, some, more, tokens, d_mid, vec, a3, *rest):
    outs, (d_hi, d_lo, sums), (total, window) = rest[:-5], rest[-5:-2], rest[-2:]
    if len(outs) == 1:
        total = outs[0]
    rows = tokens.shape[0]
    for i, part in enumerate((some, more)):

        def slot_step(step, carry, i=i, part=part):
            store_slot(window, scalars, i * part.shape[0] + step, part[step])
            return carry

        lax.fori_loop(0, part.shape[0], slot_step, 0)
    xhat, _ = standardized(tokens[...])
    n3 = triple(xhat * (1.0 + vec[0:1, :]) + vec[1:2, :])

    def part_step(part, carry):
        at = pl.ds(pl.multiple_of(part * D, D), D)
        d_proj = window[HALO : HALO + rows, at]
        hi, lo = halves(d_proj)
        d_hi[:, at] = hi
        d_lo[:, at] = lo
        total[at, :] = by_tokens(hi, lo, n3)
        sums[part] = jnp.broadcast_to(row_sum(d_proj), (8, D))
        return carry

    lax.fori_loop(0, 3, part_step, 0)
    total[3 * D :, :] = by_tokens(*halves(d_mid[...]), a3)
    scatter_parts(scalars, total, outs, first_rows)


def attend_grads(scalars, parts, some, more, tokens, d_mid, vec, a3):
    rows = tokens.shape[0]
    outs, scratch = part_outs(parts, 4 * D)
    return call(
        attend_grads_kernel,
        outs + [((rows, 3 * D), bf16)] * 2 + [((3, 8, D), f32)],
        [scratch, ((window_rows(rows), 3 * D), f32)],
        flops=10**8,
        data=1 << 18,
    )(scalars, some, more, tokens, d_mid, vec, a3)


def token_grads_kernel(scalars, d_hi, d_lo, w, tokens, d_mid, vec, sums, dvec_in, dtok, dvec):
    xhat, rstd = standardized(tokens[...])
    d_norm = by_rows(d_hi[...], d_lo[...], w[: 3 * D, :])
    dtok[...] = d_mid[...] + norm_back(d_norm, xhat, rstd, vec[0:1, :])
    new = [row_sum(d_norm * xhat), row_sum(d_norm), sums[0, 0:1], sums[2, 0:1], jnp.zeros((12, D), f32)]
    dvec[...] = dvec_in[...] + jnp.concatenate(new, axis=0)


def token_grads(scalars, *arrays):
    rows = arrays[0].shape[0]
    return call(
        token_grads_kernel, [((rows, D), f32), ((16, D), f32)], flops=10**8, data=1 << 18
    )(scalars, *arrays)


def store_split(w, at, x):
    hi, lo = halves(x)
    w[pl.ds(at, x.shape[0]), :] = jnp.concatenate([hi, lo, hi], axis=1)


def unpack_kernel(rows_of, chips, piece, step, scalars, *refs):
    mine, other, rest = refs[:4], refs[4:8], refs[8:]
    if step:
        vectors, (w, vec, bias) = rest[:2], rest[2:]
    else:
        (w,) = rest
    for i, parts in enumerate((mine, other)):
        for j in range(4):
            for k in range(chips):
                owner, quarter = place(scalars, i, j, k)
                at = rows_of(owner, quarter, piece)
                at = at if isinstance(at, tuple) else (at,)
                share = piece // len(at)
                for n, to in enumerate(at):
                    base = k * piece + n * share
                    store_split(w, to, parts[j][base : base + share, :])
    if step:
        width = D // (2 * chips)
        lane = lax.broadcasted_iota(jnp.int32, (step, D), 1)
        sums = [jnp.zeros((step, D), f32), jnp.zeros((step, D), f32)]
        for i, parts in enumerate(vectors):
            for k in range(chips):
                owner, _ = place(scalars, i, 0, k)
                block = parts[k * step : (k + 1) * step, :]
                for n in range(2):
                    mine_only = jnp.where((lane >= n * width) & (lane < (n + 1) * width), block, 0.0)
                    shift = lax.rem((owner - n) * width + D, D)
                    sums[n] = sums[n] + pltpu.roll(mine_only, shift, 1)
        vec[:step, :] = sums[0]
        vec[step:, :] = sums[1]
        bias[...] = jnp.concatenate([sums[1][s : s + 1, :] for s in range(4)], axis=1)


def unpack(scalars, chips, mine, other, rows_of, *vectors):
    total = 8 * mine[0].shape[0]
    outs = [((total, 3 * D), bf16)]
    if vectors:
        outs += [((16, D), f32), ((1, FF), f32)]
    return call(
        functools.partial(
            unpack_kernel,
            rows_of,
            chips,
            mine[0].shape[0] // chips,
            vectors[0].shape[0] // chips if vectors else 0,
        ),
        outs,
        [],
        flops=10**8,
        data=1 << 18,
    )(scalars, *mine, *other, *vectors)


def own_gradients_kernel(scalars, mine, *refs):
    others, (mom, own, keep, send, total) = refs[:3], refs[3:]
    piece = mine.shape[0] // 3
    replica = scalars[3]
    start = jnp.where(replica == 0, 4, jnp.where(replica == 2, 8, 0)) * piece
    at = pl.multiple_of(jnp.where(replica == 0, 1, jnp.where(replica == 2, 2, 0)) * piece, piece)
    own[...] = muon_momentum * mom[pl.ds(pl.multiple_of(start, piece), 4 * piece), :]
    for j, part in enumerate((mine, *others)):
        quarter = lax.bitwise_xor(replica, j)
        rows = pl.ds(pl.multiple_of(quarter * piece, piece), piece)
        own[rows, :] = own[rows, :] + (part[pl.ds(at, piece), :] if j == 0 else part[...])
    row = lax.broadcasted_iota(jnp.int32, (4 * piece, 1), 0)
    drop = ((replica == 1) & (row >= 3 * piece)) | ((replica == 3) & (row < 3 * piece))
    block = jnp.where(drop, 0.0, own[...])
    own[...] = block
    gram = fdot(block, block, TN, precise)
    for n, (row, column) in enumerate(UPPER):
        total[n * 128 : (n + 1) * 128, :] = gram[
            row * 128 : (row + 1) * 128, column * 128 : (column + 1) * 128
        ]
    chips, share, _ = keep.shape
    for i, out in enumerate((keep, send)):
        for k in range(chips):
            at = lax.bitwise_xor(scalars[5], i) * chips + lax.bitwise_xor(scalars[4], k)
            out[k] = total[pl.ds(pl.multiple_of(at * share, share), share), :]


def own_gradients(scalars, mine, others, mom, chips):
    share = 128 * len(UPPER) // (2 * chips)
    return call(
        own_gradients_kernel,
        [((mom.shape[0] // 3, D), f32)] + [((chips, share, 128), f32)] * 2,
        [((128 * len(UPPER), 128), f32)],
        flops=10**8,
        data=1 << 18,
    )(scalars, mine, *others, mom)


def all_gradients_kernel(scalars, *refs):
    parts, (mom, grads, new_mom) = refs[:4], refs[4:]
    piece = mom.shape[0] // 12
    for j in range(4):
        quarter = lax.bitwise_xor(scalars[3], j)
        for n in range(3):
            rows = pl.ds(pl.multiple_of((4 * n + quarter) * piece, piece), piece)
            grads[rows, :] = parts[j][n * piece : (n + 1) * piece, :]
    new_mom[...] = muon_momentum * mom[...] + grads[...]


def all_gradients(scalars, parts, mom):
    return call(all_gradients_kernel, [(mom.shape, f32)] * 2, flops=10**8, data=1 << 18)(
        scalars, *parts, mom
    )


def pieces(x):
    hi, mid = halves(x)
    return hi, mid, (x - hi.astype(f32) - mid.astype(f32)).astype(bf16)


def full_product(a, b):
    (ah, am, al), (bh, bm, bl) = a, b
    return mm(
        jnp.concatenate([ah, ah, am, ah, al, am], axis=1),
        jnp.concatenate([bh, bm, bh, bl, bh, bm], axis=0),
        NN,
    )


def three_product(a, b):
    (ah, am, _), (bh, bm, _) = a, b
    return mm(
        jnp.concatenate([ah, am, ah], axis=1), jnp.concatenate([bh, bh, bm], axis=0), NN
    )


def identity():
    row = lax.broadcasted_iota(jnp.int32, (D, D), 0)
    return jnp.where(row == lax.broadcasted_iota(jnp.int32, (D, D), 1), 1.0, 0.0)


def polynomial(gram, product):
    g = pieces(gram)
    return g, ns_coeffs[1] * gram + ns_coeffs[2] * product(g, g) + ns_coeffs[0] * identity()


def polar_step(gram, block):
    g, poly = polynomial(gram, full_product)
    p = pieces(poly)
    return full_product(p, pieces(full_product(p, g))), three_product(pieces(block), p)


def polar_end(gram, block):
    return three_product(pieces(block), pieces(polynomial(gram, three_product)[1]))


def polar_start(gram, block):
    scale = 1.0 / (jnp.sqrt(jnp.sum(gram * identity())) + ns_eps)
    return gram * (scale * scale), block * scale


def polar(gram, block):
    state = polar_start(gram, block)
    for _ in range(NS_STEPS - 1):
        state = polar_step(*state)
    return polar_end(*state)


def update_kernel(scalars, mine, other, own, out, total, gram, block):
    chips, share, _ = mine.shape
    for i, parts in enumerate((mine, other)):
        for k in range(chips):
            at = lax.bitwise_xor(scalars[5], i) * chips + lax.bitwise_xor(scalars[4], k)
            total[pl.ds(pl.multiple_of(at * share, share), share), :] = parts[k]
    blocks = {}
    for n, (row, column) in enumerate(UPPER):
        blocks[row, column] = total[n * 128 : (n + 1) * 128, :]
        if row != column:
            blocks[column, row] = jnp.transpose(blocks[row, column])
    gram[...], block[...] = polar_start(
        jnp.concatenate(
            [jnp.concatenate([blocks[row, column] for column in range(3)], axis=1) for row in range(3)],
            axis=0,
        ),
        own[...],
    )

    def step(_, carry):
        gram[...], block[...] = polar_step(gram[...], block[...])
        return carry

    lax.fori_loop(0, NS_STEPS - 1, step, 0)
    replica = scalars[3]
    rate = jnp.where(replica == 1, 3.0**0.5, jnp.where(replica == 0, (FF / D) ** 0.5, 1.0))
    out[...] = polar_end(gram[...], block[...]) * (-muon_rate * rate)


def update(scalars, mine, other, own):
    return call(
        update_kernel,
        [(own.shape, f32)],
        [((128 * len(UPPER), 128), f32), ((D, D), f32), (own.shape, f32)],
        flops=10**8, data=1 << 18
    )(scalars, mine, other, own)[0]


def first_message_kernel(replica, qkv, out, vectors, message):
    piece = message.shape[0] - 8
    width = vectors.shape[1]

    @pl.when(replica[0] < 3)
    def _():
        message[:piece, :] = qkv[pl.ds(pl.multiple_of(replica[0] * piece, 8), piece), :]

    @pl.when(replica[0] == 3)
    def _():
        message[:piece, :] = out[...]

    message[piece:, :] = jnp.zeros((8, D), f32)
    message[piece:, :width] = vectors[:8, :]
    message[piece : piece + 4, width : 2 * width] = vectors[8:, :]


def first_message(replica, qkv, out, vectors):
    return call(
        first_message_kernel, [((out.shape[0] + 8, D), f32)], flops=10**6, data=1 << 16
    )(replica, qkv, out, vectors)[0]


def hand_out_kernel(scalars, one, two, three, four, *outs):
    for owner, out in zip((1, 3, 0, 2), outs):
        at = lax.bitwise_xor(scalars[3], owner)
        rows = out.shape[0]
        for j, part in enumerate((one, two, three, four)):
            base = part.shape[0] - rows if owner == 3 else 0

            @pl.when(at == j)
            def _(part=part, out=out, base=base, rows=rows):
                out[...] = part[base : base + rows, :]


def hand_out(scalars, parts, cuts):
    outs = [((rows, D), f32) for rows in cuts]
    one, two, three, four = call(hand_out_kernel, outs, flops=10**8, data=1 << 18)(
        scalars, *parts
    )
    return one.T, two.T, three.T, four


def local(
    tokens,
    image_count,
    w_qkv,
    w_out,
    w_up,
    w_down,
    vectors,
    cotangent,
    mom_qkv,
    mom_out,
    mom_up,
    mom_down,
    mom_vectors,
):
    group_size = lax.axis_size("group")
    replicas = lax.axis_size("replica")
    group_index = lax.axis_index("group")
    replica_index = lax.axis_index("replica")
    chips = group_size // 2
    tok_rows = tokens.shape[0]
    slab_rows = group_size * tok_rows
    image_total = lax.dynamic_index_in_dim(image_count, replica_index, 0, keepdims=False)
    first_slot = group_index * tok_rows
    first_image = first_slot // L
    scalars = jnp.stack(
        [
            first_slot - first_image * L,
            slab_rows - first_image * L,
            image_total * L - first_slot,
            replica_index,
            group_index // 2,
            group_index % 2,
        ]
    ).astype(jnp.int32)

    def swap(x):
        return lax.ppermute(x, "group", [(i, i ^ 1) for i in range(group_size)])

    def hop(x, by):
        return lax.ppermute(x, "group", [(i, i ^ (2 * by)) for i in range(group_size)])

    def cross(x, by):
        return lax.ppermute(x, "replica", [(i, i ^ by) for i in range(replicas)])

    def halo(x):
        ends = group_size - 1
        lower = lax.ppermute(x[tok_rows - HALO :], "group", [(i, i + 1) for i in range(ends)])
        upper = lax.ppermute(x[:HALO], "group", [(i + 1, i) for i in range(ends)])
        return lower, x, upper

    def along_chips(x):
        return jnp.stack([x] + [hop(x, k) for k in range(1, chips)])

    width = D // group_size
    piece = 4 * width // replicas
    cuts = (3 * width, width, 4 * width, 4 * width)
    first_stack = jnp.concatenate([w_qkv.T, w_out.T], axis=0)
    second_stack = jnp.concatenate([w_up.T, w_down], axis=0)
    mom_stack = jnp.concatenate([mom_qkv.T, mom_out.T, mom_up.T, mom_down], axis=0)
    around = halo(tokens)

    def split(stack):
        one, two, three, four = (stack[sum(cuts[:i]) : sum(cuts[: i + 1])] for i in range(4))
        return one.T, two.T, three.T, four

    def finish(block_out, grad_tokens, grads, new_mom, dvec, updates):
        grad_vectors = lax.dynamic_slice_in_dim(dvec[:12], group_index * width, width, 1)
        new_vectors = vector_momentum * mom_vectors + grad_vectors
        return (
            block_out,
            grad_tokens,
            *split(grads),
            grad_vectors,
            *split(new_mom),
            new_vectors,
            *updates,
            -vector_rate * new_vectors,
        )

    if replicas != 4 or piece % 16:
        def rows_of(stack, inner):
            parts = lax.all_gather(stack, "group")
            rows = jnp.concatenate(
                [parts[:, :inner].reshape(-1, D), parts[:, inner:].reshape(-1, D)], axis=0
            )
            hi, lo = halves(rows)
            return jnp.concatenate([hi, lo, hi], axis=1)

        def shares_of(total, cut, inner):
            one, two = total[:cut], total[cut:]
            parts = jnp.concatenate(
                [one.reshape(group_size, inner, D), two.reshape(group_size, -1, D)], axis=1
            )
            return lax.psum_scatter(parts, "group", scatter_dimension=0)

        w_one, w_two = rows_of(first_stack, 3 * width), rows_of(second_stack, 4 * width)
        vec = jnp.pad(lax.all_gather(vectors, "group", axis=1, tiled=True), ((0, 4), (0, 0)))
        *saved, a3, middle = attend(scalars, *around, w_one, vec)
        block_out, slope, n3, m3, down = mlp(
            scalars, None, middle, cotangent, w_two, vec, vec[8:12].reshape(1, FF)
        )
        d_middle, dvec, up = mlp_back(
            scalars, None, middle, cotangent, w_two, vec, slope, n3, m3
        )
        second = jnp.concatenate([up, down], axis=0)
        d_around = halo(d_middle)
        some, more = (attend_back(scalars, i, 2, d_around, w_one, *saved) for i in (0, 2))
        first, d_hi, d_lo, sums = attend_grads(
            scalars, None, some, more, tokens, d_middle, vec, a3
        )
        grad_tokens, dvec = token_grads(
            scalars, d_hi, d_lo, w_one, tokens, d_middle, vec, sums, dvec
        )
        grads, dvec = lax.psum(
            (
                jnp.concatenate(
                    [shares_of(first, 3 * D, 3 * width), shares_of(second, FF, 4 * width)], axis=0
                ),
                lax.psum(dvec, "group"),
            ),
            "replica",
        )
        new_mom = muon_momentum * mom_stack + grads
        blocks = [new_mom[sum(cuts[:i]) : sum(cuts[: i + 1])] for i in range(4)]
        grams = lax.psum(jnp.stack([fdot(x, x, TN, precise) for x in blocks]), "group")
        updates = [
            polar(grams[i], x) * (-muon_rate * rate)
            for i, (x, rate) in enumerate(zip(blocks, (3.0**0.5, 1.0, (FF / D) ** 0.5, 1.0)))
        ]
        updates = [x if i == 3 else x.T for i, x in enumerate(updates)]
        return finish(block_out, grad_tokens, grads, new_mom, dvec, updates)

    my_second = jnp.concatenate(
        [
            lax.dynamic_slice_in_dim(second_stack, (4 * n + replica_index) * piece, piece, 0)
            for n in range(2)
        ],
        axis=0,
    )

    others = range(1, replicas)
    start = first_message(replica_index.astype(jnp.int32).reshape(1), w_qkv.T, w_out.T, vectors)
    start = [start] + [hop(start, k) for k in range(1, chips)]
    first = jnp.concatenate([x[:piece] for x in start], axis=0)
    vec_parts = jnp.concatenate([x[piece:] for x in start], axis=0)
    first, vec_parts, scalars = lax.optimization_barrier((first, vec_parts, scalars))
    first_other, vec_other = [swap(first)], swap(vec_parts)
    first = [first] + [cross(first, j) for j in others]
    first_other[0], my_second = lax.optimization_barrier((first_other[0], my_second))
    second = [my_second] + [hop(my_second, k) for k in range(1, chips)]
    first[1:], second = lax.optimization_barrier((first[1:], second))
    second = jnp.concatenate(second, axis=0)
    second = [second] + [cross(second, j) for j in others]
    second_other = [swap(second[0])]
    first_other += [swap(first[j]) for j in others]
    w_one, vec, bias = unpack(
        scalars, chips, first, first_other, first_rows, vec_parts, vec_other
    )
    *saved, a3, middle = attend(scalars, *around, w_one, vec)
    for j in others:
        second[j], middle = lax.optimization_barrier((second[j], middle))
        second_other.append(swap(second[j]))
    w_two = unpack(scalars, chips, second, second_other, second_rows)[0]
    shape = (chips, piece, D)

    def join(keep, other):
        return [x + other[j] for j, x in enumerate(keep)]

    def exchange(parts):
        return [parts[0]] + [cross(parts[j], j) for j in others]

    block_out, slope, n3, m3, *keep, send = mlp(
        scalars, shape, middle, cotangent, w_two, vec, bias
    )
    other = swap(send)
    down_keep = keep
    d_middle, dvec, *keep, send = mlp_back(
        scalars, shape, middle, cotangent, w_two, vec, slope, n3, m3
    )
    down, d_middle, send = lax.optimization_barrier((join(down_keep, other), d_middle, send))
    d_around = halo(d_middle)
    other = swap(send)
    down = exchange(down)
    some = attend_back(scalars, 0, 2, d_around, w_one, *saved)
    up, some, d_around = lax.optimization_barrier((join(keep, other), some, d_around))
    up = exchange(up)
    more = attend_back(scalars, 2, 2, d_around, w_one, *saved)
    *keep, send, d_hi, d_lo, sums = attend_grads(
        scalars, shape, some, more, tokens, d_middle, vec, a3
    )
    grad_tokens, dvec = token_grads(scalars, d_hi, d_lo, w_one, tokens, d_middle, vec, sums, dvec)
    keep, send, dvec, up, down = lax.optimization_barrier((keep, send, dvec, up, down))
    other, dvec = swap(send), dvec + swap(dvec)
    first, dvec, up, down = lax.optimization_barrier((join(keep, other), dvec, up, down))
    first = exchange(first)

    def over_chips(messages):
        return sum((hop(messages[k], k) for k in range(1, len(messages))), messages[0])

    def rows_for(parts, k):
        return sum((x[k] for x in parts[1:]), parts[0][k])

    second_sum = over_chips(
        [jnp.concatenate([rows_for(up, k), rows_for(down, k), dvec], axis=0) for k in range(chips)]
    )
    up_sum, down_sum, dvec = (
        second_sum[:piece], second_sum[piece : 2 * piece], second_sum[2 * piece :]
    )
    first_sum = over_chips([rows_for(first, k) for k in range(chips)])

    def for_replica(replica):
        return jnp.where(replica == 0, up_sum, jnp.where(replica == 2, down_sum, first_sum))

    mine = jnp.concatenate([first_sum, up_sum, down_sum], axis=0)
    taken = [cross(for_replica(lax.bitwise_xor(replica_index, j)), j) for j in others]
    own, keep, send = own_gradients(scalars, mine, taken, mom_stack, chips)
    t = keep + swap(send)
    t = t[0] + sum(hop(t[k], k) for k in range(1, chips))
    gram = along_chips(t)
    update_own = update(scalars, gram, swap(gram), own)
    mine = jnp.concatenate([mine, dvec], axis=0)
    parts = [mine] + [cross(mine, j) for j in others]
    parts, update_own = lax.optimization_barrier((parts, update_own))
    updates = [update_own] + [cross(update_own, j) for j in others]
    dvec = sum((x[3 * piece :] for x in parts[1:]), parts[0][3 * piece :])
    grads, new_mom = all_gradients(scalars, parts, mom_stack)
    updates = hand_out(scalars, updates, cuts)
    return finish(block_out, grad_tokens, grads, new_mom, dvec, updates)


def solution(mesh):
    tokens, whole, columns, rows = P(("replica", "group"), None), P(), P(None, "group"), P("group", None)
    params = (columns, columns, columns, rows, columns)
    return jax.shard_map(
        local,
        mesh=mesh,
        in_specs=(tokens, whole, *params, tokens, *params),
        out_specs=(tokens, tokens, *params, *params, *params),
        check_vma=False,
    )
```

```python
import functools

import jax
import jax.numpy as jnp
from jax import lax
from jax.experimental import pallas as pl
from jax.experimental.pallas import tpu as pltpu
from jax.sharding import PartitionSpec as P

D = 384
HEADS = 6
HEAD_DIM = 64
FF = 1536
L = 197
NS_STEPS = 5
SLOTS = 4
SLOT = 208
HALO = 200
TILE = 512

f32, bf16 = jnp.float32, jnp.bfloat16
high = lax.Precision.HIGH
precise = lax.Precision.HIGHEST
ns_coeffs = (3.4445, -4.775, 2.0315)
norm_eps = 1e-06
ns_eps = 1e-07
muon_momentum = 0.95
vector_momentum = 0.9
muon_rate = 0.5
vector_rate = 0.001
mask_fill = -1e30

UPPER = ((0, 0), (0, 1), (0, 2), (1, 1), (1, 2), (2, 2))
NN = (((1,), (0,)), ((), ()))
NT = (((1,), (1,)), ((), ()))
TN = (((0,), (0,)), ((), ()))
VMEM = pl.BlockSpec(memory_space=pltpu.VMEM)
SMEM = pl.BlockSpec(memory_space=pltpu.SMEM)


def call(body, outs, scratch=(), flops=0, data=0):
    def run(scalars, *arrays):
        return pl.pallas_call(
            body,
            out_shape=[jax.ShapeDtypeStruct(s, t) for s, t in outs],
            in_specs=[SMEM] + [VMEM] * len(arrays),
            out_specs=[VMEM] * len(outs),
            scratch_shapes=[pltpu.VMEM(s, t) for s, t in scratch],
            compiler_params=pltpu.CompilerParams(vmem_limit_bytes=28 << 20),
            cost_estimate=pl.CostEstimate(flops=flops, bytes_accessed=data, transcendentals=0),
        )(scalars, *arrays)

    return run


def mm(a, b, dims):
    return lax.dot_general(a, b, dims, preferred_element_type=f32)


def fdot(a, b, dims, precision=high):
    return lax.dot_general(a, b, dims, precision=precision, preferred_element_type=f32)


def halves(x):
    hi = x.astype(bf16)
    return hi, (x - hi.astype(f32)).astype(bf16)


def triple(x):
    hi, lo = halves(x)
    return jnp.concatenate([hi, hi, lo], axis=1)


def by_rows(hi, lo, both):
    wide = mm(hi, both[:, : 2 * D], NN)
    return wide[:, :D] + wide[:, D:] + mm(lo, both[:, :D], NN)


def by_tokens(hi, lo, other):
    wide = mm(hi, other[:, D:], TN)
    return wide[:, :D] + wide[:, D:] + mm(lo, other[:, :D], TN)


def standardized(x):
    centered = x - jnp.mean(x, axis=-1, keepdims=True)
    rstd = lax.rsqrt(jnp.mean(centered * centered, axis=-1, keepdims=True) + norm_eps)
    return centered * rstd, rstd


def norm_back(d_norm, xhat, rstd, scale):
    g = d_norm * (1.0 + scale)
    return rstd * (
        g - jnp.mean(g, axis=-1, keepdims=True) - xhat * jnp.mean(g * xhat, axis=-1, keepdims=True)
    )


def row_sum(x):
    return jnp.sum(x, axis=0, keepdims=True)


def window_start(scalars, slot):
    start = HALO - scalars[0] + L * slot
    aligned = pl.multiple_of((start // 8) * 8, 8)
    return aligned, start - aligned


def fill_window(window, scalars, inside, own, outside):
    rows = own.shape[0]
    even = scalars[5] == 0
    window[:HALO, :] = jnp.where(even, outside[...], inside[...])
    window[HALO : HALO + rows, :] = own[...]
    window[HALO + rows : 2 * HALO + rows, :] = jnp.where(even, inside[...], outside[...])
    window[2 * HALO + rows :, :] = jnp.zeros((window.shape[0] - 2 * HALO - rows, D), f32)


def load_slot(window, scalars, slot):
    aligned, shift = window_start(scalars, slot)
    block = window[pl.ds(aligned, SLOT + 8), :]
    return pltpu.roll(block, lax.rem(SLOT + 8 - shift, SLOT + 8), 0)[:SLOT]


def store_slot(window, scalars, slot, value):
    aligned, shift = window_start(scalars, slot)
    block = jnp.concatenate([value, jnp.zeros((8, value.shape[1]), f32)], axis=0)
    block = pltpu.roll(block, shift, 0)
    rows = lax.broadcasted_iota(jnp.int32, (SLOT + 8, 1), 0)
    window[pl.ds(aligned, SLOT + 8), :] = jnp.where(
        rows >= shift, block, window[pl.ds(aligned, SLOT + 8), :]
    )


def window_rows(rows):
    return 2 * HALO + rows + 96


def pairs(x):
    hi, lo = halves(x)
    return [
        jnp.concatenate([hi[:, at : at + HEAD_DIM], lo[:, at : at + HEAD_DIM]], axis=1)
        for at in range(0, D, HEAD_DIM)
    ]


def twice(x):
    return jnp.concatenate([x, x], axis=1)


def spread(x):
    hi, lo = x[:, :HEAD_DIM], x[:, HEAD_DIM:]
    return jnp.concatenate([hi, hi, lo, lo], axis=1)


def times(hi, lo, other):
    wide = mm(hi, other, NN)
    return wide[:, :HEAD_DIM] + wide[:, HEAD_DIM:] + mm(lo, other[:, :HEAD_DIM], NN)


def times_down(other, hi, lo):
    tall = mm(other, hi, NN)
    return tall[:HEAD_DIM] + tall[HEAD_DIM:] + mm(other[:HEAD_DIM], lo, NN)


def attend_kernel(
    scalars, lower, own, upper, w, vec, q2, kt2, v2, probs_hi, probs_lo, a3, middle, window, proj, att_win
):
    rows = own.shape[0]
    fill_window(window, scalars, lower, own, upper)
    step = (2 * HALO + rows) // 3

    def project_step(t, carry):
        at = pl.multiple_of(t * step, 16)
        xhat, _ = standardized(window[pl.ds(at, step), :])
        left = triple(xhat * (1.0 + vec[0:1, :]) + vec[1:2, :])
        for part, bias in ((0, vec[2:3, :]), (1, None), (2, vec[3:4, :])):
            value = mm(left, w[part * D : (part + 1) * D, :], NT)
            proj[pl.ds(at, step), part * D : (part + 1) * D] = value if bias is None else value + bias
        return carry

    lax.fori_loop(0, 3, project_step, 0)
    proj[2 * HALO + rows :, :] = jnp.zeros((96, 3 * D), f32)

    def slot_step(slot, carry):
        qkv = load_slot(proj, scalars, slot)
        keys = jnp.minimum(L, scalars[1] - L * slot)
        keep = lax.broadcasted_iota(jnp.int32, (SLOT, SLOT), 0) < keys
        q, k, v = (pairs(qkv[:, part * D : (part + 1) * D]) for part in range(3))
        heads = []
        for h in range(HEADS):
            q2[slot, h] = q[h]
            v2[slot, h] = v[h]
            kt2[slot, h] = jnp.transpose(k[h])
            scores = mm(twice(k[h]), spread(q[h]), NT) * HEAD_DIM**-0.5
            scores = jnp.where(keep, scores, mask_fill)
            weights = jnp.exp(scores - jnp.max(scores, axis=0, keepdims=True))
            weights = weights * (1.0 / jnp.sum(weights, axis=0, keepdims=True))
            hi, lo = halves(weights)
            probs_hi[slot, h] = hi
            probs_lo[slot, h] = lo
            heads.append(times_down(jnp.transpose(v[h]), hi, lo))
        store_slot(att_win, scalars, slot, jnp.transpose(jnp.concatenate(heads, axis=0)))
        return carry

    lax.fori_loop(0, SLOTS, slot_step, 0)
    att = triple(att_win[HALO : HALO + rows, :])
    a3[...] = att
    middle[...] = own[...] + mm(att, w[3 * D :, :], NT) + vec[4:5, :]


def attend(scalars, lower, own, upper, w, vec):
    rows = own.shape[0]
    return call(
        attend_kernel,
        [
            ((SLOTS, HEADS, SLOT, 128), bf16),
            ((SLOTS, HEADS, 128, SLOT), bf16),
            ((SLOTS, HEADS, SLOT, 128), bf16),
            ((SLOTS, HEADS, SLOT, SLOT), bf16),
            ((SLOTS, HEADS, SLOT, SLOT), bf16),
            ((rows, 3 * D), bf16),
            ((rows, D), f32),
        ],
        [
            ((window_rows(rows), D), f32),
            ((window_rows(rows), 3 * D), f32),
            ((window_rows(rows), D), f32),
        ],
        flops=10**8,
        data=1 << 18,
    )(scalars, lower, own, upper, w, vec)


def mlp_kernel(scalars, mid, cot, w, vec, bias, out, slope, n3, m3, *rest):
    parts, (total, h_hi, h_lo) = rest[:-3], rest[-3:]
    if len(parts) == 1:
        total = parts[0]
    rows = mid.shape[0]
    xhat, _ = standardized(mid[...])
    n3[...] = triple(xhat * (1.0 + vec[5:6, :]) + vec[6:7, :])
    live = lax.broadcasted_iota(jnp.int32, (rows, 1), 0) < scalars[2]
    m3[...] = triple(jnp.where(live, cot[...], 0.0))

    def tile_step(t, carry):
        at = pl.multiple_of(t * TILE, TILE)
        pre = mm(n3[...], w[pl.ds(at, TILE), :], NT) + bias[0:1, pl.ds(at, TILE)]
        cdf = 0.5 + 0.5 * lax.erf(pre * (0.5**0.5))
        slope[:, pl.ds(at, TILE)] = cdf + pre * (jnp.exp(-0.5 * pre * pre) * 0.3989422804014327)
        hi, lo = halves(pre * cdf)
        h_hi[:, pl.ds(at, TILE)] = hi
        h_lo[:, pl.ds(at, TILE)] = lo
        total[pl.ds(at, TILE), :] = by_tokens(hi, lo, m3)
        return carry

    lax.fori_loop(0, FF // TILE, tile_step, 0)
    out[...] = mid[...] + by_rows(h_hi[...], h_lo[...], w[FF:, :]) + vec[7:8, :]
    scatter_parts(scalars, total, parts, quarter_rows)


def mlp(scalars, parts, mid, cot, w, vec, bias):
    rows = mid.shape[0]
    outs, scratch = part_outs(parts, FF)
    return call(
        mlp_kernel,
        [((rows, D), f32), ((rows, FF), f32)] + [((rows, 3 * D), bf16)] * 2 + outs,
        [scratch] + [((rows, FF), bf16)] * 2,
        flops=10**8,
        data=1 << 18,
    )(scalars, mid, cot, w, vec, bias)


def mlp_back_kernel(scalars, mid, cot, w, vec, slope, n3, m3, dmid, dvec, *rest):
    parts, (total, d_hi, d_lo, dbias) = rest[:-4], rest[-4:]
    if len(parts) == 1:
        total = parts[0]
    rows = mid.shape[0]

    def tile_step(t, carry):
        at = pl.multiple_of(t * TILE, TILE)
        d_pre = mm(m3[...], w[pl.ds(FF + at, TILE), :], NT) * slope[:, pl.ds(at, TILE)]
        dbias[0:1, pl.ds(at, TILE)] = row_sum(d_pre)
        hi, lo = halves(d_pre)
        d_hi[:, pl.ds(at, TILE)] = hi
        d_lo[:, pl.ds(at, TILE)] = lo
        total[pl.ds(at, TILE), :] = by_tokens(hi, lo, n3)
        return carry

    lax.fori_loop(0, FF // TILE, tile_step, 0)
    scatter_parts(scalars, total, parts, quarter_rows)
    d_norm = by_rows(d_hi[...], d_lo[...], w[:FF, :])
    xhat, rstd = standardized(mid[...])
    live = lax.broadcasted_iota(jnp.int32, (rows, 1), 0) < scalars[2]
    masked = jnp.where(live, cot[...], 0.0)
    d_middle = masked + norm_back(d_norm, xhat, rstd, vec[5:6, :])
    dmid[...] = d_middle
    zero = jnp.zeros((4, D), f32)
    dvec[...] = jnp.concatenate(
        [zero, row_sum(d_middle), row_sum(d_norm * xhat), row_sum(d_norm), row_sum(masked)]
        + [dbias[0:1, i * D : (i + 1) * D] for i in range(4)]
        + [zero],
        axis=0,
    )


def mlp_back(scalars, parts, mid, cot, w, vec, slope, n3, m3):
    rows = mid.shape[0]
    outs, scratch = part_outs(parts, FF)
    return call(
        mlp_back_kernel,
        [((rows, D), f32), ((16, D), f32)] + outs,
        [scratch] + [((rows, FF), bf16)] * 2 + [((8, FF), f32)],
        flops=10**8,
        data=1 << 18,
    )(scalars, mid, cot, w, vec, slope, n3, m3)


def place(scalars, i, j, k):
    owner = 2 * lax.bitwise_xor(scalars[4], k) + lax.bitwise_xor(scalars[5], i)
    return owner, lax.bitwise_xor(scalars[3], j)


def first_rows(owner, quarter, piece):
    return pl.multiple_of(
        jnp.where(quarter < 3, owner * 3 * piece + quarter * piece, 3 * D + owner * piece), piece
    )


def second_rows(owner, quarter, piece):
    half = piece // 2
    at = owner * 4 * half + quarter * half
    return pl.multiple_of(at, half), pl.multiple_of(FF + at, half)


def quarter_rows(owner, quarter, piece):
    return pl.multiple_of(owner * 4 * piece + quarter * piece, piece)


def part_outs(parts, rows):
    if parts is None:
        return [((rows, D), f32)], ((8, D), f32)
    return [(parts, f32)] * 4 + [((4, *parts), f32)], ((rows, D), f32)


def scatter_parts(scalars, total, outs, rows_of):
    if len(outs) == 1:
        return
    chips, piece, _ = outs[0].shape
    for n in range(8):
        for k in range(chips):
            owner, quarter = place(scalars, n // 4, n % 4, k)
            rows = total[pl.ds(rows_of(owner, quarter, piece), piece), :]
            if n < 4:
                outs[n][k] = rows
            else:
                outs[4][n - 4, k] = rows


def attend_back_kernel(first_slot, scalars, lower, own, upper, w, q2, kt2, v2, probs_hi, probs_lo, out, window):
    rows = own.shape[0]
    fill_window(window, scalars, lower, own, upper)

    def slot_step(step, carry):
        slot = first_slot + step
        row = lax.broadcasted_iota(jnp.int32, (SLOT, 1), 0)
        at_own = row + L * slot - scalars[0]
        mine = (at_own >= 0) & (at_own < rows) & (row < L)
        d_mid = jnp.where(row < L, load_slot(window, scalars, slot), 0.0)
        d_out = pairs(by_rows(*halves(d_mid), w[3 * D :, :]))
        d_q, d_k, d_v = [], [], []
        for h in range(HEADS):
            hi, lo = probs_hi[slot, h], probs_lo[slot, h]
            weights = hi.astype(f32) + lo.astype(f32)
            d_weights = mm(twice(v2[slot, h]), spread(d_out[h]), NT)
            mean = jnp.sum(weights * d_weights, axis=0, keepdims=True)
            s_hi, s_lo = halves(weights * (d_weights - mean) * HEAD_DIM**-0.5)
            d_v.append(times(hi, lo, d_out[h]))
            d_k.append(times(s_hi, s_lo, q2[slot, h]))
            d_q.append(times_down(kt2[slot, h], s_hi, s_lo))
        d_q = jnp.transpose(jnp.concatenate(d_q, axis=0))
        d_proj = jnp.concatenate([d_q] + d_k + d_v, axis=1)
        out[step] = jnp.where(mine, d_proj, 0.0)
        return carry

    lax.fori_loop(0, out.shape[0], slot_step, 0)


def attend_back(scalars, first_slot, slots, around, w, *saved):
    rows = around[1].shape[0]
    return call(
        functools.partial(attend_back_kernel, first_slot),
        [((slots, SLOT, 3 * D), f32)],
        [((window_rows(rows), D), f32)],
        flops=10**8,
        data=1 << 18,
    )(scalars, *around, w, *saved)[0]


def attend_grads_kernel(scalars, some, more, tokens, d_mid, vec, a3, *rest):
    outs, (d_hi, d_lo, sums), (total, window) = rest[:-5], rest[-5:-2], rest[-2:]
    if len(outs) == 1:
        total = outs[0]
    rows = tokens.shape[0]
    for i, part in enumerate((some, more)):

        def slot_step(step, carry, i=i, part=part):
            store_slot(window, scalars, i * part.shape[0] + step, part[step])
            return carry

        lax.fori_loop(0, part.shape[0], slot_step, 0)
    xhat, _ = standardized(tokens[...])
    n3 = triple(xhat * (1.0 + vec[0:1, :]) + vec[1:2, :])

    def part_step(part, carry):
        at = pl.ds(pl.multiple_of(part * D, D), D)
        d_proj = window[HALO : HALO + rows, at]
        hi, lo = halves(d_proj)
        d_hi[:, at] = hi
        d_lo[:, at] = lo
        total[at, :] = by_tokens(hi, lo, n3)
        sums[part] = jnp.broadcast_to(row_sum(d_proj), (8, D))
        return carry

    lax.fori_loop(0, 3, part_step, 0)
    total[3 * D :, :] = by_tokens(*halves(d_mid[...]), a3)
    scatter_parts(scalars, total, outs, first_rows)


def attend_grads(scalars, parts, some, more, tokens, d_mid, vec, a3):
    rows = tokens.shape[0]
    outs, scratch = part_outs(parts, 4 * D)
    return call(
        attend_grads_kernel,
        outs + [((rows, 3 * D), bf16)] * 2 + [((3, 8, D), f32)],
        [scratch, ((window_rows(rows), 3 * D), f32)],
        flops=10**8,
        data=1 << 18,
    )(scalars, some, more, tokens, d_mid, vec, a3)


def token_grads_kernel(scalars, d_hi, d_lo, w, tokens, d_mid, vec, sums, dvec_in, dtok, dvec):
    xhat, rstd = standardized(tokens[...])
    d_norm = by_rows(d_hi[...], d_lo[...], w[: 3 * D, :])
    dtok[...] = d_mid[...] + norm_back(d_norm, xhat, rstd, vec[0:1, :])
    new = [row_sum(d_norm * xhat), row_sum(d_norm), sums[0, 0:1], sums[2, 0:1], jnp.zeros((12, D), f32)]
    dvec[...] = dvec_in[...] + jnp.concatenate(new, axis=0)


def token_grads(scalars, *arrays):
    rows = arrays[0].shape[0]
    return call(
        token_grads_kernel, [((rows, D), f32), ((16, D), f32)], flops=10**8, data=1 << 18
    )(scalars, *arrays)


def store_split(w, at, x):
    hi, lo = halves(x)
    w[pl.ds(at, x.shape[0]), :] = jnp.concatenate([hi, lo, hi], axis=1)


def unpack_kernel(rows_of, chips, piece, step, scalars, *refs):
    mine, other, rest = refs[:4], refs[4:8], refs[8:]
    if step:
        vectors, (w, vec, bias) = rest[:2], rest[2:]
    else:
        (w,) = rest
    for i, parts in enumerate((mine, other)):
        for j in range(4):
            for k in range(chips):
                owner, quarter = place(scalars, i, j, k)
                at = rows_of(owner, quarter, piece)
                at = at if isinstance(at, tuple) else (at,)
                share = piece // len(at)
                for n, to in enumerate(at):
                    base = k * piece + n * share
                    store_split(w, to, parts[j][base : base + share, :])
    if step:
        width = D // (2 * chips)
        lane = lax.broadcasted_iota(jnp.int32, (step, D), 1)
        sums = [jnp.zeros((step, D), f32), jnp.zeros((step, D), f32)]
        for i, parts in enumerate(vectors):
            for k in range(chips):
                owner, _ = place(scalars, i, 0, k)
                block = parts[k * step : (k + 1) * step, :]
                for n in range(2):
                    mine_only = jnp.where((lane >= n * width) & (lane < (n + 1) * width), block, 0.0)
                    shift = lax.rem((owner - n) * width + D, D)
                    sums[n] = sums[n] + pltpu.roll(mine_only, shift, 1)
        vec[:step, :] = sums[0]
        vec[step:, :] = sums[1]
        bias[...] = jnp.concatenate([sums[1][s : s + 1, :] for s in range(4)], axis=1)


def unpack(scalars, chips, mine, other, rows_of, *vectors):
    total = 8 * mine[0].shape[0]
    outs = [((total, 3 * D), bf16)]
    if vectors:
        outs += [((16, D), f32), ((1, FF), f32)]
    return call(
        functools.partial(
            unpack_kernel,
            rows_of,
            chips,
            mine[0].shape[0] // chips,
            vectors[0].shape[0] // chips if vectors else 0,
        ),
        outs,
        [],
        flops=10**8,
        data=1 << 18,
    )(scalars, *mine, *other, *vectors)


def own_gradients_kernel(scalars, mine, *refs):
    others, (mom, own, keep, send, total) = refs[:3], refs[3:]
    piece = mine.shape[0] // 3
    replica = scalars[3]
    start = jnp.where(replica == 0, 4, jnp.where(replica == 2, 8, 0)) * piece
    at = pl.multiple_of(jnp.where(replica == 0, 1, jnp.where(replica == 2, 2, 0)) * piece, piece)
    own[...] = muon_momentum * mom[pl.ds(pl.multiple_of(start, piece), 4 * piece), :]
    for j, part in enumerate((mine, *others)):
        quarter = lax.bitwise_xor(replica, j)
        rows = pl.ds(pl.multiple_of(quarter * piece, piece), piece)
        own[rows, :] = own[rows, :] + (part[pl.ds(at, piece), :] if j == 0 else part[...])
    row = lax.broadcasted_iota(jnp.int32, (4 * piece, 1), 0)
    drop = ((replica == 1) & (row >= 3 * piece)) | ((replica == 3) & (row < 3 * piece))
    block = jnp.where(drop, 0.0, own[...])
    own[...] = block
    gram = fdot(block, block, TN, precise)
    for n, (row, column) in enumerate(UPPER):
        total[n * 128 : (n + 1) * 128, :] = gram[
            row * 128 : (row + 1) * 128, column * 128 : (column + 1) * 128
        ]
    chips, share, _ = keep.shape
    for i, out in enumerate((keep, send)):
        for k in range(chips):
            at = lax.bitwise_xor(scalars[5], i) * chips + lax.bitwise_xor(scalars[4], k)
            out[k] = total[pl.ds(pl.multiple_of(at * share, share), share), :]


def own_gradients(scalars, mine, others, mom, chips):
    share = 128 * len(UPPER) // (2 * chips)
    return call(
        own_gradients_kernel,
        [((mom.shape[0] // 3, D), f32)] + [((chips, share, 128), f32)] * 2,
        [((128 * len(UPPER), 128), f32)],
        flops=10**8,
        data=1 << 18,
    )(scalars, mine, *others, mom)


def all_gradients_kernel(scalars, *refs):
    parts, (mom, grads, new_mom) = refs[:4], refs[4:]
    piece = mom.shape[0] // 12
    for j in range(4):
        quarter = lax.bitwise_xor(scalars[3], j)
        for n in range(3):
            rows = pl.ds(pl.multiple_of((4 * n + quarter) * piece, piece), piece)
            grads[rows, :] = parts[j][n * piece : (n + 1) * piece, :]
    new_mom[...] = muon_momentum * mom[...] + grads[...]


def all_gradients(scalars, parts, mom):
    return call(all_gradients_kernel, [(mom.shape, f32)] * 2, flops=10**8, data=1 << 18)(
        scalars, *parts, mom
    )


def pieces(x):
    hi, mid = halves(x)
    return hi, mid, (x - hi.astype(f32) - mid.astype(f32)).astype(bf16)


def full_product(a, b):
    (ah, am, al), (bh, bm, bl) = a, b
    return mm(
        jnp.concatenate([ah, ah, am, ah, al, am], axis=1),
        jnp.concatenate([bh, bm, bh, bl, bh, bm], axis=0),
        NN,
    )


def three_product(a, b):
    (ah, am, _), (bh, bm, _) = a, b
    return mm(
        jnp.concatenate([ah, am, ah], axis=1), jnp.concatenate([bh, bh, bm], axis=0), NN
    )


def identity():
    row = lax.broadcasted_iota(jnp.int32, (D, D), 0)
    return jnp.where(row == lax.broadcasted_iota(jnp.int32, (D, D), 1), 1.0, 0.0)


def polynomial(gram, product):
    g = pieces(gram)
    return g, ns_coeffs[1] * gram + ns_coeffs[2] * product(g, g) + ns_coeffs[0] * identity()


def polar_step(gram, block):
    g, poly = polynomial(gram, full_product)
    p = pieces(poly)
    return full_product(p, pieces(full_product(p, g))), three_product(pieces(block), p)


def polar_end(gram, block):
    return three_product(pieces(block), pieces(polynomial(gram, three_product)[1]))


def polar_start(gram, block):
    scale = 1.0 / (jnp.sqrt(jnp.sum(gram * identity())) + ns_eps)
    return gram * (scale * scale), block * scale


def polar(gram, block):
    state = polar_start(gram, block)
    for _ in range(NS_STEPS - 1):
        state = polar_step(*state)
    return polar_end(*state)


def update_kernel(scalars, mine, other, own, out, total, gram, block):
    chips, share, _ = mine.shape
    for i, parts in enumerate((mine, other)):
        for k in range(chips):
            at = lax.bitwise_xor(scalars[5], i) * chips + lax.bitwise_xor(scalars[4], k)
            total[pl.ds(pl.multiple_of(at * share, share), share), :] = parts[k]
    blocks = {}
    for n, (row, column) in enumerate(UPPER):
        blocks[row, column] = total[n * 128 : (n + 1) * 128, :]
        if row != column:
            blocks[column, row] = jnp.transpose(blocks[row, column])
    gram[...], block[...] = polar_start(
        jnp.concatenate(
            [jnp.concatenate([blocks[row, column] for column in range(3)], axis=1) for row in range(3)],
            axis=0,
        ),
        own[...],
    )

    def step(_, carry):
        gram[...], block[...] = polar_step(gram[...], block[...])
        return carry

    lax.fori_loop(0, NS_STEPS - 1, step, 0)
    replica = scalars[3]
    rate = jnp.where(replica == 1, 3.0**0.5, jnp.where(replica == 0, (FF / D) ** 0.5, 1.0))
    out[...] = polar_end(gram[...], block[...]) * (-muon_rate * rate)


def update(scalars, mine, other, own):
    return call(
        update_kernel,
        [(own.shape, f32)],
        [((128 * len(UPPER), 128), f32), ((D, D), f32), (own.shape, f32)],
        flops=10**8, data=1 << 18
    )(scalars, mine, other, own)[0]


def first_message_kernel(replica, qkv, out, vectors, message):
    piece = message.shape[0] - 8
    width = vectors.shape[1]

    @pl.when(replica[0] < 3)
    def _():
        message[:piece, :] = qkv[pl.ds(pl.multiple_of(replica[0] * piece, 8), piece), :]

    @pl.when(replica[0] == 3)
    def _():
        message[:piece, :] = out[...]

    message[piece:, :] = jnp.zeros((8, D), f32)
    message[piece:, :width] = vectors[:8, :]
    message[piece : piece + 4, width : 2 * width] = vectors[8:, :]


def first_message(replica, qkv, out, vectors):
    return call(
        first_message_kernel, [((out.shape[0] + 8, D), f32)], flops=10**6, data=1 << 16
    )(replica, qkv, out, vectors)[0]


def hand_out_kernel(scalars, one, two, three, four, *outs):
    for owner, out in zip((1, 3, 0, 2), outs):
        at = lax.bitwise_xor(scalars[3], owner)
        rows = out.shape[0]
        for j, part in enumerate((one, two, three, four)):
            base = part.shape[0] - rows if owner == 3 else 0

            @pl.when(at == j)
            def _(part=part, out=out, base=base, rows=rows):
                out[...] = part[base : base + rows, :]


def hand_out(scalars, parts, cuts):
    outs = [((rows, D), f32) for rows in cuts]
    one, two, three, four = call(hand_out_kernel, outs, flops=10**8, data=1 << 18)(
        scalars, *parts
    )
    return one.T, two.T, three.T, four


def local(
    tokens,
    image_count,
    w_qkv,
    w_out,
    w_up,
    w_down,
    vectors,
    cotangent,
    mom_qkv,
    mom_out,
    mom_up,
    mom_down,
    mom_vectors,
):
    group_size = lax.axis_size("group")
    replicas = lax.axis_size("replica")
    group_index = lax.axis_index("group")
    replica_index = lax.axis_index("replica")
    chips = group_size // 2
    tok_rows = tokens.shape[0]
    slab_rows = group_size * tok_rows
    image_total = lax.dynamic_index_in_dim(image_count, replica_index, 0, keepdims=False)
    first_slot = group_index * tok_rows
    first_image = first_slot // L
    scalars = jnp.stack(
        [
            first_slot - first_image * L,
            slab_rows - first_image * L,
            image_total * L - first_slot,
            replica_index,
            group_index // 2,
            group_index % 2,
        ]
    ).astype(jnp.int32)

    def swap(x):
        return lax.ppermute(x, "group", [(i, i ^ 1) for i in range(group_size)])

    def hop(x, by):
        return lax.ppermute(x, "group", [(i, i ^ (2 * by)) for i in range(group_size)])

    def cross(x, by):
        return lax.ppermute(x, "replica", [(i, i ^ by) for i in range(replicas)])

    def halo(x):
        head, tail = x[:HALO], x[tok_rows - HALO :]
        even = group_index % 2 == 0
        pairs = [(i, i + 1) for i in range(1, group_size - 1, 2)]
        inside = swap(jnp.where(even, tail, head))
        outside = lax.ppermute(
            jnp.where(even, head, tail), "group", pairs + [(j, i) for i, j in pairs]
        )
        return inside, x, outside

    def along_chips(x):
        return jnp.stack([x] + [hop(x, k) for k in range(1, chips)])

    width = D // group_size
    piece = 4 * width // replicas
    cuts = (3 * width, width, 4 * width, 4 * width)
    first_stack = jnp.concatenate([w_qkv.T, w_out.T], axis=0)
    second_stack = jnp.concatenate([w_up.T, w_down], axis=0)
    mom_stack = jnp.concatenate([mom_qkv.T, mom_out.T, mom_up.T, mom_down], axis=0)
    around = halo(tokens)

    def split(stack):
        one, two, three, four = (stack[sum(cuts[:i]) : sum(cuts[: i + 1])] for i in range(4))
        return one.T, two.T, three.T, four

    def finish(block_out, grad_tokens, grads, new_mom, dvec, updates):
        grad_vectors = lax.dynamic_slice_in_dim(dvec[:12], group_index * width, width, 1)
        new_vectors = vector_momentum * mom_vectors + grad_vectors
        return (
            block_out,
            grad_tokens,
            *split(grads),
            grad_vectors,
            *split(new_mom),
            new_vectors,
            *updates,
            -vector_rate * new_vectors,
        )

    if replicas != 4 or piece % 16:
        def rows_of(stack, inner):
            parts = lax.all_gather(stack, "group")
            rows = jnp.concatenate(
                [parts[:, :inner].reshape(-1, D), parts[:, inner:].reshape(-1, D)], axis=0
            )
            hi, lo = halves(rows)
            return jnp.concatenate([hi, lo, hi], axis=1)

        def shares_of(total, cut, inner):
            one, two = total[:cut], total[cut:]
            parts = jnp.concatenate(
                [one.reshape(group_size, inner, D), two.reshape(group_size, -1, D)], axis=1
            )
            return lax.psum_scatter(parts, "group", scatter_dimension=0)

        w_one, w_two = rows_of(first_stack, 3 * width), rows_of(second_stack, 4 * width)
        vec = jnp.pad(lax.all_gather(vectors, "group", axis=1, tiled=True), ((0, 4), (0, 0)))
        *saved, a3, middle = attend(scalars, *around, w_one, vec)
        block_out, slope, n3, m3, down = mlp(
            scalars, None, middle, cotangent, w_two, vec, vec[8:12].reshape(1, FF)
        )
        d_middle, dvec, up = mlp_back(
            scalars, None, middle, cotangent, w_two, vec, slope, n3, m3
        )
        second = jnp.concatenate([up, down], axis=0)
        d_around = halo(d_middle)
        some, more = (attend_back(scalars, i, 2, d_around, w_one, *saved) for i in (0, 2))
        first, d_hi, d_lo, sums = attend_grads(
            scalars, None, some, more, tokens, d_middle, vec, a3
        )
        grad_tokens, dvec = token_grads(
            scalars, d_hi, d_lo, w_one, tokens, d_middle, vec, sums, dvec
        )
        grads, dvec = lax.psum(
            (
                jnp.concatenate(
                    [shares_of(first, 3 * D, 3 * width), shares_of(second, FF, 4 * width)], axis=0
                ),
                lax.psum(dvec, "group"),
            ),
            "replica",
        )
        new_mom = muon_momentum * mom_stack + grads
        blocks = [new_mom[sum(cuts[:i]) : sum(cuts[: i + 1])] for i in range(4)]
        grams = lax.psum(jnp.stack([fdot(x, x, TN, precise) for x in blocks]), "group")
        updates = [
            polar(grams[i], x) * (-muon_rate * rate)
            for i, (x, rate) in enumerate(zip(blocks, (3.0**0.5, 1.0, (FF / D) ** 0.5, 1.0)))
        ]
        updates = [x if i == 3 else x.T for i, x in enumerate(updates)]
        return finish(block_out, grad_tokens, grads, new_mom, dvec, updates)

    def second_quarter(quarter):
        return jnp.concatenate(
            [
                lax.dynamic_slice_in_dim(second_stack, (4 * n + quarter) * piece, piece, 0)
                for n in range(2)
            ],
            axis=0,
        )

    my_second = second_quarter(replica_index)
    diagonal = second_quarter(lax.bitwise_xor(replica_index, 3))
    others = range(1, replicas)
    start = first_message(replica_index.astype(jnp.int32).reshape(1), w_qkv.T, w_out.T, vectors)
    start = [start] + [hop(start, k) for k in range(1, chips)]
    first = jnp.concatenate([x[:piece] for x in start], axis=0)
    vec_parts = jnp.concatenate([x[piece:] for x in start], axis=0)
    first, vec_parts, scalars, lower, upper = lax.optimization_barrier(
        (first, vec_parts, scalars, around[0], around[2])
    )
    around = lower, tokens, upper
    first_other, vec_other = [swap(first)], swap(vec_parts)
    first = [first] + [cross(first, j) for j in others]
    first_other[0], vec_other, my_second = lax.optimization_barrier(
        (first_other[0], vec_other, my_second)
    )
    second = [my_second] + [hop(my_second, k) for k in range(1, chips)]
    first[1:], second = lax.optimization_barrier((first[1:], second))
    second = jnp.concatenate(second, axis=0)
    first_other += [swap(first[j]) for j in others]
    diagonal, second, first_other = lax.optimization_barrier((diagonal, second, first_other))
    diagonal = [diagonal] + [hop(diagonal, k) for k in range(1, chips)]
    second = [second, cross(second, 1), cross(second, 2)]
    w_one, vec, bias = unpack(
        scalars, chips, first, first_other, first_rows, vec_parts, vec_other
    )
    *saved, a3, middle = attend(scalars, *around, w_one, vec)
    second[1:], diagonal, middle = lax.optimization_barrier((second[1:], diagonal, middle))
    second.append(jnp.concatenate(diagonal, axis=0))
    second_other = [swap(x) for x in second]
    w_two = unpack(scalars, chips, second, second_other, second_rows)[0]
    shape = (chips, piece, D)

    def join(keep, other):
        return [x + other[j] for j, x in enumerate(keep)]

    def exchange(parts):
        return [parts[0]] + [cross(parts[j], j) for j in others]

    block_out, slope, n3, m3, *keep, send = mlp(
        scalars, shape, middle, cotangent, w_two, vec, bias
    )
    other = swap(send)
    down_keep = keep
    d_middle, dvec, *keep, send = mlp_back(
        scalars, shape, middle, cotangent, w_two, vec, slope, n3, m3
    )
    down, d_middle, send = lax.optimization_barrier((join(down_keep, other), d_middle, send))
    d_around = halo(d_middle)
    other = swap(send)
    down = exchange(down)
    some = attend_back(scalars, 0, 2, d_around, w_one, *saved)
    up, some, d_around = lax.optimization_barrier((join(keep, other), some, d_around))
    up = exchange(up)
    more = attend_back(scalars, 2, 2, d_around, w_one, *saved)
    *keep, send, d_hi, d_lo, sums = attend_grads(
        scalars, shape, some, more, tokens, d_middle, vec, a3
    )
    grad_tokens, dvec = token_grads(scalars, d_hi, d_lo, w_one, tokens, d_middle, vec, sums, dvec)
    keep, send, dvec, up, down = lax.optimization_barrier((keep, send, dvec, up, down))
    other, dvec = swap(send), dvec + swap(dvec)
    first, dvec, up, down = lax.optimization_barrier((join(keep, other), dvec, up, down))
    first = exchange(first)

    def over_chips(messages):
        return sum((hop(messages[k], k) for k in range(1, len(messages))), messages[0])

    def rows_for(parts, k):
        return sum((x[k] for x in parts[1:]), parts[0][k])

    second_sum = over_chips(
        [jnp.concatenate([rows_for(up, k), rows_for(down, k), dvec], axis=0) for k in range(chips)]
    )
    up_sum, down_sum, dvec = (
        second_sum[:piece], second_sum[piece : 2 * piece], second_sum[2 * piece :]
    )
    first_sum = over_chips([rows_for(first, k) for k in range(chips)])

    def for_replica(replica):
        return jnp.where(replica == 0, up_sum, jnp.where(replica == 2, down_sum, first_sum))

    mine = jnp.concatenate([first_sum, up_sum, down_sum], axis=0)
    taken = [cross(for_replica(lax.bitwise_xor(replica_index, j)), j) for j in others]
    own, keep, send = own_gradients(scalars, mine, taken, mom_stack, chips)
    t = keep + swap(send)
    t = t[0] + sum(hop(t[k], k) for k in range(1, chips))
    gram = along_chips(t)
    update_own = update(scalars, gram, swap(gram), own)
    mine = jnp.concatenate([mine, dvec], axis=0)
    parts = [mine] + [cross(mine, j) for j in others]
    parts, update_own = lax.optimization_barrier((parts, update_own))
    updates = [update_own] + [cross(update_own, j) for j in others]
    dvec = sum((x[3 * piece :] for x in parts[1:]), parts[0][3 * piece :])
    grads, new_mom = all_gradients(scalars, parts, mom_stack)
    updates = hand_out(scalars, updates, cuts)
    return finish(block_out, grad_tokens, grads, new_mom, dvec, updates)


def solution(mesh):
    tokens, whole, columns, rows = P(("replica", "group"), None), P(), P(None, "group"), P("group", None)
    params = (columns, columns, columns, rows, columns)
    return jax.shard_map(
        local,
        mesh=mesh,
        in_specs=(tokens, whole, *params, tokens, *params),
        out_specs=(tokens, tokens, *params, *params, *params),
        check_vma=False,
    )
```

```python
import functools

import jax
import jax.numpy as jnp
from jax import lax
from jax.experimental import pallas as pl
from jax.experimental.pallas import tpu as pltpu
from jax.sharding import PartitionSpec as P

D = 384
HEADS = 6
HEAD_DIM = 64
FF = 1536
L = 197
NS_STEPS = 5
SLOTS = 4
SLOT = 208
HALO = 200
TILE = 512

f32, bf16 = jnp.float32, jnp.bfloat16
high = lax.Precision.HIGH
precise = lax.Precision.HIGHEST
ns_coeffs = (3.4445, -4.775, 2.0315)
norm_eps = 1e-06
ns_eps = 1e-07
muon_momentum = 0.95
vector_momentum = 0.9
muon_rate = 0.5
vector_rate = 0.001
mask_fill = -1e30

UPPER = ((0, 0), (0, 1), (0, 2), (1, 1), (1, 2), (2, 2))
NN = (((1,), (0,)), ((), ()))
NT = (((1,), (1,)), ((), ()))
TN = (((0,), (0,)), ((), ()))
VMEM = pl.BlockSpec(memory_space=pltpu.VMEM)
SMEM = pl.BlockSpec(memory_space=pltpu.SMEM)


def call(body, outs, scratch=(), flops=0, data=0):
    def run(scalars, *arrays):
        return pl.pallas_call(
            body,
            out_shape=[jax.ShapeDtypeStruct(s, t) for s, t in outs],
            in_specs=[SMEM] + [VMEM] * len(arrays),
            out_specs=[VMEM] * len(outs),
            scratch_shapes=[pltpu.VMEM(s, t) for s, t in scratch],
            compiler_params=pltpu.CompilerParams(vmem_limit_bytes=28 << 20),
            cost_estimate=pl.CostEstimate(flops=flops, bytes_accessed=data, transcendentals=0),
        )(scalars, *arrays)

    return run


def mm(a, b, dims):
    return lax.dot_general(a, b, dims, preferred_element_type=f32)


def fdot(a, b, dims, precision=high):
    return lax.dot_general(a, b, dims, precision=precision, preferred_element_type=f32)


def halves(x):
    hi = x.astype(bf16)
    return hi, (x - hi.astype(f32)).astype(bf16)


def triple(x):
    hi, lo = halves(x)
    return jnp.concatenate([hi, hi, lo], axis=1)


def by_rows(hi, lo, both):
    wide = mm(hi, both[:, : 2 * D], NN)
    return wide[:, :D] + wide[:, D:] + mm(lo, both[:, :D], NN)


def by_tokens(hi, lo, other):
    wide = mm(hi, other[:, D:], TN)
    return wide[:, :D] + wide[:, D:] + mm(lo, other[:, :D], TN)


def standardized(x):
    centered = x - jnp.mean(x, axis=-1, keepdims=True)
    rstd = lax.rsqrt(jnp.mean(centered * centered, axis=-1, keepdims=True) + norm_eps)
    return centered * rstd, rstd


def norm_back(d_norm, xhat, rstd, scale):
    g = d_norm * (1.0 + scale)
    return rstd * (
        g - jnp.mean(g, axis=-1, keepdims=True) - xhat * jnp.mean(g * xhat, axis=-1, keepdims=True)
    )


def row_sum(x):
    return jnp.sum(x, axis=0, keepdims=True)


def window_start(scalars, slot):
    start = HALO - scalars[0] + L * slot
    aligned = pl.multiple_of((start // 8) * 8, 8)
    return aligned, start - aligned


def fill_window(window, scalars, inside, own, outside):
    rows = own.shape[0]
    even = scalars[5] == 0
    window[:HALO, :] = jnp.where(even, outside[...], inside[...])
    window[HALO : HALO + rows, :] = own[...]
    window[HALO + rows : 2 * HALO + rows, :] = jnp.where(even, inside[...], outside[...])
    window[2 * HALO + rows :, :] = jnp.zeros((window.shape[0] - 2 * HALO - rows, D), f32)


def load_slot(window, scalars, slot):
    aligned, shift = window_start(scalars, slot)
    block = window[pl.ds(aligned, SLOT + 8), :]
    return pltpu.roll(block, lax.rem(SLOT + 8 - shift, SLOT + 8), 0)[:SLOT]


def store_slot(window, scalars, slot, value):
    aligned, shift = window_start(scalars, slot)
    block = jnp.concatenate([value, jnp.zeros((8, value.shape[1]), f32)], axis=0)
    block = pltpu.roll(block, shift, 0)
    rows = lax.broadcasted_iota(jnp.int32, (SLOT + 8, 1), 0)
    window[pl.ds(aligned, SLOT + 8), :] = jnp.where(
        rows >= shift, block, window[pl.ds(aligned, SLOT + 8), :]
    )


def window_rows(rows):
    return 2 * HALO + rows + 96


def pairs(x):
    hi, lo = halves(x)
    return [
        jnp.concatenate([hi[:, at : at + HEAD_DIM], lo[:, at : at + HEAD_DIM]], axis=1)
        for at in range(0, D, HEAD_DIM)
    ]


def twice(x):
    return jnp.concatenate([x, x], axis=1)


def spread(x):
    hi, lo = x[:, :HEAD_DIM], x[:, HEAD_DIM:]
    return jnp.concatenate([hi, hi, lo, lo], axis=1)


def times(hi, lo, other):
    wide = mm(hi, other, NN)
    return wide[:, :HEAD_DIM] + wide[:, HEAD_DIM:] + mm(lo, other[:, :HEAD_DIM], NN)


def times_down(other, hi, lo):
    tall = mm(other, hi, NN)
    return tall[:HEAD_DIM] + tall[HEAD_DIM:] + mm(other[:HEAD_DIM], lo, NN)


def attend_kernel(
    scalars, lower, own, upper, w, vec, q2, kt2, v2, probs_hi, probs_lo, a3, middle, window, proj, att_win
):
    rows = own.shape[0]
    fill_window(window, scalars, lower, own, upper)
    step = (2 * HALO + rows) // 3

    def project_step(t, carry):
        at = pl.multiple_of(t * step, 16)
        xhat, _ = standardized(window[pl.ds(at, step), :])
        left = triple(xhat * (1.0 + vec[0:1, :]) + vec[1:2, :])
        for part, bias in ((0, vec[2:3, :]), (1, None), (2, vec[3:4, :])):
            value = mm(left, w[part * D : (part + 1) * D, :], NT)
            proj[pl.ds(at, step), part * D : (part + 1) * D] = value if bias is None else value + bias
        return carry

    lax.fori_loop(0, 3, project_step, 0)
    proj[2 * HALO + rows :, :] = jnp.zeros((96, 3 * D), f32)

    def slot_step(slot, carry):
        qkv = load_slot(proj, scalars, slot)
        keys = jnp.minimum(L, scalars[1] - L * slot)
        keep = lax.broadcasted_iota(jnp.int32, (SLOT, SLOT), 0) < keys
        q, k, v = (pairs(qkv[:, part * D : (part + 1) * D]) for part in range(3))
        heads = []
        for h in range(HEADS):
            q2[slot, h] = q[h]
            v2[slot, h] = v[h]
            kt2[slot, h] = jnp.transpose(k[h])
            scores = mm(twice(k[h]), spread(q[h]), NT) * HEAD_DIM**-0.5
            scores = jnp.where(keep, scores, mask_fill)
            weights = jnp.exp(scores - jnp.max(scores, axis=0, keepdims=True))
            weights = weights * (1.0 / jnp.sum(weights, axis=0, keepdims=True))
            hi, lo = halves(weights)
            probs_hi[slot, h] = hi
            probs_lo[slot, h] = lo
            heads.append(times_down(jnp.transpose(v[h]), hi, lo))
        store_slot(att_win, scalars, slot, jnp.transpose(jnp.concatenate(heads, axis=0)))
        return carry

    lax.fori_loop(0, SLOTS, slot_step, 0)
    att = triple(att_win[HALO : HALO + rows, :])
    a3[...] = att
    middle[...] = own[...] + mm(att, w[3 * D :, :], NT) + vec[4:5, :]


def attend(scalars, lower, own, upper, w, vec):
    rows = own.shape[0]
    return call(
        attend_kernel,
        [
            ((SLOTS, HEADS, SLOT, 128), bf16),
            ((SLOTS, HEADS, 128, SLOT), bf16),
            ((SLOTS, HEADS, SLOT, 128), bf16),
            ((SLOTS, HEADS, SLOT, SLOT), bf16),
            ((SLOTS, HEADS, SLOT, SLOT), bf16),
            ((rows, 3 * D), bf16),
            ((rows, D), f32),
        ],
        [
            ((window_rows(rows), D), f32),
            ((window_rows(rows), 3 * D), f32),
            ((window_rows(rows), D), f32),
        ],
        flops=10**8,
        data=1 << 18,
    )(scalars, lower, own, upper, w, vec)


def mlp_kernel(scalars, mid, cot, w, vec, bias, out, slope, n3, m3, *rest):
    parts, (total, h_hi, h_lo) = rest[:-3], rest[-3:]
    if len(parts) == 1:
        total = parts[0]
    rows = mid.shape[0]
    xhat, _ = standardized(mid[...])
    n3[...] = triple(xhat * (1.0 + vec[5:6, :]) + vec[6:7, :])
    live = lax.broadcasted_iota(jnp.int32, (rows, 1), 0) < scalars[2]
    m3[...] = triple(jnp.where(live, cot[...], 0.0))

    def tile_step(t, carry):
        at = pl.multiple_of(t * TILE, TILE)
        pre = mm(n3[...], w[pl.ds(at, TILE), :], NT) + bias[0:1, pl.ds(at, TILE)]
        cdf = 0.5 + 0.5 * lax.erf(pre * (0.5**0.5))
        slope[:, pl.ds(at, TILE)] = cdf + pre * (jnp.exp(-0.5 * pre * pre) * 0.3989422804014327)
        hi, lo = halves(pre * cdf)
        h_hi[:, pl.ds(at, TILE)] = hi
        h_lo[:, pl.ds(at, TILE)] = lo
        total[pl.ds(at, TILE), :] = by_tokens(hi, lo, m3)
        return carry

    lax.fori_loop(0, FF // TILE, tile_step, 0)
    out[...] = mid[...] + by_rows(h_hi[...], h_lo[...], w[FF:, :]) + vec[7:8, :]
    scatter_parts(scalars, total, parts, quarter_rows)


def mlp(scalars, parts, mid, cot, w, vec, bias):
    rows = mid.shape[0]
    outs, scratch = part_outs(parts, FF)
    return call(
        mlp_kernel,
        [((rows, D), f32), ((rows, FF), f32)] + [((rows, 3 * D), bf16)] * 2 + outs,
        [scratch] + [((rows, FF), bf16)] * 2,
        flops=10**8,
        data=1 << 18,
    )(scalars, mid, cot, w, vec, bias)


def mlp_back_kernel(scalars, mid, cot, w, vec, slope, n3, m3, dmid, dvec, *rest):
    parts, (total, d_hi, d_lo, dbias) = rest[:-4], rest[-4:]
    if len(parts) == 1:
        total = parts[0]
    rows = mid.shape[0]

    def tile_step(t, carry):
        at = pl.multiple_of(t * TILE, TILE)
        d_pre = mm(m3[...], w[pl.ds(FF + at, TILE), :], NT) * slope[:, pl.ds(at, TILE)]
        dbias[0:1, pl.ds(at, TILE)] = row_sum(d_pre)
        hi, lo = halves(d_pre)
        d_hi[:, pl.ds(at, TILE)] = hi
        d_lo[:, pl.ds(at, TILE)] = lo
        total[pl.ds(at, TILE), :] = by_tokens(hi, lo, n3)
        return carry

    lax.fori_loop(0, FF // TILE, tile_step, 0)
    scatter_parts(scalars, total, parts, quarter_rows)
    d_norm = by_rows(d_hi[...], d_lo[...], w[:FF, :])
    xhat, rstd = standardized(mid[...])
    live = lax.broadcasted_iota(jnp.int32, (rows, 1), 0) < scalars[2]
    masked = jnp.where(live, cot[...], 0.0)
    d_middle = masked + norm_back(d_norm, xhat, rstd, vec[5:6, :])
    dmid[...] = d_middle
    zero = jnp.zeros((4, D), f32)
    dvec[...] = jnp.concatenate(
        [zero, row_sum(d_middle), row_sum(d_norm * xhat), row_sum(d_norm), row_sum(masked)]
        + [dbias[0:1, i * D : (i + 1) * D] for i in range(4)]
        + [zero],
        axis=0,
    )


def mlp_back(scalars, parts, mid, cot, w, vec, slope, n3, m3):
    rows = mid.shape[0]
    outs, scratch = part_outs(parts, FF)
    return call(
        mlp_back_kernel,
        [((rows, D), f32), ((16, D), f32)] + outs,
        [scratch] + [((rows, FF), bf16)] * 2 + [((8, FF), f32)],
        flops=10**8,
        data=1 << 18,
    )(scalars, mid, cot, w, vec, slope, n3, m3)


def place(scalars, i, j, k):
    owner = 2 * lax.bitwise_xor(scalars[4], k) + lax.bitwise_xor(scalars[5], i)
    return owner, lax.bitwise_xor(scalars[3], j)


def first_rows(owner, quarter, piece):
    return pl.multiple_of(
        jnp.where(quarter < 3, owner * 3 * piece + quarter * piece, 3 * D + owner * piece), piece
    )


def second_rows(owner, quarter, piece):
    half = piece // 2
    at = owner * 4 * half + quarter * half
    return pl.multiple_of(at, half), pl.multiple_of(FF + at, half)


def quarter_rows(owner, quarter, piece):
    return pl.multiple_of(owner * 4 * piece + quarter * piece, piece)


def part_outs(parts, rows):
    if parts is None:
        return [((rows, D), f32)], ((8, D), f32)
    return [(parts, f32)] * 4 + [((4, *parts), f32)], ((rows, D), f32)


def scatter_parts(scalars, total, outs, rows_of):
    if len(outs) == 1:
        return
    chips, piece, _ = outs[0].shape
    for n in range(8):
        for k in range(chips):
            owner, quarter = place(scalars, n // 4, n % 4, k)
            rows = total[pl.ds(rows_of(owner, quarter, piece), piece), :]
            if n < 4:
                outs[n][k] = rows
            else:
                outs[4][n - 4, k] = rows


def attend_back_kernel(first_slot, scalars, lower, own, upper, w, q2, kt2, v2, probs_hi, probs_lo, out, window):
    rows = own.shape[0]
    fill_window(window, scalars, lower, own, upper)

    def slot_step(step, carry):
        slot = first_slot + step
        row = lax.broadcasted_iota(jnp.int32, (SLOT, 1), 0)
        at_own = row + L * slot - scalars[0]
        mine = (at_own >= 0) & (at_own < rows) & (row < L)
        d_mid = jnp.where(row < L, load_slot(window, scalars, slot), 0.0)
        d_out = pairs(by_rows(*halves(d_mid), w[3 * D :, :]))
        d_q, d_k, d_v = [], [], []
        for h in range(HEADS):
            hi, lo = probs_hi[slot, h], probs_lo[slot, h]
            weights = hi.astype(f32) + lo.astype(f32)
            d_weights = mm(twice(v2[slot, h]), spread(d_out[h]), NT)
            mean = jnp.sum(weights * d_weights, axis=0, keepdims=True)
            s_hi, s_lo = halves(weights * (d_weights - mean) * HEAD_DIM**-0.5)
            d_v.append(times(hi, lo, d_out[h]))
            d_k.append(times(s_hi, s_lo, q2[slot, h]))
            d_q.append(times_down(kt2[slot, h], s_hi, s_lo))
        d_q = jnp.transpose(jnp.concatenate(d_q, axis=0))
        d_proj = jnp.concatenate([d_q] + d_k + d_v, axis=1)
        out[step] = jnp.where(mine, d_proj, 0.0)
        return carry

    lax.fori_loop(0, out.shape[0], slot_step, 0)


def attend_back(scalars, first_slot, slots, around, w, *saved):
    rows = around[1].shape[0]
    return call(
        functools.partial(attend_back_kernel, first_slot),
        [((slots, SLOT, 3 * D), f32)],
        [((window_rows(rows), D), f32)],
        flops=10**8,
        data=1 << 18,
    )(scalars, *around, w, *saved)[0]


def attend_grads_kernel(scalars, some, more, tokens, d_mid, vec, a3, *rest):
    outs, (d_hi, d_lo, sums), (total, window) = rest[:-5], rest[-5:-2], rest[-2:]
    if len(outs) == 1:
        total = outs[0]
    rows = tokens.shape[0]
    for i, part in enumerate((some, more)):

        def slot_step(step, carry, i=i, part=part):
            store_slot(window, scalars, i * part.shape[0] + step, part[step])
            return carry

        lax.fori_loop(0, part.shape[0], slot_step, 0)
    xhat, _ = standardized(tokens[...])
    n3 = triple(xhat * (1.0 + vec[0:1, :]) + vec[1:2, :])

    def part_step(part, carry):
        at = pl.ds(pl.multiple_of(part * D, D), D)
        d_proj = window[HALO : HALO + rows, at]
        hi, lo = halves(d_proj)
        d_hi[:, at] = hi
        d_lo[:, at] = lo
        total[at, :] = by_tokens(hi, lo, n3)
        sums[part] = jnp.broadcast_to(row_sum(d_proj), (8, D))
        return carry

    lax.fori_loop(0, 3, part_step, 0)
    total[3 * D :, :] = by_tokens(*halves(d_mid[...]), a3)
    scatter_parts(scalars, total, outs, first_rows)


def attend_grads(scalars, parts, some, more, tokens, d_mid, vec, a3):
    rows = tokens.shape[0]
    outs, scratch = part_outs(parts, 4 * D)
    return call(
        attend_grads_kernel,
        outs + [((rows, 3 * D), bf16)] * 2 + [((3, 8, D), f32)],
        [scratch, ((window_rows(rows), 3 * D), f32)],
        flops=10**8,
        data=1 << 18,
    )(scalars, some, more, tokens, d_mid, vec, a3)


def token_grads_kernel(scalars, d_hi, d_lo, w, tokens, d_mid, vec, sums, dvec_in, dtok, dvec):
    xhat, rstd = standardized(tokens[...])
    d_norm = by_rows(d_hi[...], d_lo[...], w[: 3 * D, :])
    dtok[...] = d_mid[...] + norm_back(d_norm, xhat, rstd, vec[0:1, :])
    new = [row_sum(d_norm * xhat), row_sum(d_norm), sums[0, 0:1], sums[2, 0:1], jnp.zeros((12, D), f32)]
    dvec[...] = dvec_in[...] + jnp.concatenate(new, axis=0)


def token_grads(scalars, *arrays):
    rows = arrays[0].shape[0]
    return call(
        token_grads_kernel, [((rows, D), f32), ((16, D), f32)], flops=10**8, data=1 << 18
    )(scalars, *arrays)


def store_split(w, at, x):
    hi, lo = halves(x)
    w[pl.ds(at, x.shape[0]), :] = jnp.concatenate([hi, lo, hi], axis=1)


def unpack_kernel(rows_of, chips, piece, step, scalars, *refs):
    mine, other, rest = refs[:4], refs[4:8], refs[8:]
    if step:
        vectors, (w, vec, bias) = rest[:2], rest[2:]
    else:
        (w,) = rest
    for i, parts in enumerate((mine, other)):
        for j in range(4):
            for k in range(chips):
                owner, quarter = place(scalars, i, j, k)
                at = rows_of(owner, quarter, piece)
                at = at if isinstance(at, tuple) else (at,)
                share = piece // len(at)
                for n, to in enumerate(at):
                    base = k * piece + n * share
                    store_split(w, to, parts[j][base : base + share, :])
    if step:
        width = D // (2 * chips)
        lane = lax.broadcasted_iota(jnp.int32, (step, D), 1)
        sums = [jnp.zeros((step, D), f32), jnp.zeros((step, D), f32)]
        for i, parts in enumerate(vectors):
            for k in range(chips):
                owner, _ = place(scalars, i, 0, k)
                block = parts[k * step : (k + 1) * step, :]
                for n in range(2):
                    mine_only = jnp.where((lane >= n * width) & (lane < (n + 1) * width), block, 0.0)
                    shift = lax.rem((owner - n) * width + D, D)
                    sums[n] = sums[n] + pltpu.roll(mine_only, shift, 1)
        vec[:step, :] = sums[0]
        vec[step:, :] = sums[1]
        bias[...] = jnp.concatenate([sums[1][s : s + 1, :] for s in range(4)], axis=1)


def unpack(scalars, chips, mine, other, rows_of, *vectors):
    total = 8 * mine[0].shape[0]
    outs = [((total, 3 * D), bf16)]
    if vectors:
        outs += [((16, D), f32), ((1, FF), f32)]
    return call(
        functools.partial(
            unpack_kernel,
            rows_of,
            chips,
            mine[0].shape[0] // chips,
            vectors[0].shape[0] // chips if vectors else 0,
        ),
        outs,
        [],
        flops=10**8,
        data=1 << 18,
    )(scalars, *mine, *other, *vectors)


def own_gradients_kernel(scalars, mine, *refs):
    others, (mom, own, keep, send, total) = refs[:3], refs[3:]
    piece = mine.shape[0] // 3
    replica = scalars[3]
    start = jnp.where(replica == 0, 4, jnp.where(replica == 2, 8, 0)) * piece
    at = pl.multiple_of(jnp.where(replica == 0, 1, jnp.where(replica == 2, 2, 0)) * piece, piece)
    own[...] = muon_momentum * mom[pl.ds(pl.multiple_of(start, piece), 4 * piece), :]
    for j, part in enumerate((mine, *others)):
        quarter = lax.bitwise_xor(replica, j)
        rows = pl.ds(pl.multiple_of(quarter * piece, piece), piece)
        own[rows, :] = own[rows, :] + (part[pl.ds(at, piece), :] if j == 0 else part[...])
    row = lax.broadcasted_iota(jnp.int32, (4 * piece, 1), 0)
    drop = ((replica == 1) & (row >= 3 * piece)) | ((replica == 3) & (row < 3 * piece))
    block = jnp.where(drop, 0.0, own[...])
    own[...] = block
    gram = fdot(block, block, TN, precise)
    for n, (row, column) in enumerate(UPPER):
        total[n * 128 : (n + 1) * 128, :] = gram[
            row * 128 : (row + 1) * 128, column * 128 : (column + 1) * 128
        ]
    chips, share, _ = keep.shape
    for i, out in enumerate((keep, send)):
        for k in range(chips):
            at = lax.bitwise_xor(scalars[5], i) * chips + lax.bitwise_xor(scalars[4], k)
            out[k] = total[pl.ds(pl.multiple_of(at * share, share), share), :]


def own_gradients(scalars, mine, others, mom, chips):
    share = 128 * len(UPPER) // (2 * chips)
    return call(
        own_gradients_kernel,
        [((mom.shape[0] // 3, D), f32)] + [((chips, share, 128), f32)] * 2,
        [((128 * len(UPPER), 128), f32)],
        flops=10**8,
        data=1 << 18,
    )(scalars, mine, *others, mom)


def all_gradients_kernel(scalars, *refs):
    parts, (mom, grads, new_mom) = refs[:4], refs[4:]
    piece = mom.shape[0] // 12
    for j in range(4):
        quarter = lax.bitwise_xor(scalars[3], j)
        for n in range(3):
            rows = pl.ds(pl.multiple_of((4 * n + quarter) * piece, piece), piece)
            grads[rows, :] = parts[j][n * piece : (n + 1) * piece, :]
    new_mom[...] = muon_momentum * mom[...] + grads[...]


def all_gradients(scalars, parts, mom):
    return call(all_gradients_kernel, [(mom.shape, f32)] * 2, flops=10**8, data=1 << 18)(
        scalars, *parts, mom
    )


def pieces(x):
    hi, mid = halves(x)
    return hi, mid, (x - hi.astype(f32) - mid.astype(f32)).astype(bf16)


def full_product(a, b):
    (ah, am, al), (bh, bm, bl) = a, b
    return mm(
        jnp.concatenate([ah, ah, am, ah, al, am], axis=1),
        jnp.concatenate([bh, bm, bh, bl, bh, bm], axis=0),
        NN,
    )


def three_product(a, b):
    (ah, am, _), (bh, bm, _) = a, b
    return mm(
        jnp.concatenate([ah, am, ah], axis=1), jnp.concatenate([bh, bh, bm], axis=0), NN
    )


def identity():
    row = lax.broadcasted_iota(jnp.int32, (D, D), 0)
    return jnp.where(row == lax.broadcasted_iota(jnp.int32, (D, D), 1), 1.0, 0.0)


def polynomial(gram, product):
    g = pieces(gram)
    return g, ns_coeffs[1] * gram + ns_coeffs[2] * product(g, g) + ns_coeffs[0] * identity()


def polar_step(gram, block):
    g, poly = polynomial(gram, full_product)
    p = pieces(poly)
    return full_product(p, pieces(full_product(p, g))), three_product(pieces(block), p)


def polar_end(gram, block):
    return three_product(pieces(block), pieces(polynomial(gram, three_product)[1]))


def polar_start(gram, block):
    scale = 1.0 / (jnp.sqrt(jnp.sum(gram * identity())) + ns_eps)
    return gram * (scale * scale), block * scale


def polar(gram, block):
    gram, block = polar_start(gram, block)
    for step_index in range(NS_STEPS):
        square = fdot(gram, gram, NN, precise)
        poly = ns_coeffs[1] * gram + ns_coeffs[2] * square + ns_coeffs[0] * identity()
        if step_index + 1 < NS_STEPS:
            gram = fdot(poly, fdot(poly, gram, NN, precise), NN, precise)
        block = fdot(block, poly, NN, precise)
    return block


def update_kernel(scalars, mine, other, own, out, total, gram, block):
    chips, share, _ = mine.shape
    for i, parts in enumerate((mine, other)):
        for k in range(chips):
            at = lax.bitwise_xor(scalars[5], i) * chips + lax.bitwise_xor(scalars[4], k)
            total[pl.ds(pl.multiple_of(at * share, share), share), :] = parts[k]
    blocks = {}
    for n, (row, column) in enumerate(UPPER):
        blocks[row, column] = total[n * 128 : (n + 1) * 128, :]
        if row != column:
            blocks[column, row] = jnp.transpose(blocks[row, column])
    gram[...], block[...] = polar_start(
        jnp.concatenate(
            [jnp.concatenate([blocks[row, column] for column in range(3)], axis=1) for row in range(3)],
            axis=0,
        ),
        own[...],
    )

    def step(_, carry):
        gram[...], block[...] = polar_step(gram[...], block[...])
        return carry

    lax.fori_loop(0, NS_STEPS - 1, step, 0)
    replica = scalars[3]
    rate = jnp.where(replica == 1, 3.0**0.5, jnp.where(replica == 0, (FF / D) ** 0.5, 1.0))
    out[...] = polar_end(gram[...], block[...]) * (-muon_rate * rate)


def update(scalars, mine, other, own):
    return call(
        update_kernel,
        [(own.shape, f32)],
        [((128 * len(UPPER), 128), f32), ((D, D), f32), (own.shape, f32)],
        flops=10**8, data=1 << 18
    )(scalars, mine, other, own)[0]


def first_message_kernel(replica, qkv, out, vectors, message):
    piece = message.shape[0] - 8
    width = vectors.shape[1]

    @pl.when(replica[0] < 3)
    def _():
        message[:piece, :] = qkv[pl.ds(pl.multiple_of(replica[0] * piece, 8), piece), :]

    @pl.when(replica[0] == 3)
    def _():
        message[:piece, :] = out[...]

    message[piece:, :] = jnp.zeros((8, D), f32)
    message[piece:, :width] = vectors[:8, :]
    message[piece : piece + 4, width : 2 * width] = vectors[8:, :]


def first_message(replica, qkv, out, vectors):
    return call(
        first_message_kernel, [((out.shape[0] + 8, D), f32)], flops=10**6, data=1 << 16
    )(replica, qkv, out, vectors)[0]


def hand_out_kernel(scalars, one, two, three, four, *outs):
    for owner, out in zip((1, 3, 0, 2), outs):
        at = lax.bitwise_xor(scalars[3], owner)
        rows = out.shape[0]
        for j, part in enumerate((one, two, three, four)):
            base = part.shape[0] - rows if owner == 3 else 0

            @pl.when(at == j)
            def _(part=part, out=out, base=base, rows=rows):
                out[...] = part[base : base + rows, :]


def hand_out(scalars, parts, cuts):
    outs = [((rows, D), f32) for rows in cuts]
    one, two, three, four = call(hand_out_kernel, outs, flops=10**8, data=1 << 18)(
        scalars, *parts
    )
    return one.T, two.T, three.T, four


def local(
    tokens,
    image_count,
    w_qkv,
    w_out,
    w_up,
    w_down,
    vectors,
    cotangent,
    mom_qkv,
    mom_out,
    mom_up,
    mom_down,
    mom_vectors,
):
    group_size = lax.axis_size("group")
    replicas = lax.axis_size("replica")
    group_index = lax.axis_index("group")
    replica_index = lax.axis_index("replica")
    chips = group_size // 2
    tok_rows = tokens.shape[0]
    slab_rows = group_size * tok_rows
    image_total = lax.dynamic_index_in_dim(image_count, replica_index, 0, keepdims=False)
    first_slot = group_index * tok_rows
    first_image = first_slot // L
    scalars = jnp.stack(
        [
            first_slot - first_image * L,
            slab_rows - first_image * L,
            image_total * L - first_slot,
            replica_index,
            group_index // 2,
            group_index % 2,
        ]
    ).astype(jnp.int32)

    def swap(x):
        return lax.ppermute(x, "group", [(i, i ^ 1) for i in range(group_size)])

    def hop(x, by):
        return lax.ppermute(x, "group", [(i, i ^ (2 * by)) for i in range(group_size)])

    def cross(x, by):
        return lax.ppermute(x, "replica", [(i, i ^ by) for i in range(replicas)])

    def halo(x):
        head, tail = x[:HALO], x[tok_rows - HALO :]
        even = group_index % 2 == 0
        pairs = [(i, i + 1) for i in range(1, group_size - 1, 2)]
        inside = swap(jnp.where(even, tail, head))
        outside = lax.ppermute(
            jnp.where(even, head, tail), "group", pairs + [(j, i) for i, j in pairs]
        )
        return inside, x, outside

    def along_chips(x):
        return jnp.stack([x] + [hop(x, k) for k in range(1, chips)])

    width = D // group_size
    piece = 4 * width // replicas
    cuts = (3 * width, width, 4 * width, 4 * width)
    first_stack = jnp.concatenate([w_qkv.T, w_out.T], axis=0)
    second_stack = jnp.concatenate([w_up.T, w_down], axis=0)
    mom_stack = jnp.concatenate([mom_qkv.T, mom_out.T, mom_up.T, mom_down], axis=0)
    around = halo(tokens)

    def split(stack):
        one, two, three, four = (stack[sum(cuts[:i]) : sum(cuts[: i + 1])] for i in range(4))
        return one.T, two.T, three.T, four

    def finish(block_out, grad_tokens, grads, new_mom, dvec, updates):
        grad_vectors = lax.dynamic_slice_in_dim(dvec[:12], group_index * width, width, 1)
        new_vectors = vector_momentum * mom_vectors + grad_vectors
        return (
            block_out,
            grad_tokens,
            *split(grads),
            grad_vectors,
            *split(new_mom),
            new_vectors,
            *updates,
            -vector_rate * new_vectors,
        )

    if replicas != 4 or piece % 16:
        def rows_of(stack, inner):
            parts = lax.all_gather(stack, "group")
            rows = jnp.concatenate(
                [parts[:, :inner].reshape(-1, D), parts[:, inner:].reshape(-1, D)], axis=0
            )
            hi = lax.reduce_precision(rows, 8, 7)
            lo = lax.reduce_precision(rows - hi, 8, 7)
            return jnp.concatenate([hi, lo, hi], axis=1).astype(bf16)

        def shares_of(total, cut, inner):
            one, two = total[:cut], total[cut:]
            parts = jnp.concatenate(
                [one.reshape(group_size, inner, D), two.reshape(group_size, -1, D)], axis=1
            )
            return lax.psum_scatter(parts, "group", scatter_dimension=0)

        w_one, w_two = rows_of(first_stack, 3 * width), rows_of(second_stack, 4 * width)
        vec = jnp.pad(lax.all_gather(vectors, "group", axis=1, tiled=True), ((0, 4), (0, 0)))
        *saved, a3, middle = attend(scalars, *around, w_one, vec)
        block_out, slope, n3, m3, down = mlp(
            scalars, None, middle, cotangent, w_two, vec, vec[8:12].reshape(1, FF)
        )
        d_middle, dvec, up = mlp_back(
            scalars, None, middle, cotangent, w_two, vec, slope, n3, m3
        )
        second = jnp.concatenate([up, down], axis=0)
        d_around = halo(d_middle)
        some, more = (attend_back(scalars, i, 2, d_around, w_one, *saved) for i in (0, 2))
        first, d_hi, d_lo, sums = attend_grads(
            scalars, None, some, more, tokens, d_middle, vec, a3
        )
        grad_tokens, dvec = token_grads(
            scalars, d_hi, d_lo, w_one, tokens, d_middle, vec, sums, dvec
        )
        grads, dvec = lax.psum(
            (
                jnp.concatenate(
                    [shares_of(first, 3 * D, 3 * width), shares_of(second, FF, 4 * width)], axis=0
                ),
                lax.psum(dvec, "group"),
            ),
            "replica",
        )
        new_mom = muon_momentum * mom_stack + grads
        blocks = [new_mom[sum(cuts[:i]) : sum(cuts[: i + 1])] for i in range(4)]
        grams = lax.psum(jnp.stack([fdot(x, x, TN, precise) for x in blocks]), "group")
        updates = [
            polar(grams[i], x) * (-muon_rate * rate)
            for i, (x, rate) in enumerate(zip(blocks, (3.0**0.5, 1.0, (FF / D) ** 0.5, 1.0)))
        ]
        updates = [x if i == 3 else x.T for i, x in enumerate(updates)]
        return finish(block_out, grad_tokens, grads, new_mom, dvec, updates)

    def second_quarter(quarter):
        return jnp.concatenate(
            [
                lax.dynamic_slice_in_dim(second_stack, (4 * n + quarter) * piece, piece, 0)
                for n in range(2)
            ],
            axis=0,
        )

    my_second = second_quarter(replica_index)
    diagonal = second_quarter(lax.bitwise_xor(replica_index, 3))
    others = range(1, replicas)
    start = first_message(replica_index.astype(jnp.int32).reshape(1), w_qkv.T, w_out.T, vectors)
    start = [start] + [hop(start, k) for k in range(1, chips)]
    first = jnp.concatenate([x[:piece] for x in start], axis=0)
    vec_parts = jnp.concatenate([x[piece:] for x in start], axis=0)
    first, vec_parts, scalars, lower, upper = lax.optimization_barrier(
        (first, vec_parts, scalars, around[0], around[2])
    )
    around = lower, tokens, upper
    first_other, vec_other = [swap(first)], swap(vec_parts)
    first = [first] + [cross(first, j) for j in others]
    first_other[0], vec_other, my_second = lax.optimization_barrier(
        (first_other[0], vec_other, my_second)
    )
    second = [my_second] + [hop(my_second, k) for k in range(1, chips)]
    first[1:], second = lax.optimization_barrier((first[1:], second))
    second = jnp.concatenate(second, axis=0)
    first_other += [swap(first[j]) for j in others]
    diagonal, second, first_other = lax.optimization_barrier((diagonal, second, first_other))
    diagonal = [diagonal] + [hop(diagonal, k) for k in range(1, chips)]
    second = [second, cross(second, 1), cross(second, 2)]
    w_one, vec, bias = unpack(
        scalars, chips, first, first_other, first_rows, vec_parts, vec_other
    )
    *saved, a3, middle = attend(scalars, *around, w_one, vec)
    second[1:], diagonal, middle = lax.optimization_barrier((second[1:], diagonal, middle))
    second.append(jnp.concatenate(diagonal, axis=0))
    second_other = [swap(x) for x in second]
    w_two = unpack(scalars, chips, second, second_other, second_rows)[0]
    shape = (chips, piece, D)

    def join(keep, other):
        return [x + other[j] for j, x in enumerate(keep)]

    def exchange(parts):
        return [parts[0]] + [cross(parts[j], j) for j in others]

    block_out, slope, n3, m3, *keep, send = mlp(
        scalars, shape, middle, cotangent, w_two, vec, bias
    )
    other = swap(send)
    down_keep = keep
    d_middle, dvec, *keep, send = mlp_back(
        scalars, shape, middle, cotangent, w_two, vec, slope, n3, m3
    )
    down, d_middle, send = lax.optimization_barrier((join(down_keep, other), d_middle, send))
    d_around = halo(d_middle)
    other = swap(send)
    down = exchange(down)
    some = attend_back(scalars, 0, 2, d_around, w_one, *saved)
    up, some, d_around = lax.optimization_barrier((join(keep, other), some, d_around))
    up = exchange(up)
    more = attend_back(scalars, 2, 2, d_around, w_one, *saved)
    *keep, send, d_hi, d_lo, sums = attend_grads(
        scalars, shape, some, more, tokens, d_middle, vec, a3
    )
    grad_tokens, dvec = token_grads(scalars, d_hi, d_lo, w_one, tokens, d_middle, vec, sums, dvec)
    keep, send, dvec, up, down = lax.optimization_barrier((keep, send, dvec, up, down))
    other, dvec = swap(send), dvec + swap(dvec)
    first, dvec, up, down = lax.optimization_barrier((join(keep, other), dvec, up, down))
    first = exchange(first)

    def over_chips(messages):
        return sum((hop(messages[k], k) for k in range(1, len(messages))), messages[0])

    def rows_for(parts, k):
        return sum((x[k] for x in parts[1:]), parts[0][k])

    second_sum = over_chips(
        [jnp.concatenate([rows_for(up, k), rows_for(down, k), dvec], axis=0) for k in range(chips)]
    )
    up_sum, down_sum, dvec = (
        second_sum[:piece], second_sum[piece : 2 * piece], second_sum[2 * piece :]
    )
    first_sum = over_chips([rows_for(first, k) for k in range(chips)])

    def for_replica(replica):
        return jnp.where(replica == 0, up_sum, jnp.where(replica == 2, down_sum, first_sum))

    mine = jnp.concatenate([first_sum, up_sum, down_sum], axis=0)
    taken = [cross(for_replica(lax.bitwise_xor(replica_index, j)), j) for j in others]
    own, keep, send = own_gradients(scalars, mine, taken, mom_stack, chips)
    t = keep + swap(send)
    t = t[0] + sum(hop(t[k], k) for k in range(1, chips))
    gram = along_chips(t)
    update_own = update(scalars, gram, swap(gram), own)
    mine = jnp.concatenate([mine, dvec], axis=0)
    parts = [mine] + [cross(mine, j) for j in others]
    parts, update_own = lax.optimization_barrier((parts, update_own))
    updates = [update_own] + [cross(update_own, j) for j in others]
    dvec = sum((x[3 * piece :] for x in parts[1:]), parts[0][3 * piece :])
    grads, new_mom = all_gradients(scalars, parts, mom_stack)
    updates = hand_out(scalars, updates, cuts)
    return finish(block_out, grad_tokens, grads, new_mom, dvec, updates)


def solution(mesh):
    tokens, whole, columns, rows = P(("replica", "group"), None), P(), P(None, "group"), P("group", None)
    params = (columns, columns, columns, rows, columns)
    return jax.shard_map(
        local,
        mesh=mesh,
        in_specs=(tokens, whole, *params, tokens, *params),
        out_specs=(tokens, tokens, *params, *params, *params),
        check_vma=False,
    )
```

```python
import functools

import jax
import jax.numpy as jnp
from jax import lax
from jax.experimental import pallas as pl
from jax.experimental.pallas import tpu as pltpu
from jax.sharding import PartitionSpec as P

D = 384
HEADS = 6
HEAD_DIM = 64
FF = 1536
L = 197
NS_STEPS = 5
SLOTS = 4
SLOT = 208
HALO = 200
TILE = 512

f32, bf16 = jnp.float32, jnp.bfloat16
high = lax.Precision.HIGH
precise = lax.Precision.HIGHEST
ns_coeffs = (3.4445, -4.775, 2.0315)
norm_eps = 1e-06
ns_eps = 1e-07
muon_momentum = 0.95
vector_momentum = 0.9
muon_rate = 0.5
vector_rate = 0.001
mask_fill = -1e30

UPPER = ((0, 0), (0, 1), (0, 2), (1, 1), (1, 2), (2, 2))
NN = (((1,), (0,)), ((), ()))
NT = (((1,), (1,)), ((), ()))
TN = (((0,), (0,)), ((), ()))
VMEM = pl.BlockSpec(memory_space=pltpu.VMEM)
SMEM = pl.BlockSpec(memory_space=pltpu.SMEM)


def call(body, outs, scratch=(), flops=0, data=0):
    def run(scalars, *arrays):
        return pl.pallas_call(
            body,
            out_shape=[jax.ShapeDtypeStruct(s, t) for s, t in outs],
            in_specs=[SMEM] + [VMEM] * len(arrays),
            out_specs=[VMEM] * len(outs),
            scratch_shapes=[pltpu.VMEM(s, t) for s, t in scratch],
            compiler_params=pltpu.CompilerParams(vmem_limit_bytes=28 << 20),
            cost_estimate=pl.CostEstimate(flops=flops, bytes_accessed=data, transcendentals=0),
        )(scalars, *arrays)

    return run


def mm(a, b, dims):
    return lax.dot_general(a, b, dims, preferred_element_type=f32)


def fdot(a, b, dims, precision=high):
    return lax.dot_general(a, b, dims, precision=precision, preferred_element_type=f32)


def halves(x):
    hi = x.astype(bf16)
    return hi, (x - hi.astype(f32)).astype(bf16)


def triple(x):
    hi, lo = halves(x)
    return jnp.concatenate([hi, hi, lo], axis=1)


def by_rows(hi, lo, both):
    wide = mm(hi, both[:, : 2 * D], NN)
    return wide[:, :D] + wide[:, D:] + mm(lo, both[:, :D], NN)


def by_tokens(hi, lo, other):
    wide = mm(hi, other[:, D:], TN)
    return wide[:, :D] + wide[:, D:] + mm(lo, other[:, :D], TN)


def standardized(x):
    centered = x - jnp.mean(x, axis=-1, keepdims=True)
    rstd = lax.rsqrt(jnp.mean(centered * centered, axis=-1, keepdims=True) + norm_eps)
    return centered * rstd, rstd


def norm_back(d_norm, xhat, rstd, scale):
    g = d_norm * (1.0 + scale)
    return rstd * (
        g - jnp.mean(g, axis=-1, keepdims=True) - xhat * jnp.mean(g * xhat, axis=-1, keepdims=True)
    )


def row_sum(x):
    return jnp.sum(x, axis=0, keepdims=True)


def window_start(scalars, slot):
    start = HALO - scalars[0] + L * slot
    aligned = pl.multiple_of((start // 8) * 8, 8)
    return aligned, start - aligned


def fill_window(window, scalars, inside, own, outside):
    rows = own.shape[0]
    even = scalars[5] == 0
    window[:HALO, :] = jnp.where(even, outside[...], inside[...])
    window[HALO : HALO + rows, :] = own[...]
    window[HALO + rows : 2 * HALO + rows, :] = jnp.where(even, inside[...], outside[...])
    window[2 * HALO + rows :, :] = jnp.zeros((window.shape[0] - 2 * HALO - rows, D), f32)


def load_slot(window, scalars, slot):
    aligned, shift = window_start(scalars, slot)
    block = window[pl.ds(aligned, SLOT + 8), :]
    return pltpu.roll(block, lax.rem(SLOT + 8 - shift, SLOT + 8), 0)[:SLOT]


def store_slot(window, scalars, slot, value):
    aligned, shift = window_start(scalars, slot)
    block = jnp.concatenate([value, jnp.zeros((8, value.shape[1]), f32)], axis=0)
    block = pltpu.roll(block, shift, 0)
    rows = lax.broadcasted_iota(jnp.int32, (SLOT + 8, 1), 0)
    window[pl.ds(aligned, SLOT + 8), :] = jnp.where(
        rows >= shift, block, window[pl.ds(aligned, SLOT + 8), :]
    )


def window_rows(rows):
    return 2 * HALO + rows + 96


def pairs(x):
    hi, lo = halves(x)
    return [
        jnp.concatenate([hi[:, at : at + HEAD_DIM], lo[:, at : at + HEAD_DIM]], axis=1)
        for at in range(0, D, HEAD_DIM)
    ]


def twice(x):
    return jnp.concatenate([x, x], axis=1)


def spread(x):
    hi, lo = x[:, :HEAD_DIM], x[:, HEAD_DIM:]
    return jnp.concatenate([hi, hi, lo, lo], axis=1)


def times(hi, lo, other):
    wide = mm(hi, other, NN)
    return wide[:, :HEAD_DIM] + wide[:, HEAD_DIM:] + mm(lo, other[:, :HEAD_DIM], NN)


def times_down(other, hi, lo):
    tall = mm(other, hi, NN)
    return tall[:HEAD_DIM] + tall[HEAD_DIM:] + mm(other[:HEAD_DIM], lo, NN)


def attend_kernel(
    scalars, lower, own, upper, w, vec, q2, kt2, v2, probs_hi, probs_lo, a3, middle, window, proj, att_win
):
    rows = own.shape[0]
    fill_window(window, scalars, lower, own, upper)
    step = (2 * HALO + rows) // 3

    def project_step(t, carry):
        at = pl.multiple_of(t * step, 16)
        xhat, _ = standardized(window[pl.ds(at, step), :])
        left = triple(xhat * (1.0 + vec[0:1, :]) + vec[1:2, :])
        for part, bias in ((0, vec[2:3, :]), (1, None), (2, vec[3:4, :])):
            value = mm(left, w[part * D : (part + 1) * D, :], NT)
            proj[pl.ds(at, step), part * D : (part + 1) * D] = value if bias is None else value + bias
        return carry

    lax.fori_loop(0, 3, project_step, 0)
    proj[2 * HALO + rows :, :] = jnp.zeros((96, 3 * D), f32)

    def slot_step(slot, carry):
        qkv = load_slot(proj, scalars, slot)
        keys = jnp.minimum(L, scalars[1] - L * slot)
        keep = lax.broadcasted_iota(jnp.int32, (SLOT, SLOT), 0) < keys
        q, k, v = (pairs(qkv[:, part * D : (part + 1) * D]) for part in range(3))
        heads = []
        for h in range(HEADS):
            q2[slot, h] = q[h]
            v2[slot, h] = v[h]
            kt2[slot, h] = jnp.transpose(k[h])
            scores = mm(twice(k[h]), spread(q[h]), NT) * HEAD_DIM**-0.5
            scores = jnp.where(keep, scores, mask_fill)
            weights = jnp.exp(scores - jnp.max(scores, axis=0, keepdims=True))
            weights = weights * (1.0 / jnp.sum(weights, axis=0, keepdims=True))
            hi, lo = halves(weights)
            probs_hi[slot, h] = hi
            probs_lo[slot, h] = lo
            heads.append(times_down(jnp.transpose(v[h]), hi, lo))
        store_slot(att_win, scalars, slot, jnp.transpose(jnp.concatenate(heads, axis=0)))
        return carry

    lax.fori_loop(0, SLOTS, slot_step, 0)
    att = triple(att_win[HALO : HALO + rows, :])
    a3[...] = att
    middle[...] = own[...] + mm(att, w[3 * D :, :], NT) + vec[4:5, :]


def attend(scalars, lower, own, upper, w, vec):
    rows = own.shape[0]
    return call(
        attend_kernel,
        [
            ((SLOTS, HEADS, SLOT, 128), bf16),
            ((SLOTS, HEADS, 128, SLOT), bf16),
            ((SLOTS, HEADS, SLOT, 128), bf16),
            ((SLOTS, HEADS, SLOT, SLOT), bf16),
            ((SLOTS, HEADS, SLOT, SLOT), bf16),
            ((rows, 3 * D), bf16),
            ((rows, D), f32),
        ],
        [
            ((window_rows(rows), D), f32),
            ((window_rows(rows), 3 * D), f32),
            ((window_rows(rows), D), f32),
        ],
        flops=10**8,
        data=1 << 18,
    )(scalars, lower, own, upper, w, vec)


def mlp_kernel(scalars, mid, cot, w, vec, bias, out, slope, n3, m3, *rest):
    parts, (total, h_hi, h_lo) = rest[:-3], rest[-3:]
    if len(parts) == 1:
        total = parts[0]
    rows = mid.shape[0]
    xhat, _ = standardized(mid[...])
    n3[...] = triple(xhat * (1.0 + vec[5:6, :]) + vec[6:7, :])
    live = lax.broadcasted_iota(jnp.int32, (rows, 1), 0) < scalars[2]
    m3[...] = triple(jnp.where(live, cot[...], 0.0))

    def tile_step(t, carry):
        at = pl.multiple_of(t * TILE, TILE)
        pre = mm(n3[...], w[pl.ds(at, TILE), :], NT) + bias[0:1, pl.ds(at, TILE)]
        cdf = 0.5 + 0.5 * lax.erf(pre * (0.5**0.5))
        slope[:, pl.ds(at, TILE)] = cdf + pre * (jnp.exp(-0.5 * pre * pre) * 0.3989422804014327)
        hi, lo = halves(pre * cdf)
        h_hi[:, pl.ds(at, TILE)] = hi
        h_lo[:, pl.ds(at, TILE)] = lo
        total[pl.ds(at, TILE), :] = by_tokens(hi, lo, m3)
        return carry

    lax.fori_loop(0, FF // TILE, tile_step, 0)
    out[...] = mid[...] + by_rows(h_hi[...], h_lo[...], w[FF:, :]) + vec[7:8, :]
    scatter_parts(scalars, total, parts, quarter_rows)


def mlp(scalars, parts, mid, cot, w, vec, bias):
    rows = mid.shape[0]
    outs, scratch = part_outs(parts, FF)
    return call(
        mlp_kernel,
        [((rows, D), f32), ((rows, FF), f32)] + [((rows, 3 * D), bf16)] * 2 + outs,
        [scratch] + [((rows, FF), bf16)] * 2,
        flops=10**8,
        data=1 << 18,
    )(scalars, mid, cot, w, vec, bias)


def mlp_back_kernel(scalars, mid, cot, w, vec, slope, n3, m3, dmid, dvec, *rest):
    parts, (total, d_hi, d_lo, dbias) = rest[:-4], rest[-4:]
    if len(parts) == 1:
        total = parts[0]
    rows = mid.shape[0]

    def tile_step(t, carry):
        at = pl.multiple_of(t * TILE, TILE)
        d_pre = mm(m3[...], w[pl.ds(FF + at, TILE), :], NT) * slope[:, pl.ds(at, TILE)]
        dbias[0:1, pl.ds(at, TILE)] = row_sum(d_pre)
        hi, lo = halves(d_pre)
        d_hi[:, pl.ds(at, TILE)] = hi
        d_lo[:, pl.ds(at, TILE)] = lo
        total[pl.ds(at, TILE), :] = by_tokens(hi, lo, n3)
        return carry

    lax.fori_loop(0, FF // TILE, tile_step, 0)
    scatter_parts(scalars, total, parts, quarter_rows)
    d_norm = by_rows(d_hi[...], d_lo[...], w[:FF, :])
    xhat, rstd = standardized(mid[...])
    live = lax.broadcasted_iota(jnp.int32, (rows, 1), 0) < scalars[2]
    masked = jnp.where(live, cot[...], 0.0)
    d_middle = masked + norm_back(d_norm, xhat, rstd, vec[5:6, :])
    dmid[...] = d_middle
    zero = jnp.zeros((4, D), f32)
    dvec[...] = jnp.concatenate(
        [zero, row_sum(d_middle), row_sum(d_norm * xhat), row_sum(d_norm), row_sum(masked)]
        + [dbias[0:1, i * D : (i + 1) * D] for i in range(4)]
        + [zero],
        axis=0,
    )


def mlp_back(scalars, parts, mid, cot, w, vec, slope, n3, m3):
    rows = mid.shape[0]
    outs, scratch = part_outs(parts, FF)
    return call(
        mlp_back_kernel,
        [((rows, D), f32), ((16, D), f32)] + outs,
        [scratch] + [((rows, FF), bf16)] * 2 + [((8, FF), f32)],
        flops=10**8,
        data=1 << 18,
    )(scalars, mid, cot, w, vec, slope, n3, m3)


def place(scalars, i, j, k):
    owner = 2 * lax.bitwise_xor(scalars[4], k) + lax.bitwise_xor(scalars[5], i)
    return owner, lax.bitwise_xor(scalars[3], j)


def first_rows(owner, quarter, piece):
    return pl.multiple_of(
        jnp.where(quarter < 3, owner * 3 * piece + quarter * piece, 3 * D + owner * piece), piece
    )


def second_rows(owner, quarter, piece):
    half = piece // 2
    at = owner * 4 * half + quarter * half
    return pl.multiple_of(at, half), pl.multiple_of(FF + at, half)


def quarter_rows(owner, quarter, piece):
    return pl.multiple_of(owner * 4 * piece + quarter * piece, piece)


def part_outs(parts, rows):
    if parts is None:
        return [((rows, D), f32)], ((8, D), f32)
    return [(parts, f32)] * 4 + [((4, *parts), f32)], ((rows, D), f32)


def scatter_parts(scalars, total, outs, rows_of):
    if len(outs) == 1:
        return
    chips, piece, _ = outs[0].shape
    for n in range(8):
        for k in range(chips):
            owner, quarter = place(scalars, n // 4, n % 4, k)
            rows = total[pl.ds(rows_of(owner, quarter, piece), piece), :]
            if n < 4:
                outs[n][k] = rows
            else:
                outs[4][n - 4, k] = rows


def attend_back_kernel(first_slot, scalars, lower, own, upper, w, q2, kt2, v2, probs_hi, probs_lo, out, window):
    rows = own.shape[0]
    fill_window(window, scalars, lower, own, upper)

    def slot_step(step, carry):
        slot = first_slot + step
        row = lax.broadcasted_iota(jnp.int32, (SLOT, 1), 0)
        at_own = row + L * slot - scalars[0]
        mine = (at_own >= 0) & (at_own < rows) & (row < L)
        d_mid = jnp.where(row < L, load_slot(window, scalars, slot), 0.0)
        d_out = pairs(by_rows(*halves(d_mid), w[3 * D :, :]))
        d_q, d_k, d_v = [], [], []
        for h in range(HEADS):
            hi, lo = probs_hi[slot, h], probs_lo[slot, h]
            weights = hi.astype(f32) + lo.astype(f32)
            d_weights = mm(twice(v2[slot, h]), spread(d_out[h]), NT)
            mean = jnp.sum(weights * d_weights, axis=0, keepdims=True)
            s_hi, s_lo = halves(weights * (d_weights - mean) * HEAD_DIM**-0.5)
            d_v.append(times(hi, lo, d_out[h]))
            d_k.append(times(s_hi, s_lo, q2[slot, h]))
            d_q.append(times_down(kt2[slot, h], s_hi, s_lo))
        d_q = jnp.transpose(jnp.concatenate(d_q, axis=0))
        d_proj = jnp.concatenate([d_q] + d_k + d_v, axis=1)
        out[step] = jnp.where(mine, d_proj, 0.0)
        return carry

    lax.fori_loop(0, out.shape[0], slot_step, 0)


def attend_back(scalars, first_slot, slots, around, w, *saved):
    rows = around[1].shape[0]
    return call(
        functools.partial(attend_back_kernel, first_slot),
        [((slots, SLOT, 3 * D), f32)],
        [((window_rows(rows), D), f32)],
        flops=10**8,
        data=1 << 18,
    )(scalars, *around, w, *saved)[0]


def attend_grads_kernel(scalars, some, more, tokens, d_mid, vec, a3, *rest):
    outs, (d_hi, d_lo, sums), (total, window) = rest[:-5], rest[-5:-2], rest[-2:]
    if len(outs) == 1:
        total = outs[0]
    rows = tokens.shape[0]
    for i, part in enumerate((some, more)):

        def slot_step(step, carry, i=i, part=part):
            store_slot(window, scalars, i * part.shape[0] + step, part[step])
            return carry

        lax.fori_loop(0, part.shape[0], slot_step, 0)
    xhat, _ = standardized(tokens[...])
    n3 = triple(xhat * (1.0 + vec[0:1, :]) + vec[1:2, :])

    def part_step(part, carry):
        at = pl.ds(pl.multiple_of(part * D, D), D)
        d_proj = window[HALO : HALO + rows, at]
        hi, lo = halves(d_proj)
        d_hi[:, at] = hi
        d_lo[:, at] = lo
        total[at, :] = by_tokens(hi, lo, n3)
        sums[part] = jnp.broadcast_to(row_sum(d_proj), (8, D))
        return carry

    lax.fori_loop(0, 3, part_step, 0)
    total[3 * D :, :] = by_tokens(*halves(d_mid[...]), a3)
    scatter_parts(scalars, total, outs, first_rows)


def attend_grads(scalars, parts, some, more, tokens, d_mid, vec, a3):
    rows = tokens.shape[0]
    outs, scratch = part_outs(parts, 4 * D)
    return call(
        attend_grads_kernel,
        outs + [((rows, 3 * D), bf16)] * 2 + [((3, 8, D), f32)],
        [scratch, ((window_rows(rows), 3 * D), f32)],
        flops=10**8,
        data=1 << 18,
    )(scalars, some, more, tokens, d_mid, vec, a3)


def token_grads_kernel(scalars, d_hi, d_lo, w, tokens, d_mid, vec, sums, dvec_in, dtok, dvec):
    xhat, rstd = standardized(tokens[...])
    d_norm = by_rows(d_hi[...], d_lo[...], w[: 3 * D, :])
    dtok[...] = d_mid[...] + norm_back(d_norm, xhat, rstd, vec[0:1, :])
    new = [row_sum(d_norm * xhat), row_sum(d_norm), sums[0, 0:1], sums[2, 0:1], jnp.zeros((12, D), f32)]
    dvec[...] = dvec_in[...] + jnp.concatenate(new, axis=0)


def token_grads(scalars, *arrays):
    rows = arrays[0].shape[0]
    return call(
        token_grads_kernel, [((rows, D), f32), ((16, D), f32)], flops=10**8, data=1 << 18
    )(scalars, *arrays)


def store_split(w, at, x):
    hi, lo = halves(x)
    w[pl.ds(at, x.shape[0]), :] = jnp.concatenate([hi, lo, hi], axis=1)


def unpack_kernel(rows_of, chips, piece, step, scalars, *refs):
    mine, other, rest = refs[:4], refs[4:8], refs[8:]
    if step:
        vectors, (w, vec, bias) = rest[:2], rest[2:]
    else:
        (w,) = rest
    for i, parts in enumerate((mine, other)):
        for j in range(4):
            for k in range(chips):
                owner, quarter = place(scalars, i, j, k)
                at = rows_of(owner, quarter, piece)
                at = at if isinstance(at, tuple) else (at,)
                share = piece // len(at)
                for n, to in enumerate(at):
                    base = k * piece + n * share
                    store_split(w, to, parts[j][base : base + share, :])
    if step:
        width = D // (2 * chips)
        lane = lax.broadcasted_iota(jnp.int32, (step, D), 1)
        sums = [jnp.zeros((step, D), f32), jnp.zeros((step, D), f32)]
        for i, parts in enumerate(vectors):
            for k in range(chips):
                owner, _ = place(scalars, i, 0, k)
                block = parts[k * step : (k + 1) * step, :]
                for n in range(2):
                    mine_only = jnp.where((lane >= n * width) & (lane < (n + 1) * width), block, 0.0)
                    shift = lax.rem((owner - n) * width + D, D)
                    sums[n] = sums[n] + pltpu.roll(mine_only, shift, 1)
        vec[:step, :] = sums[0]
        vec[step:, :] = sums[1]
        bias[...] = jnp.concatenate([sums[1][s : s + 1, :] for s in range(4)], axis=1)


def unpack(scalars, chips, mine, other, rows_of, *vectors):
    total = 8 * mine[0].shape[0]
    outs = [((total, 3 * D), bf16)]
    if vectors:
        outs += [((16, D), f32), ((1, FF), f32)]
    return call(
        functools.partial(
            unpack_kernel,
            rows_of,
            chips,
            mine[0].shape[0] // chips,
            vectors[0].shape[0] // chips if vectors else 0,
        ),
        outs,
        [],
        flops=10**8,
        data=1 << 18,
    )(scalars, *mine, *other, *vectors)


def own_gradients_kernel(scalars, mine, *refs):
    others, (mom, own, keep, send, total) = refs[:3], refs[3:]
    piece = mine.shape[0] // 3
    replica = scalars[3]
    start = jnp.where(replica == 0, 4, jnp.where(replica == 2, 8, 0)) * piece
    at = pl.multiple_of(jnp.where(replica == 0, 1, jnp.where(replica == 2, 2, 0)) * piece, piece)
    own[...] = muon_momentum * mom[pl.ds(pl.multiple_of(start, piece), 4 * piece), :]
    for j, part in enumerate((mine, *others)):
        quarter = lax.bitwise_xor(replica, j)
        rows = pl.ds(pl.multiple_of(quarter * piece, piece), piece)
        own[rows, :] = own[rows, :] + (part[pl.ds(at, piece), :] if j == 0 else part[...])
    row = lax.broadcasted_iota(jnp.int32, (4 * piece, 1), 0)
    drop = ((replica == 1) & (row >= 3 * piece)) | ((replica == 3) & (row < 3 * piece))
    block = jnp.where(drop, 0.0, own[...])
    own[...] = block
    gram = fdot(block, block, TN, precise)
    for n, (row, column) in enumerate(UPPER):
        total[n * 128 : (n + 1) * 128, :] = gram[
            row * 128 : (row + 1) * 128, column * 128 : (column + 1) * 128
        ]
    chips, share, _ = keep.shape
    for i, out in enumerate((keep, send)):
        for k in range(chips):
            at = lax.bitwise_xor(scalars[5], i) * chips + lax.bitwise_xor(scalars[4], k)
            out[k] = total[pl.ds(pl.multiple_of(at * share, share), share), :]


def own_gradients(scalars, mine, others, mom, chips):
    share = 128 * len(UPPER) // (2 * chips)
    return call(
        own_gradients_kernel,
        [((mom.shape[0] // 3, D), f32)] + [((chips, share, 128), f32)] * 2,
        [((128 * len(UPPER), 128), f32)],
        flops=10**8,
        data=1 << 18,
    )(scalars, mine, *others, mom)


def all_gradients_kernel(scalars, *refs):
    parts, (mom, grads, new_mom) = refs[:4], refs[4:]
    piece = mom.shape[0] // 12
    for j in range(4):
        quarter = lax.bitwise_xor(scalars[3], j)
        for n in range(3):
            rows = pl.ds(pl.multiple_of((4 * n + quarter) * piece, piece), piece)
            grads[rows, :] = parts[j][n * piece : (n + 1) * piece, :]
    new_mom[...] = muon_momentum * mom[...] + grads[...]


def all_gradients(scalars, parts, mom):
    return call(all_gradients_kernel, [(mom.shape, f32)] * 2, flops=10**8, data=1 << 18)(
        scalars, *parts, mom
    )


def pieces(x):
    hi, mid = halves(x)
    return hi, mid, (x - hi.astype(f32) - mid.astype(f32)).astype(bf16)


def full_product(a, b):
    (ah, am, al), (bh, bm, bl) = a, b
    return mm(
        jnp.concatenate([ah, ah, am, ah, al, am], axis=1),
        jnp.concatenate([bh, bm, bh, bl, bh, bm], axis=0),
        NN,
    )


def three_product(a, b):
    (ah, am, _), (bh, bm, _) = a, b
    return mm(
        jnp.concatenate([ah, am, ah], axis=1), jnp.concatenate([bh, bh, bm], axis=0), NN
    )


def identity():
    row = lax.broadcasted_iota(jnp.int32, (D, D), 0)
    return jnp.where(row == lax.broadcasted_iota(jnp.int32, (D, D), 1), 1.0, 0.0)


def polynomial(gram, product):
    g = pieces(gram)
    return g, ns_coeffs[1] * gram + ns_coeffs[2] * product(g, g) + ns_coeffs[0] * identity()


def polar_step(gram, block):
    g, poly = polynomial(gram, full_product)
    p = pieces(poly)
    return full_product(p, pieces(full_product(p, g))), three_product(pieces(block), p)


def polar_end(gram, block):
    return three_product(pieces(block), pieces(polynomial(gram, three_product)[1]))


def polar_start(gram, block):
    scale = 1.0 / (jnp.sqrt(jnp.sum(gram * identity())) + ns_eps)
    return gram * (scale * scale), block * scale


def polar(gram, block):
    gram, block = polar_start(gram, block)
    for step_index in range(NS_STEPS):
        square = fdot(gram, gram, NN, precise)
        poly = ns_coeffs[1] * gram + ns_coeffs[2] * square + ns_coeffs[0] * identity()
        if step_index + 1 < NS_STEPS:
            gram = fdot(poly, fdot(poly, gram, NN, precise), NN, precise)
        block = fdot(block, poly, NN, precise)
    return block


def update_kernel(scalars, mine, other, own, out, total, gram, block):
    chips, share, _ = mine.shape
    for i, parts in enumerate((mine, other)):
        for k in range(chips):
            at = lax.bitwise_xor(scalars[5], i) * chips + lax.bitwise_xor(scalars[4], k)
            total[pl.ds(pl.multiple_of(at * share, share), share), :] = parts[k]
    blocks = {}
    for n, (row, column) in enumerate(UPPER):
        blocks[row, column] = total[n * 128 : (n + 1) * 128, :]
        if row != column:
            blocks[column, row] = jnp.transpose(blocks[row, column])
    gram[...], block[...] = polar_start(
        jnp.concatenate(
            [jnp.concatenate([blocks[row, column] for column in range(3)], axis=1) for row in range(3)],
            axis=0,
        ),
        own[...],
    )

    def step(_, carry):
        gram[...], block[...] = polar_step(gram[...], block[...])
        return carry

    lax.fori_loop(0, NS_STEPS - 1, step, 0)
    replica = scalars[3]
    rate = jnp.where(replica == 1, 3.0**0.5, jnp.where(replica == 0, (FF / D) ** 0.5, 1.0))
    out[...] = polar_end(gram[...], block[...]) * (-muon_rate * rate)


def update(scalars, mine, other, own):
    return call(
        update_kernel,
        [(own.shape, f32)],
        [((128 * len(UPPER), 128), f32), ((D, D), f32), (own.shape, f32)],
        flops=10**8, data=1 << 18
    )(scalars, mine, other, own)[0]


def first_message_kernel(replica, qkv, out, vectors, message, rows, arrived):
    piece = out.shape[0]
    width = vectors.shape[1]
    small = pltpu.make_async_copy(vectors, rows, arrived.at[1])
    small.start()

    @pl.when(replica[0] < 3)
    def _():
        source = qkv.at[pl.ds(pl.multiple_of(replica[0] * piece, piece), piece), :]
        copy = pltpu.make_async_copy(source, message.at[pl.ds(0, piece), :], arrived.at[0])
        copy.start()
        copy.wait()

    @pl.when(replica[0] == 3)
    def _():
        copy = pltpu.make_async_copy(out, message.at[pl.ds(0, piece), :], arrived.at[0])
        copy.start()
        copy.wait()

    small.wait()
    message[piece:, :] = jnp.zeros((8, D), f32)
    message[piece:, :width] = rows[:8, :]
    message[piece : piece + 4, width : 2 * width] = rows[8:, :]


def first_message(replica, qkv, out, vectors):
    return pl.pallas_call(
        first_message_kernel,
        out_shape=jax.ShapeDtypeStruct((out.shape[0] + 8, D), f32),
        in_specs=[SMEM] + [pl.BlockSpec(memory_space=pltpu.HBM)] * 3,
        out_specs=VMEM,
        scratch_shapes=[pltpu.VMEM(vectors.shape, f32), pltpu.SemaphoreType.DMA((2,))],
    )(replica, qkv, out, vectors)


def hand_out_kernel(scalars, one, two, three, four, *outs):
    for owner, out in zip((1, 3, 0, 2), outs):
        at = lax.bitwise_xor(scalars[3], owner)
        rows = out.shape[0]
        for j, part in enumerate((one, two, three, four)):
            base = part.shape[0] - rows if owner == 3 else 0

            @pl.when(at == j)
            def _(part=part, out=out, base=base, rows=rows):
                out[...] = part[base : base + rows, :]


def hand_out(scalars, parts, cuts):
    outs = [((rows, D), f32) for rows in cuts]
    one, two, three, four = call(hand_out_kernel, outs, flops=10**8, data=1 << 18)(
        scalars, *parts
    )
    return one.T, two.T, three.T, four


def local(
    tokens,
    image_count,
    w_qkv,
    w_out,
    w_up,
    w_down,
    vectors,
    cotangent,
    mom_qkv,
    mom_out,
    mom_up,
    mom_down,
    mom_vectors,
):
    group_size = lax.axis_size("group")
    replicas = lax.axis_size("replica")
    group_index = lax.axis_index("group")
    replica_index = lax.axis_index("replica")
    chips = group_size // 2
    tok_rows = tokens.shape[0]
    slab_rows = group_size * tok_rows
    image_total = lax.dynamic_index_in_dim(image_count, replica_index, 0, keepdims=False)
    first_slot = group_index * tok_rows
    first_image = first_slot // L
    scalars = jnp.stack(
        [
            first_slot - first_image * L,
            slab_rows - first_image * L,
            image_total * L - first_slot,
            replica_index,
            group_index // 2,
            group_index % 2,
        ]
    ).astype(jnp.int32)

    def swap(x):
        return lax.ppermute(x, "group", [(i, i ^ 1) for i in range(group_size)])

    def hop(x, by):
        return lax.ppermute(x, "group", [(i, i ^ (2 * by)) for i in range(group_size)])

    def cross(x, by):
        return lax.ppermute(x, "replica", [(i, i ^ by) for i in range(replicas)])

    def halo(x):
        head, tail = x[:HALO], x[tok_rows - HALO :]
        even = group_index % 2 == 0
        pairs = [(i, i + 1) for i in range(1, group_size - 1, 2)]
        inside = swap(jnp.where(even, tail, head))
        outside = lax.ppermute(
            jnp.where(even, head, tail), "group", pairs + [(j, i) for i, j in pairs]
        )
        return inside, x, outside

    def along_chips(x):
        return jnp.stack([x] + [hop(x, k) for k in range(1, chips)])

    width = D // group_size
    piece = 4 * width // replicas
    cuts = (3 * width, width, 4 * width, 4 * width)
    first_stack = jnp.concatenate([w_qkv.T, w_out.T], axis=0)
    second_stack = jnp.concatenate([w_up.T, w_down], axis=0)
    mom_stack = jnp.concatenate([mom_qkv.T, mom_out.T, mom_up.T, mom_down], axis=0)
    around = halo(tokens)

    def split(stack):
        one, two, three, four = (stack[sum(cuts[:i]) : sum(cuts[: i + 1])] for i in range(4))
        return one.T, two.T, three.T, four

    def finish(block_out, grad_tokens, grads, new_mom, dvec, updates):
        grad_vectors = lax.dynamic_slice_in_dim(dvec[:12], group_index * width, width, 1)
        new_vectors = vector_momentum * mom_vectors + grad_vectors
        return (
            block_out,
            grad_tokens,
            *split(grads),
            grad_vectors,
            *split(new_mom),
            new_vectors,
            *updates,
            -vector_rate * new_vectors,
        )

    if replicas != 4 or piece % 16:
        def rows_of(stack, inner):
            parts = lax.all_gather(stack, "group")
            rows = jnp.concatenate(
                [parts[:, :inner].reshape(-1, D), parts[:, inner:].reshape(-1, D)], axis=0
            )
            hi = lax.reduce_precision(rows, 8, 7)
            lo = lax.reduce_precision(rows - hi, 8, 7)
            return jnp.concatenate([hi, lo, hi], axis=1).astype(bf16)

        def shares_of(total, cut, inner):
            one, two = total[:cut], total[cut:]
            parts = jnp.concatenate(
                [one.reshape(group_size, inner, D), two.reshape(group_size, -1, D)], axis=1
            )
            return lax.psum_scatter(parts, "group", scatter_dimension=0)

        w_one, w_two = rows_of(first_stack, 3 * width), rows_of(second_stack, 4 * width)
        vec = jnp.pad(lax.all_gather(vectors, "group", axis=1, tiled=True), ((0, 4), (0, 0)))
        *saved, a3, middle = attend(scalars, *around, w_one, vec)
        block_out, slope, n3, m3, down = mlp(
            scalars, None, middle, cotangent, w_two, vec, vec[8:12].reshape(1, FF)
        )
        d_middle, dvec, up = mlp_back(
            scalars, None, middle, cotangent, w_two, vec, slope, n3, m3
        )
        second = jnp.concatenate([up, down], axis=0)
        d_around = halo(d_middle)
        some, more = (attend_back(scalars, i, 2, d_around, w_one, *saved) for i in (0, 2))
        first, d_hi, d_lo, sums = attend_grads(
            scalars, None, some, more, tokens, d_middle, vec, a3
        )
        grad_tokens, dvec = token_grads(
            scalars, d_hi, d_lo, w_one, tokens, d_middle, vec, sums, dvec
        )
        grads, dvec = lax.psum(
            (
                jnp.concatenate(
                    [shares_of(first, 3 * D, 3 * width), shares_of(second, FF, 4 * width)], axis=0
                ),
                lax.psum(dvec, "group"),
            ),
            "replica",
        )
        new_mom = muon_momentum * mom_stack + grads
        blocks = [new_mom[sum(cuts[:i]) : sum(cuts[: i + 1])] for i in range(4)]
        grams = lax.psum(jnp.stack([fdot(x, x, TN, precise) for x in blocks]), "group")
        updates = [
            polar(grams[i], x) * (-muon_rate * rate)
            for i, (x, rate) in enumerate(zip(blocks, (3.0**0.5, 1.0, (FF / D) ** 0.5, 1.0)))
        ]
        updates = [x if i == 3 else x.T for i, x in enumerate(updates)]
        return finish(block_out, grad_tokens, grads, new_mom, dvec, updates)

    def second_quarter(quarter):
        return jnp.concatenate(
            [
                lax.dynamic_slice_in_dim(second_stack, (4 * n + quarter) * piece, piece, 0)
                for n in range(2)
            ],
            axis=0,
        )

    my_second = second_quarter(replica_index)
    diagonal = second_quarter(lax.bitwise_xor(replica_index, 3))
    others = range(1, replicas)
    start = first_message(replica_index.astype(jnp.int32).reshape(1), w_qkv.T, w_out.T, vectors)
    start = [start] + [hop(start, k) for k in range(1, chips)]
    first = jnp.concatenate([x[:piece] for x in start], axis=0)
    vec_parts = jnp.concatenate([x[piece:] for x in start], axis=0)
    first, vec_parts, scalars, lower, upper = lax.optimization_barrier(
        (first, vec_parts, scalars, around[0], around[2])
    )
    around = lower, tokens, upper
    first_other, vec_other = [swap(first)], swap(vec_parts)
    first = [first] + [cross(first, j) for j in others]
    first_other[0], vec_other, my_second = lax.optimization_barrier(
        (first_other[0], vec_other, my_second)
    )
    second = [my_second] + [hop(my_second, k) for k in range(1, chips)]
    first[1:], second = lax.optimization_barrier((first[1:], second))
    second = jnp.concatenate(second, axis=0)
    first_other += [swap(first[j]) for j in others]
    diagonal, second, first_other = lax.optimization_barrier((diagonal, second, first_other))
    diagonal = [diagonal] + [hop(diagonal, k) for k in range(1, chips)]
    second = [second, cross(second, 1), cross(second, 2)]
    w_one, vec, bias = unpack(
        scalars, chips, first, first_other, first_rows, vec_parts, vec_other
    )
    *saved, a3, middle = attend(scalars, *around, w_one, vec)
    second[1:], diagonal, middle = lax.optimization_barrier((second[1:], diagonal, middle))
    second.append(jnp.concatenate(diagonal, axis=0))
    second_other = [swap(x) for x in second]
    w_two = unpack(scalars, chips, second, second_other, second_rows)[0]
    shape = (chips, piece, D)

    def join(keep, other):
        return [x + other[j] for j, x in enumerate(keep)]

    def exchange(parts):
        return [parts[0]] + [cross(parts[j], j) for j in others]

    block_out, slope, n3, m3, *keep, send = mlp(
        scalars, shape, middle, cotangent, w_two, vec, bias
    )
    other = swap(send)
    down_keep = keep
    d_middle, dvec, *keep, send = mlp_back(
        scalars, shape, middle, cotangent, w_two, vec, slope, n3, m3
    )
    down, d_middle, send = lax.optimization_barrier((join(down_keep, other), d_middle, send))
    d_around = halo(d_middle)
    other = swap(send)
    down = exchange(down)
    some = attend_back(scalars, 0, 2, d_around, w_one, *saved)
    up, some, d_around = lax.optimization_barrier((join(keep, other), some, d_around))
    up = exchange(up)
    more = attend_back(scalars, 2, 2, d_around, w_one, *saved)
    *keep, send, d_hi, d_lo, sums = attend_grads(
        scalars, shape, some, more, tokens, d_middle, vec, a3
    )
    grad_tokens, dvec = token_grads(scalars, d_hi, d_lo, w_one, tokens, d_middle, vec, sums, dvec)
    keep, send, dvec, up, down = lax.optimization_barrier((keep, send, dvec, up, down))
    other, dvec = swap(send), dvec + swap(dvec)
    first, dvec, up, down = lax.optimization_barrier((join(keep, other), dvec, up, down))
    first = exchange(first)

    def over_chips(messages):
        return sum((hop(messages[k], k) for k in range(1, len(messages))), messages[0])

    def rows_for(parts, k):
        return sum((x[k] for x in parts[1:]), parts[0][k])

    second_sum = over_chips(
        [jnp.concatenate([rows_for(up, k), rows_for(down, k), dvec], axis=0) for k in range(chips)]
    )
    up_sum, down_sum, dvec = (
        second_sum[:piece], second_sum[piece : 2 * piece], second_sum[2 * piece :]
    )
    first_sum = over_chips([rows_for(first, k) for k in range(chips)])

    def for_replica(replica):
        return jnp.where(replica == 0, up_sum, jnp.where(replica == 2, down_sum, first_sum))

    mine = jnp.concatenate([first_sum, up_sum, down_sum], axis=0)
    taken = [cross(for_replica(lax.bitwise_xor(replica_index, j)), j) for j in others]
    own, keep, send = own_gradients(scalars, mine, taken, mom_stack, chips)
    t = keep + swap(send)
    t = t[0] + sum(hop(t[k], k) for k in range(1, chips))
    gram = along_chips(t)
    update_own = update(scalars, gram, swap(gram), own)
    mine = jnp.concatenate([mine, dvec], axis=0)
    parts = [mine] + [cross(mine, j) for j in others]
    parts, update_own = lax.optimization_barrier((parts, update_own))
    updates = [update_own] + [cross(update_own, j) for j in others]
    dvec = sum((x[3 * piece :] for x in parts[1:]), parts[0][3 * piece :])
    grads, new_mom = all_gradients(scalars, parts, mom_stack)
    updates = hand_out(scalars, updates, cuts)
    return finish(block_out, grad_tokens, grads, new_mom, dvec, updates)


def solution(mesh):
    tokens, whole, columns, rows = P(("replica", "group"), None), P(), P(None, "group"), P("group", None)
    params = (columns, columns, columns, rows, columns)
    return jax.shard_map(
        local,
        mesh=mesh,
        in_specs=(tokens, whole, *params, tokens, *params),
        out_specs=(tokens, tokens, *params, *params, *params),
        check_vma=False,
    )
```
